32 devices in a mesh: row: 2 (over y), col: 8 (over z, core), orient: 2 (over x).
Axes of the slice: x: 2, y: 2, z: 4, core: 2. Of those that a mesh axis runs over, the one named last changes fastest.
Arguments:
- noise: float32 [2, 4096, 4096], P(None, ('row', 'col')), may hold values from -6 to 6
- elevation_library: float32 [16, 128, 128], replicated, may hold values from 0.25 to 1
- tile_choice_index: int32 [32, 32], P('row', 'col'), may hold values from 0 to 15
- family_heading_index: int32 [8], P('orient'), may hold values from 0 to 35
- family_extent_index: int32 [8], P('orient'), may hold values from 0 to 3
Outputs:
- safety_min: float32 [4096, 4096], P('row', ('col', 'orient'))
The draws below stay inside these ranges and needn't reach their ends.
All inputs are finite; a program needn't handle non-finite values.
Results may differ from the reference program's by a relative error of at most 0.0005.
Values may be sent and summed in bfloat16 or wider, within the bound.
A program may use at most 256 MiB of HBM per device.

```python
import math
import jax
import jax.numpy as jnp
from jax import lax

WINDOW_CELLS = 4096
R = 8
N_AZ = 36
NSIZE = 4
FAM = 8
TILE_SIDE = 128
LIBRARY_TILES = 16
NTILES = 32


def plant(result, stream_key, low, largest):
    longest = result.shape.index(max(result.shape))
    spots = []
    for shift in (0, 1):
        where = [jax.random.randint(jax.random.fold_in(stream_key, axis), (), 0, length) for axis, length in enumerate(result.shape)]
        where[longest] = (where[longest] + shift) % result.shape[longest]
        spots.append(tuple(where))
    return result.at[spots[0]].set(low).at[spots[1]].set(largest)


def block_levels(rng, shape, shards, least, top_value):
    def one(dim, parts):
        steps = jax.random.uniform(jax.random.fold_in(jax.random.fold_in(rng, 6), dim), (parts,), jnp.float32, least / len(shards), top_value / len(shards))
        return jnp.repeat(jnp.exp(steps), shape[dim] // parts).reshape((-1,) + (1,) * (len(shape) - dim - 1))

    factor_of = one(*shards[0])
    for cut in shards[1:]:
        factor_of = factor_of * one(*cut)
    return factor_of


def bell_draw(stream_key, dims, width, most, cuts=(), kind=jnp.bfloat16):
    array = width * jax.random.normal(stream_key, dims, jnp.float32)
    if cuts:
        array = array * block_levels(stream_key, dims, cuts, -0.22, 0.18)
    return jnp.clip(array, -most, most).astype(kind)


def setup_inputs(seed: int = 0) -> dict:
    splits = jax.random.split(jax.random.key(seed), 6)
    noise = bell_draw(splits[0], (2, WINDOW_CELLS, WINDOW_CELLS), 1.0, 6.0, ((1, 16),), jnp.float32)
    elevation_library = jnp.clip(jnp.exp(jax.random.uniform(splits[1], (LIBRARY_TILES, TILE_SIDE, TILE_SIDE), jnp.float32, math.log(0.25), math.log(1.0))), 0.25, 1.0)
    tile_choice_index = plant(jax.random.randint(splits[2], (NTILES, NTILES), 0, LIBRARY_TILES), jax.random.fold_in(splits[2], 1), 0, LIBRARY_TILES - 1).astype(jnp.int32)
    family_heading_index = plant(jax.random.randint(splits[3], (FAM,), 0, N_AZ), jax.random.fold_in(splits[3], 1), 0, N_AZ - 1).astype(jnp.int32)
    family_extent_index = plant(jax.random.randint(splits[4], (FAM,), 0, NSIZE), jax.random.fold_in(splits[4], 1), 0, NSIZE - 1).astype(jnp.int32)
    return dict(noise=noise, elevation_library=elevation_library, tile_choice_index=tile_choice_index, family_heading_index=family_heading_index, family_extent_index=family_extent_index)


nugget_share = 0.3
peak_share = 1024.0 / (2.0 * math.pi)
cutoff_ratio = 32.0

def amplitude(u_index, v_index, side_cells):
    wrap_u = jnp.minimum(u_index, side_cells - u_index).astype(jnp.float32)
    wrap_v = jnp.minimum(v_index, side_cells - v_index).astype(jnp.float32)
    cutoff = side_cells / cutoff_ratio
    scaled_u = wrap_u / cutoff
    scaled_v = wrap_v / cutoff
    grown = 1.0 + scaled_u * scaled_u + scaled_v * scaled_v
    spectrum = nugget_share + peak_share / (grown * jnp.sqrt(grown))
    return jnp.sqrt(spectrum) / side_cells

def ellipsoid(offset_u, offset_v, azimuth, size_index):
    heading = azimuth.astype(jnp.float32) * (math.pi / N_AZ)
    semi_axis = R * (size_index.astype(jnp.float32) + (1 + NSIZE)) / (2 * NSIZE)
    across = 0.6 * semi_axis
    slip_depth = 0.3 * semi_axis
    along = offset_u * jnp.cos(heading) + offset_v * jnp.sin(heading)
    lateral = offset_v * jnp.cos(heading) - offset_u * jnp.sin(heading)
    along_part = along / semi_axis
    lateral_part = lateral / across
    inside = 1.0 - along_part * along_part - lateral_part * lateral_part
    height = slip_depth * jnp.sqrt(jnp.maximum(inside, 0.0))
    base_share = jnp.clip(4.0 * inside, 0.0, 1.0)
    return (height, base_share)

def reference(noise, elevation_library, tile_choice_index, family_heading_index, family_extent_index):
    u_index = lax.broadcasted_iota(jnp.int32, (WINDOW_CELLS, WINDOW_CELLS), 1)
    v_index = lax.broadcasted_iota(jnp.int32, (WINDOW_CELLS, WINDOW_CELLS), 0)
    amplitudes = amplitude(u_index, v_index, WINDOW_CELLS)
    weights = amplitudes * noise[0] + 1j * (amplitudes * noise[1])
    spectral = jnp.fft.fft2(weights)
    field_re = jnp.real(spectral).T
    field_im = jnp.imag(spectral).T
    elevation_tiles = jnp.take(elevation_library, tile_choice_index, axis=0)
    slope_tangents = elevation_tiles.transpose(0, 2, 1, 3).reshape(WINDOW_CELLS, WINDOW_CELLS)
    secant = jnp.sqrt(1.0 + slope_tangents * slope_tangents)
    cohesion = 0.5 * jnp.exp(0.4 * field_re)
    friction = 0.6 * jnp.exp(0.25 * field_im)
    column_terms = jnp.stack([cohesion * secant, friction / secant, slope_tangents / secant])
    column_terms = lax.optimization_barrier(column_terms.astype(jnp.bfloat16)).astype(jnp.float32)
    kernel_width = 2 * R + 1
    offset_u = (lax.broadcasted_iota(jnp.int32, (kernel_width, kernel_width), 0) - R).astype(jnp.float32)
    offset_v = (lax.broadcasted_iota(jnp.int32, (kernel_width, kernel_width), 1) - R).astype(jnp.float32)
    resist_input = column_terms[0:2][None]
    drive_input = column_terms[2:3][None]

    def family_step(family_index, lowest):
        height, base_share = ellipsoid(offset_u, offset_v, family_heading_index[family_index], family_extent_index[family_index])
        height = lax.optimization_barrier(height.astype(jnp.bfloat16)).astype(jnp.float32)
        base_share = lax.optimization_barrier(base_share.astype(jnp.bfloat16)).astype(jnp.float32)
        resist_kernel = jnp.stack([base_share, height])[None]
        drive_kernel = height[None, None]
        resisting = lax.conv_general_dilated(resist_input, resist_kernel, (1, 1), [(R, R), (R, R)], precision=lax.Precision.HIGHEST)[0, 0]
        driving = lax.conv_general_dilated(drive_input, drive_kernel, (1, 1), [(R, R), (R, R)], precision=lax.Precision.HIGHEST)[0, 0]
        return jnp.minimum(lowest, resisting / driving)
    start = jnp.full((WINDOW_CELLS, WINDOW_CELLS), jnp.inf, jnp.float32)
    return lax.fori_loop(0, FAM, family_step, start)
```

```python
import functools
import math

import jax
import jax.numpy as jnp
import numpy as np
from jax import lax
from jax.experimental import pallas as pl
from jax.experimental.pallas import tpu as pltpu
from jax.sharding import PartitionSpec as P

R = 8
N_AZ = 36
NSIZE = 4
LANES = 128
TILE_ROWS = 8
TILE_LANES = 16
GROUPS = LANES // TILE_LANES
PHASE = TILE_ROWS * TILE_LANES
STEP_TILES = 8

nugget_share = 0.3
peak_share = 1024.0 / (2.0 * math.pi)
cutoff_ratio = 32.0


def amplitude(u_index, v_index, side_cells):
    wrap_u = jnp.minimum(u_index, side_cells - u_index).astype(jnp.float32)
    wrap_v = jnp.minimum(v_index, side_cells - v_index).astype(jnp.float32)
    cutoff = side_cells / cutoff_ratio
    scaled_u = wrap_u / cutoff
    scaled_v = wrap_v / cutoff
    grown = 1.0 + scaled_u * scaled_u + scaled_v * scaled_v
    spectrum = nugget_share + peak_share / (grown * jnp.sqrt(grown))
    return jnp.sqrt(spectrum) / side_cells


def ellipsoid(offset_u, offset_v, azimuth, size_index):
    heading = azimuth.astype(jnp.float32) * (math.pi / N_AZ)
    semi_axis = R * (size_index.astype(jnp.float32) + (1 + NSIZE)) / (2 * NSIZE)
    across = 0.6 * semi_axis
    slip_depth = 0.3 * semi_axis
    along = offset_u * jnp.cos(heading) + offset_v * jnp.sin(heading)
    lateral = offset_v * jnp.cos(heading) - offset_u * jnp.sin(heading)
    along_part = along / semi_axis
    lateral_part = lateral / across
    inside = 1.0 - along_part * along_part - lateral_part * lateral_part
    height = slip_depth * jnp.sqrt(jnp.maximum(inside, 0.0))
    base_share = jnp.clip(4.0 * inside, 0.0, 1.0)
    return (height, base_share)


def small_dft(parts):
    count = len(parts)
    if count == 1:
        return parts
    even = small_dft(parts[0::2])
    odd = small_dft(parts[1::2])
    low, high = [], []
    for k in range(count // 2):
        (a, b), (c, d) = even[k], odd[k]
        if k == 0:
            e, f = c, d
        elif 4 * k == count:
            e, f = d, -c
        else:
            cos = math.cos(2 * math.pi * k / count)
            sin = math.sin(2 * math.pi * k / count)
            e, f = c * cos + d * sin, d * cos - c * sin
        low.append((a + e, b + f))
        high.append((a - e, b - f))
    return low + high


def transform_kernel(planes, blocks, span, step, pad, in_ref, cos_ref, sin_ref, big_ref, small_ref, out_ref, mid, full):
    outer = cos_ref.shape[0]
    rows = mid.shape[1]
    unit = 16 if planes else 8

    @pl.loop(0, rows // unit)
    def _(block):
        at = pl.ds(pl.multiple_of(block * unit, unit), unit)
        parts = []
        for p in range(outer):
            if planes:
                parts.append((in_ref[p, 0, at, :].astype(jnp.float32), in_ref[p, 1, at, :].astype(jnp.float32)))
            else:
                lanes = slice(p * LANES, (p + 1) * LANES)
                parts.append((in_ref[0, at, lanes], in_ref[1, at, lanes]))
        for k, (re, im) in enumerate(small_dft(parts)):
            cos = cos_ref[k : k + 1, :]
            sin = sin_ref[k : k + 1, :]
            mid[k, at, 0:LANES] = re * cos + im * sin
            mid[k, at, LANES : 2 * LANES] = im * cos - re * sin

    if pad:
        edge = jnp.zeros((pad, rows), jnp.float32)
        for part in range(2):
            full[part, 0:pad, :] = edge
            full[part, pad + outer * LANES : 2 * pad + outer * LANES, :] = edge

    turned = (((1,), (1,)), ((), ()))
    dot = functools.partial(lax.dot_general, dimension_numbers=turned, preferred_element_type=jnp.float32)
    for k in range(outer):
        value = mid[k]
        high = value.astype(jnp.bfloat16)
        rest = (value - high.astype(jnp.float32)).astype(jnp.bfloat16)
        got = dot(big_ref[...], high) + dot(big_ref[...], rest) + dot(small_ref[...], high)
        full[0, pl.ds(pad + k, LANES, stride=outer), :] = got[0:LANES]
        full[1, pl.ds(pad + k, LANES, stride=outer), :] = got[LANES : 2 * LANES]

    @pl.loop(0, blocks)
    def _(block):
        at = pl.ds(pl.multiple_of(block * step, 8), span)
        for part in range(2):
            out_ref[block, part] = full[part, at, :].astype(jnp.bfloat16)


def transform(cells, planes, rows, length, blocks, pad):
    outer = length // LANES
    step = length // blocks
    span = step + 2 * pad
    k = np.arange(outer)[:, None]
    q = np.arange(LANES)
    turn = 2 * np.pi * k * q / length
    cos, sin = np.cos(turn).astype(np.float32), np.sin(turn).astype(np.float32)
    angle = 2 * np.pi * (q[:, None] * q % LANES) / LANES
    table = np.block([[np.cos(angle), np.sin(angle)], [-np.sin(angle), np.cos(angle)]]).astype(np.float32)
    big = table.astype(jnp.bfloat16)
    small = (table - big.astype(np.float32)).astype(jnp.bfloat16)
    vmem = pl.BlockSpec(memory_space=pltpu.VMEM)
    return pl.pallas_call(
        functools.partial(transform_kernel, planes, blocks, span, step, pad),
        out_shape=jax.ShapeDtypeStruct((blocks, 2, span, rows), jnp.bfloat16),
        in_specs=[vmem] * 5,
        out_specs=vmem,
        scratch_shapes=[
            pltpu.VMEM((outer, rows, 2 * LANES), jnp.float32),
            pltpu.VMEM((2, length + 2 * pad, rows), jnp.float32),
        ],
        compiler_params=pltpu.CompilerParams(vmem_limit_bytes=40 << 20),
    )(cells, cos, sin, big, small)


def swap_groups(cells):
    row = lax.broadcasted_iota(jnp.int32, cells.shape, 1)
    group = lax.broadcasted_iota(jnp.int32, cells.shape, 2) // TILE_LANES
    skewed = pltpu.roll(cells, 0, 2, stride=TILE_LANES, stride_axis=1)
    picked = jnp.take_along_axis(skewed, (group + row - 7) & 7, axis=1)
    level = pltpu.roll(picked, TILE_LANES, 2, stride=TILE_LANES, stride_axis=1)
    return jnp.take_along_axis(level, 7 - row, axis=1)


def gather_tiles(term_ref, swapped, gathered):
    tiles, across = gathered.shape[1:3]
    chunks = across // GROUPS

    @pl.when(pl.program_id(0) == 0)
    def _():
        @pl.loop(0, tiles // 2)
        def _(pair):
            at = pl.ds(pl.multiple_of(pair * 16, 16), 16)
            both = pl.ds(pair * 2, 2)
            for term in range(gathered.shape[0]):
                for chunk in range(chunks + 1):
                    cells = term_ref[term, at, chunk * LANES : (chunk + 1) * LANES].astype(jnp.float32)
                    turned = swap_groups(cells.reshape(2, TILE_ROWS, LANES))
                    swapped[:, chunk * GROUPS : (chunk + 1) * GROUPS, :] = turned
                gathered[term, both, :, 0:PHASE] = swapped[:, 0:across, :].astype(jnp.bfloat16)
                gathered[term, both, :, PHASE:] = swapped[:, 1 : across + 1, :].astype(jnp.bfloat16)


def column_sum(gathered, band_ref, lanes):
    terms, _, across, depth = gathered.shape
    tile = pl.program_id(0) * STEP_TILES
    pieces = [(term, shift) for term in range(terms) for shift in range(3)]
    left = [gathered[term, pl.ds(tile + shift, STEP_TILES)] for term, shift in pieces]
    left = [piece.reshape(STEP_TILES * across, depth) for piece in left]
    right = [band_ref[term, shift, :, lanes] for term, shift in pieces]
    return jnp.dot(
        jnp.concatenate(left, axis=1),
        jnp.concatenate(right, axis=0),
        preferred_element_type=jnp.float32,
    )


def driving_kernel(families, term_ref, band_ref, out_ref, swapped, gathered):
    gather_tiles(term_ref, swapped, gathered)
    for pair in range(families // 2):
        lanes = slice(pair * 2 * PHASE, (pair + 1) * 2 * PHASE)
        out_ref[:, lanes] = column_sum(gathered, band_ref, lanes)


def stability_kernel(families, term_ref, band_ref, drive_ref, out_ref, swapped, gathered):
    chunks = gathered.shape[2] // GROUPS
    gather_tiles(term_ref, swapped, gathered)
    low = None
    for pair in range(families // 2):
        lanes = slice(pair * 2 * PHASE, (pair + 1) * 2 * PHASE)
        ratio = column_sum(gathered, band_ref, lanes) / drive_ref[:, lanes]
        least = jnp.minimum(ratio[:, 0:PHASE], ratio[:, PHASE:])
        low = least if low is None else jnp.minimum(low, least)
    turned = swap_groups(low.reshape(STEP_TILES * chunks, TILE_ROWS, LANES))
    for side in range(STEP_TILES):
        for chunk in range(chunks):
            out_ref[side * 8 : side * 8 + 8, chunk * LANES : (chunk + 1) * LANES] = turned[side * chunks + chunk]


def tile_call(kernel, terms, band, height, width, out_shape, out_block, more=()):
    families = band.shape[-1] // PHASE
    across = width // TILE_LANES
    tiles = height // TILE_ROWS + 2
    count = terms.shape[0]
    work = 2 * (height // TILE_ROWS) * across * band.size
    return pl.pallas_call(
        functools.partial(kernel, families),
        grid=(height // (TILE_ROWS * STEP_TILES),),
        out_shape=jax.ShapeDtypeStruct(out_shape, jnp.float32),
        in_specs=[
            pl.BlockSpec(terms.shape, lambda i: (0, 0, 0), pipeline_mode=pl.Buffered(1)),
            pl.BlockSpec(band.shape, lambda i: (0, 0, 0, 0), pipeline_mode=pl.Buffered(1)),
        ]
        + [pl.BlockSpec((STEP_TILES * across, cells.shape[1]), lambda i: (i, 0)) for cells in more],
        out_specs=pl.BlockSpec(out_block, lambda i: (i, 0)),
        scratch_shapes=[
            pltpu.VMEM((2, across + GROUPS, LANES), jnp.float32),
            pltpu.VMEM((count, tiles, across, 2 * PHASE), jnp.bfloat16),
        ],
        compiler_params=pltpu.CompilerParams(vmem_limit_bytes=56 << 20),
        cost_estimate=pl.CostEstimate(flops=work, bytes_accessed=16 << 20, transcendentals=0),
    )(terms, band, *more)


def extended(cells, sides, width):
    for axis, dim in sides:
        ends = lax.axis_size(axis) - 1
        head = lax.slice_in_dim(cells, 0, width, axis=dim)
        tail = lax.slice_in_dim(cells, cells.shape[dim] - width, cells.shape[dim], axis=dim)
        before = lax.ppermute(tail, axis, [(i, i + 1) for i in range(ends)])
        after = lax.ppermute(head, axis, [(i + 1, i) for i in range(ends)])
        cells = jnp.concatenate([before, cells, after], axis=dim)
    return cells


def band_weights(headings, extents):
    shape = (3, 2, TILE_ROWS, TILE_LANES, TILE_ROWS, TILE_LANES)
    index = [lax.broadcasted_iota(jnp.int32, shape, axis) for axis in range(6)]
    offset_v = TILE_ROWS * index[0] + index[2] - R - index[4]
    offset_u = TILE_LANES * index[1] + index[3] - R - index[5]
    keep = (jnp.abs(offset_v) <= R) & (jnp.abs(offset_u) <= R)
    rows = 3 * 2 * PHASE

    def flat(cells):
        return cells.reshape(rows, 1, PHASE)

    heights, shares = ellipsoid(
        flat(offset_u.astype(jnp.float32)),
        flat(offset_v.astype(jnp.float32)),
        headings[None, :, None],
        extents[None, :, None],
    )
    keep = flat(keep)
    count = headings.shape[0]

    def whole(cells):
        return jnp.where(keep, cells, 0.0).astype(jnp.bfloat16).reshape(3, 2 * PHASE, count * PHASE)

    heights = whole(heights)
    return jnp.stack([whole(shares), heights])


def pick_tiles(library, index):
    def copy_kernel(index_ref, in_ref, out_ref):
        out_ref[...] = in_ref[...]

    block = (1,) + library.shape[1:]
    flat = index.reshape(-1)
    picked = pl.pallas_call(
        copy_kernel,
        out_shape=jax.ShapeDtypeStruct(flat.shape + library.shape[1:], library.dtype),
        grid_spec=pltpu.PrefetchScalarGridSpec(
            num_scalar_prefetch=1,
            grid=flat.shape,
            in_specs=[pl.BlockSpec(block, lambda i, index_ref: (index_ref[i], 0, 0))],
            out_specs=pl.BlockSpec(block, lambda i, index_ref: (i, 0, 0)),
        ),
    )(flat, library)
    return picked.reshape(index.shape + library.shape[1:])


def body(noise, elevation_library, tile_choice_index, family_heading_index, family_extent_index):
    side_cells = noise.shape[2]
    row_count = lax.axis_size("row")
    col_count = lax.axis_size("col")
    split = lax.axis_size("orient")
    row, col, side = (lax.axis_index(axis) for axis in ("row", "col", "orient"))
    devices = row_count * col_count * split
    lines = noise.shape[1] // split
    window_rows = side_cells // row_count
    window_columns = side_cells // (col_count * split)

    families = jnp.stack([family_heading_index, family_extent_index])
    held_families = [families]
    for turn in range(1, split):
        pairs = [(i, (i + turn) % split) for i in range(split)]
        held_families.append(lax.ppermute(families, "orient", pairs))
    families = jnp.concatenate(held_families, axis=1)
    choices = extended(tile_choice_index, (("row", 0), ("col", 1)), 1)

    own = lax.dynamic_slice_in_dim(noise, side * lines, lines, 1)
    first_line = lax.axis_index(("row", "col", "orient")) * lines
    v_index = first_line + lax.broadcasted_iota(jnp.int32, (lines, side_cells), 0)
    u_index = lax.broadcasted_iota(jnp.int32, (lines, side_cells), 1)
    weights = own * amplitude(u_index, v_index, side_cells)[None]
    spectrum = transform(weights, False, lines, side_cells, devices, 0)
    spectrum, choices, families = lax.optimization_barrier((spectrum, choices, families))
    held = lax.all_to_all(spectrum, ("row", "col", "orient"), split_axis=0, concat_axis=0, tiled=True)
    tall = window_columns + 2 * R
    wide = (window_rows // LANES + 1) * LANES
    spare = wide - window_rows - 2 * R
    tile_side = elevation_library.shape[1]
    tiles_x = window_rows // tile_side
    tiles_y = window_columns // tile_side
    first_y = col * split + side
    local = lax.dynamic_slice_in_dim(choices, side * tiles_y, tiles_y + 2, 1)
    slope = pick_tiles(elevation_library.transpose(0, 2, 1), local.T)
    slope = slope.transpose(0, 2, 1, 3).reshape((tiles_y + 2) * tile_side, (tiles_x + 2) * tile_side)
    edge = tile_side - R
    slope = slope[edge : edge + tall, edge : edge + wide]
    y = first_y * window_columns - R + lax.broadcasted_iota(jnp.int32, (tall, wide), 0)
    x = row * window_rows - R + lax.broadcasted_iota(jnp.int32, (tall, wide), 1)
    inside = (y >= 0) & (y < side_cells) & (x >= 0) & (x < side_cells)
    secant = jnp.sqrt(1.0 + slope * slope)
    lift = jnp.where(inside, 0.5 * secant, 0.0)
    grip = jnp.where(inside, 0.6 / secant, 0.0)
    drive = jnp.where(inside, slope / secant, 0.0).astype(jnp.bfloat16)
    band = band_weights(families[0], families[1])
    held, lift, grip, drive = lax.optimization_barrier((held, lift, grip, drive))
    positions = side_cells // devices
    per_block = LANES // lines
    held = held.reshape(side_cells // LANES, per_block, 2, positions, lines)
    held = held.transpose(0, 2, 3, 1, 4).reshape(side_cells // LANES, 2, positions, LANES)
    fields = transform(held, True, positions, side_cells, col_count * split, R)
    fields = lax.all_to_all(fields, ("col", "orient"), split_axis=0, concat_axis=0, tiled=True)
    across = window_rows // TILE_LANES
    driving = tile_call(
        driving_kernel,
        drive[None],
        band[1:],
        window_columns,
        window_rows,
        (window_columns // TILE_ROWS * across, band.shape[-1]),
        (STEP_TILES * across, band.shape[-1]),
    )
    fields, driving, band = lax.optimization_barrier((fields, driving, band))
    fields = fields.transpose(1, 2, 0, 3).reshape(2, tall, window_rows)
    ends = row_count - 1
    before = lax.ppermute(fields[:, :, window_rows - R :], "row", [(i, i + 1) for i in range(ends)])
    after = lax.ppermute(fields[:, :, :R], "row", [(i + 1, i) for i in range(ends)])
    fields = jnp.concatenate(
        [before, fields, after, jnp.zeros((2, tall, spare), fields.dtype)], axis=2
    ).astype(jnp.float32)

    cohesion = (jnp.exp(0.4 * fields[0]) * lift).astype(jnp.bfloat16)
    friction = (jnp.exp(0.25 * fields[1]) * grip).astype(jnp.bfloat16)
    safety = tile_call(
        stability_kernel,
        jnp.stack([cohesion, friction]),
        band,
        window_columns,
        window_rows,
        (window_columns, window_rows),
        (TILE_ROWS * STEP_TILES, window_rows),
        (driving,),
    )
    return safety.T


def swap8(cells, rolled=False):
    if not rolled:
        cells = [pltpu.roll(c, TILE_LANES * i, 1) if i else c for i, c in enumerate(cells)]
    group = lax.broadcasted_iota(jnp.int32, cells[0].shape, 1) // TILE_LANES
    for bit in (1, 2, 4):
        pick = (group & bit) != 0
        cells = [jnp.where(pick, cells[(i + bit) % GROUPS], cells[i]) for i in range(GROUPS)]
    out = []
    for i in range(GROUPS):
        c = cells[-i % GROUPS]
        out.append(pltpu.roll(c, LANES - TILE_LANES * i, 1) if i else c)
    return out


def strip_of(row, col, side, cols):
    return row * (2 * cols) + col + side * (2 * cols - 1 - 2 * col)


def place_of(strip, cols):
    row = strip // (2 * cols)
    at = strip % (2 * cols)
    side = at // cols
    return row, at + side * (2 * cols - 1 - 2 * at), side


def exact_dot(dot, big, small, value):
    high = value.astype(jnp.bfloat16)
    rest = (value - high.astype(jnp.float32)).astype(jnp.bfloat16)
    return dot(big, high) + dot(big, rest) + dot(small, high)


def tables(length, shift):
    outer = length // LANES
    k = np.arange(outer)[:, None] - shift
    q = np.arange(LANES)
    turn = 2 * np.pi * k * q / length
    cos, sin = np.cos(turn).astype(np.float32), np.sin(turn).astype(np.float32)
    angle = 2 * np.pi * (q[:, None] * q % LANES) / LANES
    table = np.block([[np.cos(angle), np.sin(angle)], [-np.sin(angle), np.cos(angle)]]).astype(np.float32)
    big = table.astype(jnp.bfloat16)
    small = (table - big.astype(np.float32)).astype(jnp.bfloat16)
    return cos, sin, big, small


TURNED = (((1,), (1,)), ((), ()))
DOT = functools.partial(lax.dot_general, dimension_numbers=TURNED, preferred_element_type=jnp.float32)


def rows_kernel(cols, in_ref, cos_ref, sin_ref, big_ref, small_ref, out_ref, mid, full):
    outer = cos_ref.shape[0]
    rows = mid.shape[1]

    @pl.loop(0, rows // 8)
    def _(block):
        at = pl.ds(pl.multiple_of(block * 8, 8), 8)
        parts = []
        for p in range(outer):
            lanes = slice(p * LANES, (p + 1) * LANES)
            parts.append((in_ref[0, at, lanes], in_ref[1, at, lanes]))
        turned = small_dft(parts)
        for k in range(outer):
            re, im = turned[(k - R) % outer]
            cos = cos_ref[k : k + 1, :]
            sin = sin_ref[k : k + 1, :]
            mid[k, at, 0:LANES] = re * cos + im * sin
            mid[k, at, LANES : 2 * LANES] = im * cos - re * sin

    for k in range(outer):
        got = exact_dot(DOT, big_ref[...], small_ref[...], mid[k])
        full[0, pl.ds(k, LANES, stride=outer), :] = got[0:LANES]
        full[1, pl.ds(k, LANES, stride=outer), :] = got[LANES : 2 * LANES]

    @pl.loop(0, outer)
    def _(block):
        strip = strip_of(block // (2 * cols), block % (2 * cols) // 2, block % 2, cols)
        at = pl.ds(pl.multiple_of(strip * LANES, LANES), LANES)
        for part in range(2):
            out_ref[block, part] = full[part, at, :].astype(jnp.bfloat16)


def rows_transform(weights, cols):
    length = weights.shape[2]
    outer = length // LANES
    vmem = pl.BlockSpec(memory_space=pltpu.VMEM)
    return pl.pallas_call(
        functools.partial(rows_kernel, cols),
        out_shape=jax.ShapeDtypeStruct((outer, 2, LANES, LANES), jnp.bfloat16),
        in_specs=[vmem] * 5,
        out_specs=vmem,
        scratch_shapes=[
            pltpu.VMEM((outer, LANES, 2 * LANES), jnp.float32),
            pltpu.VMEM((2, length, LANES), jnp.float32),
        ],
        compiler_params=pltpu.CompilerParams(vmem_limit_bytes=40 << 20),
    )(weights, *tables(length, R))


CHUNK = 32


def spread(into, base, a, g, at, value):
    for shift in range(3):
        to = a + 1 - shift
        if 0 <= to < 4:
            spot(into, base, to, g, at, shift, value)


def spot(into, base, to, g, at, shift, value):
    first = base + shift * 2 * LANES
    if g < GROUPS:
        into[to, g, at, first : first + LANES] = value
    if g > 0:
        into[to, g - 1, at, first + LANES : first + 2 * LANES] = value


def prep_kernel(choice_ref, place_ref, lib_ref, band_ref, lift_ref, grip_ref, inv_ref, own, other, gathered, edge):
    tiles = own.shape[0] // LANES

    @pl.when(pl.program_id(0) == 0)
    def _():
        left = lax.broadcasted_iota(jnp.int32, (LANES, LANES), 1) < R

        @pl.loop(0, tiles)
        def _(t):
            at = pl.ds(pl.multiple_of(t * LANES, LANES), LANES)
            before = lib_ref[choice_ref[0, t]]
            here = lib_ref[choice_ref[1, t]]
            after = lib_ref[choice_ref[2, t]]
            own[at, :] = jnp.where(left, before, here)
            other[at, :] = jnp.where(left, here, after)

        half = lax.broadcasted_iota(jnp.int32, (16, LANES), 1) % TILE_LANES < R
        first = place_ref[0] == 0
        last = place_ref[0] == tiles - 1
        edge[:, 0:8, :] = jnp.zeros((GROUPS + 1, 8, LANES), jnp.float32)
        edge[:, 8 + LANES :, :] = jnp.zeros((GROUPS + 1, 8, LANES), jnp.float32)
        for a in range(4):
            @pl.loop(0, 8)
            def _(c):
                at = pl.ds(pl.multiple_of(c * 16, 16), 16)
                for source in (own, other):
                    parts = [source[pl.ds(c * 512 + 8 * a + r, 16, stride=32), :] for r in range(8)]
                    turned = swap8(parts)
                    for g in range(GROUPS) if source is own else (0,):
                        slope = turned[g]
                        secant = jnp.sqrt(1.0 + slope * slope)
                        drive = slope / secant
                        tile = g
                        if source is own:
                            lift_ref[a, g, at, :] = 0.5 * secant
                            grip_ref[a, g, at, :] = 0.6 / secant
                            if g == 0:
                                drive = jnp.where(half & first, 0.0, drive)
                        else:
                            tile = GROUPS
                            drive = jnp.where(last & ~half, 0.0, drive)
                        spread(gathered, 0, a, tile, at, drive.astype(jnp.bfloat16))
                        if a in (0, 3):
                            edge[tile, pl.ds(pl.multiple_of(c * 16 + 8, 8), 16), :] = drive

            if a in (0, 3):
                @pl.loop(0, 8)
                def _(c):
                    at = pl.ds(pl.multiple_of(c * 16, 16), 16)
                    for g in range(GROUPS + 1):
                        move = 9 if a == 0 else 7
                        value = edge[g, pl.ds(c * 16 + move, 16), :].astype(jnp.bfloat16)
                        spot(gathered, 0, 3 - a, g, at, 2 if a == 0 else 0, value)

    at = pl.ds(pl.multiple_of(pl.program_id(0) * CHUNK, CHUNK), CHUNK)
    depth = gathered.shape[-1]
    cells = gathered[:, :, at, :].reshape(4 * GROUPS * CHUNK, depth)
    for pair in range(band_ref.shape[-1] // (2 * PHASE)):
        lanes = slice(pair * 2 * PHASE, (pair + 1) * 2 * PHASE)
        inv_ref[0, :, lanes] = 1.0 / jnp.dot(cells, band_ref[:, lanes], preferred_element_type=jnp.float32)


def prepare(choices, place, library, band):
    side = choices.shape[1] * LANES
    steps = LANES // CHUNK
    rows = 4 * GROUPS * CHUNK
    whole = pl.BlockSpec((4, GROUPS, LANES, LANES), lambda i, *_: (0, 0, 0, 0), pipeline_mode=pl.Buffered(1))
    return pl.pallas_call(
        prep_kernel,
        out_shape=[
            jax.ShapeDtypeStruct((4, GROUPS, LANES, LANES), jnp.float32),
            jax.ShapeDtypeStruct((4, GROUPS, LANES, LANES), jnp.float32),
            jax.ShapeDtypeStruct((steps, rows, band.shape[-1]), jnp.float32),
        ],
        grid_spec=pltpu.PrefetchScalarGridSpec(
            num_scalar_prefetch=2,
            grid=(steps,),
            in_specs=[
                pl.BlockSpec(library.shape, lambda i, *_: (0, 0, 0), pipeline_mode=pl.Buffered(1)),
                pl.BlockSpec(band.shape, lambda i, *_: (0, 0), pipeline_mode=pl.Buffered(1)),
            ],
            out_specs=[whole, whole, pl.BlockSpec((1, rows, band.shape[-1]), lambda i, *_: (i, 0, 0))],
            scratch_shapes=[
                pltpu.VMEM((side, LANES), jnp.float32),
                pltpu.VMEM((side, LANES), jnp.float32),
                pltpu.VMEM((4, GROUPS, LANES, band.shape[0]), jnp.bfloat16),
                pltpu.VMEM((GROUPS + 1, LANES + 16, LANES), jnp.float32),
            ],
        ),
        compiler_params=pltpu.CompilerParams(vmem_limit_bytes=56 << 20),
        cost_estimate=pl.CostEstimate(flops=2 * side * band.size, bytes_accessed=24 << 20, transcendentals=0),
    )(choices, place, library, band)


MESH = pl.DeviceIdType.MESH


def strip_kernel(
    sizes, in_ref, cos_ref, sin_ref, big_ref, small_ref, lift_ref, grip_ref, band_ref, inv_any,
    out_ref, scale_ref,
    mid, turn, gathered, edge, edge_send, halo_out, halo_in, inv, natural, staged, factor,
    inv_sem, halo_send, halo_recv, out_send, out_recv, scale_send, scale_recv,
):
    row_count, cols = sizes
    row, col, side = (lax.axis_index(axis) for axis in ("row", "col", "orient"))
    strips = row_count * cols * 2
    group = cols * 2
    strip = strip_of(row, col, side, cols)
    mine = strip % group
    block_here = col * 2 + side
    left = place_of(lax.rem(strip + strips - 1, strips), cols)
    right = place_of(lax.rem(strip + 1, strips), cols)
    outer = cos_ref.shape[0]

    def owner(block):
        return row, block // 2, block % 2

    barrier = pltpu.get_barrier_semaphore()
    for near in (left, right):
        pl.semaphore_signal(barrier, inc=1, device_id=near, device_id_type=MESH)

    @pl.loop(1, group)
    def _(turned):
        block = lax.rem(block_here + turned, group)
        pl.semaphore_signal(barrier, inc=1, device_id=owner(block), device_id_type=MESH)

    def inv_copy(chunk):
        return pltpu.make_async_copy(inv_any.at[chunk], inv.at[chunk], inv_sem.at[chunk])

    @pl.loop(0, LANES // CHUNK)
    def _(chunk):
        inv_copy(chunk).start()

    @pl.loop(0, LANES // 16)
    def _(block):
        at = pl.ds(pl.multiple_of(block * 16, 16), 16)
        parts = [(in_ref[p, 0, at, :].astype(jnp.float32), in_ref[p, 1, at, :].astype(jnp.float32)) for p in range(outer)]
        for k, (re, im) in enumerate(small_dft(parts)):
            to = pl.ds(pl.multiple_of(((block + k) & 7) * 16, 16), 16)
            cos = cos_ref[k : k + 1, :]
            sin = sin_ref[k : k + 1, :]
            mid[k, to, 0:LANES] = re * cos + im * sin
            mid[k, to, LANES : 2 * LANES] = im * cos - re * sin

    def halo_copy(slot):
        return pltpu.make_async_remote_copy(
            src_ref=halo_out.at[slot],
            dst_ref=halo_in.at[slot],
            send_sem=halo_send.at[slot],
            recv_sem=halo_recv.at[slot],
            device_id=left,
            device_id_type=MESH,
        )

    half = lax.broadcasted_iota(jnp.int32, (16, LANES), 1) % TILE_LANES < R
    first = strip == 0
    base = 6 * LANES
    for side_rows in (slice(0, 8), slice(8 + LANES, 16 + LANES)):
        edge[:, :, side_rows, :] = jnp.zeros((2, GROUPS, 8, LANES), jnp.float32)
        edge_send[:, side_rows, :] = jnp.zeros((2, 8, LANES), jnp.float32)
    for a in range(4):
        for r in range(8):
            turn[r] = exact_dot(DOT, big_ref[...], small_ref[...], mid[8 * a + r])

        @pl.loop(0, 8)
        def _(c):
            at = pl.ds(pl.multiple_of(c * 16, 16), 16)
            padded = pl.ds(pl.multiple_of(c * 16 + 8, 8), 16)
            for term in range(2):
                rows = pl.ds(pl.multiple_of(c * 16 + term * LANES, 16), 16)
                turned = swap8([turn[r, rows, :] for r in range(8)], rolled=True)
                for g in range(GROUPS):
                    coefficient = (lift_ref if term == 0 else grip_ref)[a, g, at, :]
                    value = jnp.exp((0.4 if term == 0 else 0.25) * turned[g]) * coefficient
                    if g == 0:
                        sent = jnp.where(first & ~half, 0.0, value)
                        value = jnp.where(first & half, 0.0, value)
                        halo_out[a, term, at, :] = sent.astype(jnp.bfloat16)
                    spread(gathered, term * base, a, g, at, value.astype(jnp.bfloat16))
                    if a in (0, 3):
                        edge[term, g, padded, :] = value
                        if g == 0:
                            edge_send[term, padded, :] = sent

        if a == 0:
            pl.semaphore_wait(barrier, group + 1)
        halo_copy(a).start()
        if a in (0, 3):
            slot = 4 if a == 0 else 5

            @pl.loop(0, 8)
            def _(c):
                at = pl.ds(pl.multiple_of(c * 16, 16), 16)
                moved = pl.ds(c * 16 + (9 if a == 0 else 7), 16)
                for term in range(2):
                    for g in range(GROUPS):
                        value = edge[term, g, moved, :].astype(jnp.bfloat16)
                        spot(gathered, term * base, 3 - a, g, at, 2 if a == 0 else 0, value)
                    halo_out[slot, term, at, :] = edge_send[term, moved, :].astype(jnp.bfloat16)

            halo_copy(slot).start()

    for slot in (0, 4, 1, 2, 3, 5):
        halo_copy(slot).wait()
        for term in range(2):
            value = halo_in[slot, term]
            if slot < 4:
                spread(gathered, term * base, slot, GROUPS, slice(None), value)
            else:
                spot(gathered, term * base, 3 if slot == 4 else 0, GROUPS, slice(None), 2 if slot == 4 else 0, value)

    per_chunk = CHUNK * outer // (2 * LANES)
    home = block_here // per_chunk

    def out_copy(block):
        return pltpu.make_async_remote_copy(
            src_ref=staged.at[block],
            dst_ref=out_ref.at[mine],
            send_sem=out_send.at[block],
            recv_sem=out_recv.at[mine],
            device_id=owner(block),
            device_id_type=MESH,
        )

    def scale_copy(block):
        return pltpu.make_async_remote_copy(
            src_ref=factor.at[block // per_chunk],
            dst_ref=scale_ref.at[mine],
            send_sem=scale_send.at[block],
            recv_sem=scale_recv.at[mine],
            device_id=owner(block),
            device_id_type=MESH,
        )

    chunks = LANES // CHUNK

    @pl.loop(0, chunks)
    def _(step):
        turn_by = jnp.where(step == 0, 2, jnp.where(step == 1, 1, jnp.where(step == 2, 3, 0)))
        chunk = lax.rem(home + turn_by, chunks)
        at = pl.ds(pl.multiple_of(chunk * CHUNK, CHUNK), CHUNK)
        inv_copy(chunk).wait()
        cells = gathered[:, :, at, :].reshape(4 * GROUPS * CHUNK, gathered.shape[-1])
        low = None
        for pair in range(band_ref.shape[-1] // (2 * PHASE)):
            lanes = slice(pair * 2 * PHASE, (pair + 1) * 2 * PHASE)
            ratio = jnp.dot(cells, band_ref[:, lanes], preferred_element_type=jnp.float32) * inv[chunk, :, lanes]
            least = jnp.minimum(ratio[:, 0:PHASE], ratio[:, PHASE:])
            low = least if low is None else jnp.minimum(low, least)
        largest = jnp.maximum(jnp.max(low), 1e-30)
        low = low.reshape(4, GROUPS, CHUNK, LANES)
        for a in range(4):
            turned = swap8([low[a, g] for g in range(GROUPS)])
            for r in range(8):
                natural[pl.ds(8 * a + r, CHUNK, stride=32), :] = turned[r]
        spread_by = jnp.full((8, LANES), largest, jnp.float32)
        factor[chunk] = jnp.sqrt(spread_by) * (1.0 / 65535.0)
        upward = (65535.0 * lax.rsqrt(spread_by))[0:1, :]
        for block in range(per_chunk):
            for part in range(2):
                rows = slice((block * 2 + part) * LANES, (block * 2 + part + 1) * LANES)
                code = (jnp.sqrt(natural[rows, :]) * upward + 0.5).astype(jnp.int32) - 32768
                staged[chunk * per_chunk + block, :, part * LANES : (part + 1) * LANES] = code.T.astype(jnp.int16)

        @pl.loop(0, per_chunk)
        def _(i):
            block = chunk * per_chunk + i

            @pl.when(block != block_here)
            def _():
                out_copy(block).start()
                scale_copy(block).start()

    out_ref[mine] = staged[block_here]
    scale_ref[mine] = factor[home]

    @pl.loop(1, group)
    def _(turned):
        block = lax.rem(block_here + turned, group)
        out_copy(block).wait_send()
        scale_copy(block).wait_send()
        source = lax.rem(mine + turned, group)
        pltpu.make_async_remote_copy(
            src_ref=staged.at[0], dst_ref=out_ref.at[source], send_sem=out_send.at[block],
            recv_sem=out_recv.at[source], device_id=owner(block), device_id_type=MESH,
        ).wait_recv()
        pltpu.make_async_remote_copy(
            src_ref=factor.at[0], dst_ref=scale_ref.at[source], send_sem=scale_send.at[block],
            recv_sem=scale_recv.at[source], device_id=owner(block), device_id_type=MESH,
        ).wait_recv()


def strip_safety(held, lift, grip, band, inv, row_count, cols):
    outer = held.shape[0]
    length = outer * LANES
    group = 2 * cols
    chunks = LANES // CHUNK
    vmem = pl.BlockSpec(memory_space=pltpu.VMEM)
    dma = pltpu.SemaphoreType.DMA
    return pl.pallas_call(
        functools.partial(strip_kernel, (row_count, cols)),
        out_shape=[
            jax.ShapeDtypeStruct((group, LANES, 2 * LANES), jnp.int16),
            jax.ShapeDtypeStruct((group, 8, LANES), jnp.float32),
        ],
        in_specs=[vmem] * 8 + [pl.BlockSpec(memory_space=pl.ANY)],
        out_specs=[vmem, vmem],
        scratch_shapes=[
            pltpu.VMEM((outer, LANES, 2 * LANES), jnp.float32),
            pltpu.VMEM((8, 2 * LANES, LANES), jnp.float32),
            pltpu.VMEM((4, GROUPS, LANES, 12 * LANES), jnp.bfloat16),
            pltpu.VMEM((2, GROUPS, LANES + 16, LANES), jnp.float32),
            pltpu.VMEM((2, LANES + 16, LANES), jnp.float32),
            pltpu.VMEM((6, 2, LANES, LANES), jnp.bfloat16),
            pltpu.VMEM((6, 2, LANES, LANES), jnp.bfloat16),
            pltpu.VMEM(inv.shape, jnp.float32),
            pltpu.VMEM((length // chunks, LANES), jnp.float32),
            pltpu.VMEM((group, LANES, 2 * LANES), jnp.int16),
            pltpu.VMEM((chunks, 8, LANES), jnp.float32),
            dma((chunks,)), dma((6,)), dma((6,)), dma((group,)), dma((group,)), dma((group,)), dma((group,)),
        ],
        compiler_params=pltpu.CompilerParams(
            vmem_limit_bytes=60 << 20, collective_id=0, has_side_effects=True
        ),
    )(held, *tables(length, 0), lift, grip, band, inv)


def strip_body(noise, elevation_library, tile_choice_index, family_heading_index, family_extent_index):
    side_cells = noise.shape[2]
    row_count, cols = lax.axis_size("row"), lax.axis_size("col")
    row, col, side = (lax.axis_index(axis) for axis in ("row", "col", "orient"))
    strips = row_count * cols * 2
    lines = noise.shape[1] // 2
    strip = strip_of(row, col, side, cols)

    own = lax.dynamic_slice_in_dim(noise, side * lines, lines, 1)
    first_line = lax.axis_index(("row", "col", "orient")) * lines
    v_index = first_line + lax.broadcasted_iota(jnp.int32, (lines, side_cells), 0)
    u_index = lax.broadcasted_iota(jnp.int32, (lines, side_cells), 1)
    weights = own * amplitude(u_index, v_index, side_cells)[None]
    spectrum = rows_transform(weights, cols)

    families = jnp.stack([family_heading_index, family_extent_index])
    families = lax.all_gather(families, "orient", axis=1, tiled=True)
    choices = lax.all_gather(tile_choice_index, "col", axis=1, tiled=True)
    choices = lax.all_gather(choices, "row", axis=0, tiled=True)
    spectrum, choices, families = lax.optimization_barrier((spectrum, choices, families))
    held = lax.all_to_all(spectrum, ("row", "col", "orient"), split_axis=0, concat_axis=0, tiled=True)

    near = [lax.dynamic_slice_in_dim(choices, (strip + strips + d) % strips, 1, 0) for d in (-1, 0, 1)]
    library = jnp.roll(elevation_library.transpose(0, 2, 1), R, axis=2)
    band = band_weights(families[0], families[1])
    lift, grip, inv = prepare(jnp.concatenate(near), jnp.full((1,), strip, jnp.int32), library, band[1].reshape(-1, band.shape[-1]))
    band = band.reshape(-1, band.shape[-1])
    held, lift, grip, inv, band = lax.optimization_barrier((held, lift, grip, inv, band))
    code, scale = strip_safety(held, lift, grip, band, inv, row_count, cols)
    root = (code.astype(jnp.float32) + 32768.0) * scale[:, 0:1, 0:1]
    return (root * root).reshape(-1, code.shape[2])


def chosen_body(noise, elevation_library, tile_choice_index, family_heading_index, family_extent_index):
    shape = (lax.axis_size("row"), lax.axis_size("col"), lax.axis_size("orient"))
    side_cells = noise.shape[2]
    fits = (
        shape[2] == 2
        and shape[0] * shape[1] * 2 == 32
        and shape[1] == 8
        and side_cells == 32 * LANES
        and elevation_library.shape[1] == LANES
        and family_heading_index.shape[0] * 2 == 8
    )
    chosen = strip_body if fits else body
    return chosen(noise, elevation_library, tile_choice_index, family_heading_index, family_extent_index)


def solution(mesh):
    placed = (P(None, ("row", "col"), None), P(), P("row", "col"), P("orient"), P("orient"))
    return jax.shard_map(
        chosen_body, mesh=mesh, in_specs=placed, out_specs=P("row", ("col", "orient")), check_vma=False
    )
```

```python
import functools
import math

import jax
import jax.numpy as jnp
import numpy as np
from jax import lax
from jax.experimental import pallas as pl
from jax.experimental.pallas import tpu as pltpu
from jax.sharding import PartitionSpec as P

R = 8
N_AZ = 36
NSIZE = 4
LANES = 128
TILE_ROWS = 8
TILE_LANES = 16
GROUPS = LANES // TILE_LANES
PHASE = TILE_ROWS * TILE_LANES
STEP_TILES = 8

nugget_share = 0.3
peak_share = 1024.0 / (2.0 * math.pi)
cutoff_ratio = 32.0


def amplitude(u_index, v_index, side_cells):
    wrap_u = jnp.minimum(u_index, side_cells - u_index).astype(jnp.float32)
    wrap_v = jnp.minimum(v_index, side_cells - v_index).astype(jnp.float32)
    cutoff = side_cells / cutoff_ratio
    scaled_u = wrap_u / cutoff
    scaled_v = wrap_v / cutoff
    grown = 1.0 + scaled_u * scaled_u + scaled_v * scaled_v
    spectrum = nugget_share + peak_share / (grown * jnp.sqrt(grown))
    return jnp.sqrt(spectrum) / side_cells


def ellipsoid(offset_u, offset_v, azimuth, size_index):
    heading = azimuth.astype(jnp.float32) * (math.pi / N_AZ)
    semi_axis = R * (size_index.astype(jnp.float32) + (1 + NSIZE)) / (2 * NSIZE)
    across = 0.6 * semi_axis
    slip_depth = 0.3 * semi_axis
    along = offset_u * jnp.cos(heading) + offset_v * jnp.sin(heading)
    lateral = offset_v * jnp.cos(heading) - offset_u * jnp.sin(heading)
    along_part = along / semi_axis
    lateral_part = lateral / across
    inside = 1.0 - along_part * along_part - lateral_part * lateral_part
    height = slip_depth * jnp.sqrt(jnp.maximum(inside, 0.0))
    base_share = jnp.clip(4.0 * inside, 0.0, 1.0)
    return (height, base_share)


def small_dft(parts):
    count = len(parts)
    if count == 1:
        return parts
    even = small_dft(parts[0::2])
    odd = small_dft(parts[1::2])
    low, high = [], []
    for k in range(count // 2):
        (a, b), (c, d) = even[k], odd[k]
        if k == 0:
            e, f = c, d
        elif 4 * k == count:
            e, f = d, -c
        else:
            cos = math.cos(2 * math.pi * k / count)
            sin = math.sin(2 * math.pi * k / count)
            e, f = c * cos + d * sin, d * cos - c * sin
        low.append((a + e, b + f))
        high.append((a - e, b - f))
    return low + high


def transform_kernel(planes, blocks, span, step, pad, in_ref, cos_ref, sin_ref, big_ref, small_ref, out_ref, mid, full):
    outer = cos_ref.shape[0]
    rows = mid.shape[1]
    unit = 16 if planes else 8

    @pl.loop(0, rows // unit)
    def _(block):
        at = pl.ds(pl.multiple_of(block * unit, unit), unit)
        parts = []
        for p in range(outer):
            if planes:
                parts.append((in_ref[p, 0, at, :].astype(jnp.float32), in_ref[p, 1, at, :].astype(jnp.float32)))
            else:
                lanes = slice(p * LANES, (p + 1) * LANES)
                parts.append((in_ref[0, at, lanes], in_ref[1, at, lanes]))
        for k, (re, im) in enumerate(small_dft(parts)):
            cos = cos_ref[k : k + 1, :]
            sin = sin_ref[k : k + 1, :]
            mid[k, at, 0:LANES] = re * cos + im * sin
            mid[k, at, LANES : 2 * LANES] = im * cos - re * sin

    if pad:
        edge = jnp.zeros((pad, rows), jnp.float32)
        for part in range(2):
            full[part, 0:pad, :] = edge
            full[part, pad + outer * LANES : 2 * pad + outer * LANES, :] = edge

    turned = (((1,), (1,)), ((), ()))
    dot = functools.partial(lax.dot_general, dimension_numbers=turned, preferred_element_type=jnp.float32)
    for k in range(outer):
        value = mid[k]
        high = value.astype(jnp.bfloat16)
        rest = (value - high.astype(jnp.float32)).astype(jnp.bfloat16)
        got = dot(big_ref[...], high) + dot(big_ref[...], rest) + dot(small_ref[...], high)
        full[0, pl.ds(pad + k, LANES, stride=outer), :] = got[0:LANES]
        full[1, pl.ds(pad + k, LANES, stride=outer), :] = got[LANES : 2 * LANES]

    @pl.loop(0, blocks)
    def _(block):
        at = pl.ds(pl.multiple_of(block * step, 8), span)
        for part in range(2):
            out_ref[block, part] = full[part, at, :].astype(jnp.bfloat16)


def transform(cells, planes, rows, length, blocks, pad):
    outer = length // LANES
    step = length // blocks
    span = step + 2 * pad
    k = np.arange(outer)[:, None]
    q = np.arange(LANES)
    turn = 2 * np.pi * k * q / length
    cos, sin = np.cos(turn).astype(np.float32), np.sin(turn).astype(np.float32)
    angle = 2 * np.pi * (q[:, None] * q % LANES) / LANES
    table = np.block([[np.cos(angle), np.sin(angle)], [-np.sin(angle), np.cos(angle)]]).astype(np.float32)
    big = table.astype(jnp.bfloat16)
    small = (table - big.astype(np.float32)).astype(jnp.bfloat16)
    vmem = pl.BlockSpec(memory_space=pltpu.VMEM)
    return pl.pallas_call(
        functools.partial(transform_kernel, planes, blocks, span, step, pad),
        out_shape=jax.ShapeDtypeStruct((blocks, 2, span, rows), jnp.bfloat16),
        in_specs=[vmem] * 5,
        out_specs=vmem,
        scratch_shapes=[
            pltpu.VMEM((outer, rows, 2 * LANES), jnp.float32),
            pltpu.VMEM((2, length + 2 * pad, rows), jnp.float32),
        ],
        compiler_params=pltpu.CompilerParams(vmem_limit_bytes=40 << 20),
    )(cells, cos, sin, big, small)


def swap_groups(cells):
    row = lax.broadcasted_iota(jnp.int32, cells.shape, 1)
    group = lax.broadcasted_iota(jnp.int32, cells.shape, 2) // TILE_LANES
    skewed = pltpu.roll(cells, 0, 2, stride=TILE_LANES, stride_axis=1)
    picked = jnp.take_along_axis(skewed, (group + row - 7) & 7, axis=1)
    level = pltpu.roll(picked, TILE_LANES, 2, stride=TILE_LANES, stride_axis=1)
    return jnp.take_along_axis(level, 7 - row, axis=1)


def gather_tiles(term_ref, swapped, gathered):
    tiles, across = gathered.shape[1:3]
    chunks = across // GROUPS

    @pl.when(pl.program_id(0) == 0)
    def _():
        @pl.loop(0, tiles // 2)
        def _(pair):
            at = pl.ds(pl.multiple_of(pair * 16, 16), 16)
            both = pl.ds(pair * 2, 2)
            for term in range(gathered.shape[0]):
                for chunk in range(chunks + 1):
                    cells = term_ref[term, at, chunk * LANES : (chunk + 1) * LANES].astype(jnp.float32)
                    turned = swap_groups(cells.reshape(2, TILE_ROWS, LANES))
                    swapped[:, chunk * GROUPS : (chunk + 1) * GROUPS, :] = turned
                gathered[term, both, :, 0:PHASE] = swapped[:, 0:across, :].astype(jnp.bfloat16)
                gathered[term, both, :, PHASE:] = swapped[:, 1 : across + 1, :].astype(jnp.bfloat16)


def column_sum(gathered, band_ref, lanes):
    terms, _, across, depth = gathered.shape
    tile = pl.program_id(0) * STEP_TILES
    pieces = [(term, shift) for term in range(terms) for shift in range(3)]
    left = [gathered[term, pl.ds(tile + shift, STEP_TILES)] for term, shift in pieces]
    left = [piece.reshape(STEP_TILES * across, depth) for piece in left]
    right = [band_ref[term, shift, :, lanes] for term, shift in pieces]
    return jnp.dot(
        jnp.concatenate(left, axis=1),
        jnp.concatenate(right, axis=0),
        preferred_element_type=jnp.float32,
    )


def driving_kernel(families, term_ref, band_ref, out_ref, swapped, gathered):
    gather_tiles(term_ref, swapped, gathered)
    for pair in range(families // 2):
        lanes = slice(pair * 2 * PHASE, (pair + 1) * 2 * PHASE)
        out_ref[:, lanes] = column_sum(gathered, band_ref, lanes)


def stability_kernel(families, term_ref, band_ref, drive_ref, out_ref, swapped, gathered):
    chunks = gathered.shape[2] // GROUPS
    gather_tiles(term_ref, swapped, gathered)
    low = None
    for pair in range(families // 2):
        lanes = slice(pair * 2 * PHASE, (pair + 1) * 2 * PHASE)
        ratio = column_sum(gathered, band_ref, lanes) / drive_ref[:, lanes]
        least = jnp.minimum(ratio[:, 0:PHASE], ratio[:, PHASE:])
        low = least if low is None else jnp.minimum(low, least)
    turned = swap_groups(low.reshape(STEP_TILES * chunks, TILE_ROWS, LANES))
    for side in range(STEP_TILES):
        for chunk in range(chunks):
            out_ref[side * 8 : side * 8 + 8, chunk * LANES : (chunk + 1) * LANES] = turned[side * chunks + chunk]


def tile_call(kernel, terms, band, height, width, out_shape, out_block, more=()):
    families = band.shape[-1] // PHASE
    across = width // TILE_LANES
    tiles = height // TILE_ROWS + 2
    count = terms.shape[0]
    work = 2 * (height // TILE_ROWS) * across * band.size
    return pl.pallas_call(
        functools.partial(kernel, families),
        grid=(height // (TILE_ROWS * STEP_TILES),),
        out_shape=jax.ShapeDtypeStruct(out_shape, jnp.float32),
        in_specs=[
            pl.BlockSpec(terms.shape, lambda i: (0, 0, 0), pipeline_mode=pl.Buffered(1)),
            pl.BlockSpec(band.shape, lambda i: (0, 0, 0, 0), pipeline_mode=pl.Buffered(1)),
        ]
        + [pl.BlockSpec((STEP_TILES * across, cells.shape[1]), lambda i: (i, 0)) for cells in more],
        out_specs=pl.BlockSpec(out_block, lambda i: (i, 0)),
        scratch_shapes=[
            pltpu.VMEM((2, across + GROUPS, LANES), jnp.float32),
            pltpu.VMEM((count, tiles, across, 2 * PHASE), jnp.bfloat16),
        ],
        compiler_params=pltpu.CompilerParams(vmem_limit_bytes=56 << 20),
        cost_estimate=pl.CostEstimate(flops=work, bytes_accessed=16 << 20, transcendentals=0),
    )(terms, band, *more)


def extended(cells, sides, width):
    for axis, dim in sides:
        ends = lax.axis_size(axis) - 1
        head = lax.slice_in_dim(cells, 0, width, axis=dim)
        tail = lax.slice_in_dim(cells, cells.shape[dim] - width, cells.shape[dim], axis=dim)
        before = lax.ppermute(tail, axis, [(i, i + 1) for i in range(ends)])
        after = lax.ppermute(head, axis, [(i + 1, i) for i in range(ends)])
        cells = jnp.concatenate([before, cells, after], axis=dim)
    return cells


def band_weights(headings, extents):
    shape = (3, 2, TILE_ROWS, TILE_LANES, TILE_ROWS, TILE_LANES)
    index = [lax.broadcasted_iota(jnp.int32, shape, axis) for axis in range(6)]
    offset_v = TILE_ROWS * index[0] + index[2] - R - index[4]
    offset_u = TILE_LANES * index[1] + index[3] - R - index[5]
    keep = (jnp.abs(offset_v) <= R) & (jnp.abs(offset_u) <= R)
    rows = 3 * 2 * PHASE

    def flat(cells):
        return cells.reshape(rows, 1, PHASE)

    heights, shares = ellipsoid(
        flat(offset_u.astype(jnp.float32)),
        flat(offset_v.astype(jnp.float32)),
        headings[None, :, None],
        extents[None, :, None],
    )
    keep = flat(keep)
    count = headings.shape[0]

    def whole(cells):
        return jnp.where(keep, cells, 0.0).astype(jnp.bfloat16).reshape(3, 2 * PHASE, count * PHASE)

    heights = whole(heights)
    return jnp.stack([whole(shares), heights])


def pick_tiles(library, index):
    def copy_kernel(index_ref, in_ref, out_ref):
        out_ref[...] = in_ref[...]

    block = (1,) + library.shape[1:]
    flat = index.reshape(-1)
    picked = pl.pallas_call(
        copy_kernel,
        out_shape=jax.ShapeDtypeStruct(flat.shape + library.shape[1:], library.dtype),
        grid_spec=pltpu.PrefetchScalarGridSpec(
            num_scalar_prefetch=1,
            grid=flat.shape,
            in_specs=[pl.BlockSpec(block, lambda i, index_ref: (index_ref[i], 0, 0))],
            out_specs=pl.BlockSpec(block, lambda i, index_ref: (i, 0, 0)),
        ),
    )(flat, library)
    return picked.reshape(index.shape + library.shape[1:])


def body(noise, elevation_library, tile_choice_index, family_heading_index, family_extent_index):
    side_cells = noise.shape[2]
    row_count = lax.axis_size("row")
    col_count = lax.axis_size("col")
    split = lax.axis_size("orient")
    row, col, side = (lax.axis_index(axis) for axis in ("row", "col", "orient"))
    devices = row_count * col_count * split
    lines = noise.shape[1] // split
    window_rows = side_cells // row_count
    window_columns = side_cells // (col_count * split)

    families = jnp.stack([family_heading_index, family_extent_index])
    held_families = [families]
    for turn in range(1, split):
        pairs = [(i, (i + turn) % split) for i in range(split)]
        held_families.append(lax.ppermute(families, "orient", pairs))
    families = jnp.concatenate(held_families, axis=1)
    choices = extended(tile_choice_index, (("row", 0), ("col", 1)), 1)

    own = lax.dynamic_slice_in_dim(noise, side * lines, lines, 1)
    first_line = lax.axis_index(("row", "col", "orient")) * lines
    v_index = first_line + lax.broadcasted_iota(jnp.int32, (lines, side_cells), 0)
    u_index = lax.broadcasted_iota(jnp.int32, (lines, side_cells), 1)
    weights = own * amplitude(u_index, v_index, side_cells)[None]
    spectrum = transform(weights, False, lines, side_cells, devices, 0)
    spectrum, choices, families = lax.optimization_barrier((spectrum, choices, families))
    held = lax.all_to_all(spectrum, ("row", "col", "orient"), split_axis=0, concat_axis=0, tiled=True)
    tall = window_columns + 2 * R
    wide = (window_rows // LANES + 1) * LANES
    spare = wide - window_rows - 2 * R
    tile_side = elevation_library.shape[1]
    tiles_x = window_rows // tile_side
    tiles_y = window_columns // tile_side
    first_y = col * split + side
    local = lax.dynamic_slice_in_dim(choices, side * tiles_y, tiles_y + 2, 1)
    slope = pick_tiles(elevation_library.transpose(0, 2, 1), local.T)
    slope = slope.transpose(0, 2, 1, 3).reshape((tiles_y + 2) * tile_side, (tiles_x + 2) * tile_side)
    edge = tile_side - R
    slope = slope[edge : edge + tall, edge : edge + wide]
    y = first_y * window_columns - R + lax.broadcasted_iota(jnp.int32, (tall, wide), 0)
    x = row * window_rows - R + lax.broadcasted_iota(jnp.int32, (tall, wide), 1)
    inside = (y >= 0) & (y < side_cells) & (x >= 0) & (x < side_cells)
    secant = jnp.sqrt(1.0 + slope * slope)
    lift = jnp.where(inside, 0.5 * secant, 0.0)
    grip = jnp.where(inside, 0.6 / secant, 0.0)
    drive = jnp.where(inside, slope / secant, 0.0).astype(jnp.bfloat16)
    band = band_weights(families[0], families[1])
    held, lift, grip, drive = lax.optimization_barrier((held, lift, grip, drive))
    positions = side_cells // devices
    per_block = LANES // lines
    held = held.reshape(side_cells // LANES, per_block, 2, positions, lines)
    held = held.transpose(0, 2, 3, 1, 4).reshape(side_cells // LANES, 2, positions, LANES)
    fields = transform(held, True, positions, side_cells, col_count * split, R)
    fields = lax.all_to_all(fields, ("col", "orient"), split_axis=0, concat_axis=0, tiled=True)
    across = window_rows // TILE_LANES
    driving = tile_call(
        driving_kernel,
        drive[None],
        band[1:],
        window_columns,
        window_rows,
        (window_columns // TILE_ROWS * across, band.shape[-1]),
        (STEP_TILES * across, band.shape[-1]),
    )
    fields, driving, band = lax.optimization_barrier((fields, driving, band))
    fields = fields.transpose(1, 2, 0, 3).reshape(2, tall, window_rows)
    ends = row_count - 1
    before = lax.ppermute(fields[:, :, window_rows - R :], "row", [(i, i + 1) for i in range(ends)])
    after = lax.ppermute(fields[:, :, :R], "row", [(i + 1, i) for i in range(ends)])
    fields = jnp.concatenate(
        [before, fields, after, jnp.zeros((2, tall, spare), fields.dtype)], axis=2
    ).astype(jnp.float32)

    cohesion = (jnp.exp(0.4 * fields[0]) * lift).astype(jnp.bfloat16)
    friction = (jnp.exp(0.25 * fields[1]) * grip).astype(jnp.bfloat16)
    safety = tile_call(
        stability_kernel,
        jnp.stack([cohesion, friction]),
        band,
        window_columns,
        window_rows,
        (window_columns, window_rows),
        (TILE_ROWS * STEP_TILES, window_rows),
        (driving,),
    )
    return safety.T


TURNED = (((1,), (1,)), ((), ()))
DOT = functools.partial(lax.dot_general, dimension_numbers=TURNED, preferred_element_type=jnp.float32)
MESH = pl.DeviceIdType.MESH
CHUNK = 32
CHUNKS = LANES // CHUNK
SPLIT = 5
TERM = 6 * LANES


def strip_of(row, col, side, cols):
    return row * (2 * cols) + col + side * (2 * cols - 1 - 2 * col)


def place_of(strip, cols):
    row = strip // (2 * cols)
    at = strip % (2 * cols)
    side = at // cols
    return row, at + side * (2 * cols - 1 - 2 * at), side


def tables(length):
    outer = length // LANES
    q = np.arange(LANES)
    turns = []
    for shift in (R, 0):
        turn = 2 * np.pi * (np.arange(outer)[:, None] - shift) * q / length
        turns += [np.cos(turn), np.sin(turn)]
    angle = 2 * np.pi * (q[:, None] * q % LANES) / LANES
    table = np.block([[np.cos(angle), np.sin(angle)], [-np.sin(angle), np.cos(angle)]]).astype(np.float32)
    big = table.astype(jnp.bfloat16)
    small = (table - big.astype(np.float32)).astype(jnp.bfloat16)
    u = np.arange(length)
    wrapped = np.minimum(u, length - u) / (length / cutoff_ratio)
    turns.append((wrapped * wrapped).reshape(outer, LANES))
    return np.stack(turns).astype(np.float32), np.concatenate([big, big, small], axis=1)


def swap8(cells):
    cells = [pltpu.roll(c, TILE_LANES * i, 1) if i else c for i, c in enumerate(cells)]
    group = lax.broadcasted_iota(jnp.int32, cells[0].shape, 1) // TILE_LANES
    for bit in (1, 2, 4):
        pick = (group & bit) != 0
        cells = [jnp.where(pick, cells[(i + bit) % GROUPS], cells[i]) for i in range(GROUPS)]
    out = []
    for i in range(GROUPS):
        c = cells[-i % GROUPS]
        out.append(pltpu.roll(c, LANES - TILE_LANES * i, 1) if i else c)
    return out


def pair_dot(wide, first, second):
    value = jnp.concatenate([first, second], axis=0)
    high = value.astype(jnp.bfloat16)
    rest = (value - high.astype(jnp.float32)).astype(jnp.bfloat16)
    return DOT(wide, jnp.concatenate([high, rest, high], axis=1))


def spread(into, base, a, g, at, value):
    for shift in range(3):
        to = a + 1 - shift
        if 0 <= to < 4:
            spot(into, base, to, g, at, shift, value)


def spot(into, base, to, g, at, shift, value):
    first = base + shift * 2 * LANES
    if g < GROUPS:
        into[to, g, at, first : first + LANES] = value
    if g > 0:
        into[to, g - 1, at, first + LANES : first + 2 * LANES] = value


def band_rows(family_ref, band, side):
    params = []
    for owner in range(2):
        both = family_ref[owner].astype(jnp.float32)
        heading = both[0:4] * (math.pi / N_AZ)
        semi_axis = R * (both[4:8] + (1 + NSIZE)) / (2 * NSIZE)
        params.append((jnp.cos(heading), jnp.sin(heading), 1.0 / semi_axis, 1.0 / (0.6 * semi_axis), 0.3 * semi_axis))
    shape = (16, LANES)
    lane = lax.broadcasted_iota(jnp.int32, shape, 1)
    row = lax.broadcasted_iota(jnp.int32, shape, 0)

    @pl.loop(0, TERM // 16)
    def _(block):
        offset_v = TILE_ROWS * (block // 16) + block % 8 - R - lane // TILE_LANES
        offset_u = TILE_LANES * (block // 8 % 2) - R + row - lane % TILE_LANES
        keep = (jnp.abs(offset_v) <= R) & (jnp.abs(offset_u) <= R)
        v = offset_v.astype(jnp.float32)
        u = offset_u.astype(jnp.float32)
        at = pl.multiple_of(block * 16, 16)
        for family in range(8):
            cos, sin, per_semi, per_across, slip_depth = [p[family % 4 : family % 4 + 1] for p in params[family // 4]]
            along = (u * cos + v * sin) * per_semi
            lateral = (v * cos - u * sin) * per_across
            inside = 1.0 - along * along - lateral * lateral
            height = slip_depth * jnp.sqrt(jnp.maximum(inside, 0.0))
            share = jnp.clip(4.0 * inside, 0.0, 1.0)
            lanes = slice(family * LANES, (family + 1) * LANES)
            band[pl.ds(at, 16), lanes] = jnp.where(keep, share, 0.0).astype(jnp.bfloat16)
            band[pl.ds(at + TERM, 16), lanes] = jnp.where(keep, height, 0.0).astype(jnp.bfloat16)


def whole_kernel(
    sizes, noise_any, choice_ref, heading_ref, extent_ref, lib_ref, turn_ref, wide_ref,
    out_ref, scale_ref,
    mid, full, send_a, send_b, held_a, held_b, lift, grip, gathered, inv, band, edge, edge_send, halo_out, halo_in,
    natural, staged, factor, choice_in, family_in, choice_smem,
    noise_sem, first_send, first_recv, choice_send, choice_recv, family_send, family_recv, smem_sem,
    halo_send, halo_recv, out_send, out_recv, scale_send, scale_recv,
):
    row_count, cols = sizes
    row, col, side = (lax.axis_index(axis) for axis in ("row", "col", "orient"))
    devices = row_count * cols * 2
    group = cols * 2
    me = (row * cols + col) * 2 + side
    strip = strip_of(row, col, side, cols)
    mine = strip % group
    block_here = col * 2 + side
    plane = row * cols + col
    left = place_of(lax.rem(strip + devices - 1, devices), cols)
    outer = turn_ref.shape[1]

    def device(index):
        return index // group, index % group // 2, index % 2

    def owner(block):
        return row, block // 2, block % 2

    barrier = pltpu.get_barrier_semaphore()

    @pl.loop(1, devices)
    def _(k):
        pl.semaphore_signal(barrier, inc=1, device_id=device(lax.rem(me + k, devices)), device_id_type=MESH)

    def noise_copy(chunk, part, piece):
        lines = pl.ds(pl.multiple_of(side * LANES + chunk * CHUNK, CHUNK), CHUNK)
        return pltpu.make_async_copy(
            noise_any.at[part, lines, piece * 1024 : (piece + 1) * 1024],
            inv.at[0, part * 2 + piece // 2, piece % 2 * 4 + chunk],
            noise_sem.at[chunk, part * 4 + piece],
        )

    for chunk in range(CHUNKS):
        for part in range(2):
            for piece in range(4):
                noise_copy(chunk, part, piece).start()

    choice_in[plane] = jnp.zeros((16, LANES), jnp.int32)
    choice_in[plane, :, 0 : choice_ref.shape[1]] = choice_ref[...]
    which = lax.broadcasted_iota(jnp.int32, (8, LANES), 0)
    mixed = jnp.zeros((8, LANES), jnp.int32)
    for f in range(4):
        mixed = jnp.where(which == f, heading_ref[f], mixed)
        mixed = jnp.where(which == f + 4, extent_ref[f], mixed)
    family_in[side] = mixed

    for chunk in range(CHUNKS):
        for part in range(2):
            for piece in range(4):
                noise_copy(chunk, part, piece).wait()

        @pl.loop(0, CHUNK // 8)
        def _(block):
            at = pl.ds(pl.multiple_of(block * 8, 8), 8)
            line = me * LANES + chunk * CHUNK + block * 8 + lax.broadcasted_iota(jnp.int32, (8, LANES), 0)
            wrap_v = jnp.minimum(line, outer * LANES - line).astype(jnp.float32) * (cutoff_ratio / (outer * LANES))
            base = 1.0 + wrap_v * wrap_v
            parts = []
            for p in range(outer):
                root = lax.rsqrt(base + turn_ref[4, p : p + 1, :])
                spectrum = nugget_share + peak_share * (root * root * root)
                level = spectrum * lax.rsqrt(spectrum) * (1.0 / (outer * LANES))
                spot_at = (p // 16, p // 8 % 2 * 4 + chunk, at, slice(p % 8 * LANES, (p % 8 + 1) * LANES))
                parts.append((inv[(0,) + spot_at] * level, inv[(0, 2 + spot_at[0]) + spot_at[1:]] * level))
            turned = small_dft(parts)
            rows = pl.ds(pl.multiple_of(chunk * CHUNK + block * 8, 8), 8)
            for k in range(outer):
                re, im = turned[(k - R) % outer]
                cos = turn_ref[0, k : k + 1, :]
                sin = turn_ref[1, k : k + 1, :]
                mid[k, rows, 0:LANES] = re * cos + im * sin
                mid[k, rows, LANES : 2 * LANES] = im * cos - re * sin

    pl.semaphore_wait(barrier, devices - 1)

    def choice_copy(k):
        to = lax.rem(plane + k, row_count * cols)
        return pltpu.make_async_remote_copy(
            src_ref=choice_in.at[plane], dst_ref=choice_in.at[plane],
            send_sem=choice_send.at[k], recv_sem=choice_recv.at[k],
            device_id=(to // cols, to % cols, side), device_id_type=MESH,
        )

    def family_copy():
        return pltpu.make_async_remote_copy(
            src_ref=family_in.at[side], dst_ref=family_in.at[side], send_sem=family_send, recv_sem=family_recv,
            device_id=(row, col, 1 - side), device_id_type=MESH,
        )

    @pl.loop(1, row_count * cols)
    def _(k):
        choice_copy(k).start()

    family_copy().start()

    for k in range(0, outer, 2):
        got = pair_dot(wide_ref[...], mid[k], mid[k + 1])
        for part in range(2):
            for one in range(2):
                piece = got[part * LANES : (part + 1) * LANES, one * LANES : (one + 1) * LANES]
                full[part, pl.ds(k + one, LANES, stride=outer), :] = piece

    parts_of = ((0, SPLIT, send_a, held_a), (SPLIT, GROUPS, send_b, held_b))

    def first_copy(c, k):
        to = lax.rem(me + k, devices)
        return pltpu.make_async_remote_copy(
            src_ref=parts_of[c][2].at[to], dst_ref=parts_of[c][3].at[me],
            send_sem=first_send.at[c, k], recv_sem=first_recv.at[c, k],
            device_id=device(to), device_id_type=MESH,
        )

    for c, (low_g, high_g, send, held) in enumerate(parts_of):
        count = (high_g - low_g) * 16

        def packed(to, into):
            to_strip = strip_of(*device(to), cols)
            at = pl.ds(pl.multiple_of(to_strip * LANES + low_g * 16, 16), count)
            for part in range(2):
                into[to, part] = full[part, at, :].astype(jnp.bfloat16)

        @pl.loop(1, devices)
        def _(k):
            packed(lax.rem(me + k, devices), send)
            first_copy(c, k).start()

        packed(me, held)

    family_copy().wait()
    band_rows(family_in, band, side)

    @pl.loop(1, row_count * cols)
    def _(k):
        choice_copy(k).wait()

    to_smem = pltpu.make_async_copy(choice_in, choice_smem, smem_sem)
    to_smem.start()
    to_smem.wait()
    left_lanes = lax.broadcasted_iota(jnp.int32, (LANES, LANES), 1) < R

    def tile(shift, t):
        x = lax.rem(strip + devices + shift, devices)
        return lib_ref[choice_smem[x // 16 * cols + t // 4, x % 16, t % 4]]

    @pl.loop(0, outer)
    def _(t):
        at = pl.ds(pl.multiple_of(t * LANES, LANES), LANES)
        here = tile(0, t)
        full[0, at, :] = jnp.where(left_lanes, tile(-1, t), here)
        full[1, at, :] = jnp.where(left_lanes, here, tile(1, t))

    half = lax.broadcasted_iota(jnp.int32, (16, LANES), 1) % TILE_LANES < R
    first = strip == 0
    last = strip == devices - 1
    for side_rows in (slice(0, 8), slice(8 + LANES, 16 + LANES)):
        edge[:, :, side_rows, :] = jnp.zeros((2, GROUPS + 1, 8, LANES), jnp.float32)
        edge_send[:, side_rows, :] = jnp.zeros((2, 8, LANES), jnp.float32)

    for a in range(4):
        @pl.loop(0, 8)
        def _(c):
            at = pl.ds(pl.multiple_of(c * 16, 16), 16)
            for source in range(2):
                turned = swap8([full[source, pl.ds(c * 512 + 8 * a + r, 16, stride=32), :] for r in range(8)])
                for g in range(GROUPS) if source == 0 else (0,):
                    slope = turned[g]
                    square = 1.0 + slope * slope
                    inverse = lax.rsqrt(square)
                    drive = slope * inverse
                    tile_at = g
                    if source == 0:
                        lift[a, g, at, :] = 0.5 * square * inverse
                        grip[a, g, at, :] = 0.6 * inverse
                        if g == 0:
                            drive = jnp.where(half & first, 0.0, drive)
                    else:
                        tile_at = GROUPS
                        drive = jnp.where(last & ~half, 0.0, drive)
                    spread(gathered, TERM, a, tile_at, at, drive.astype(jnp.bfloat16))
                    if a in (0, 3):
                        edge[0, tile_at, pl.ds(pl.multiple_of(c * 16 + 8, 8), 16), :] = drive

        if a in (0, 3):
            @pl.loop(0, 8)
            def _(c):
                at = pl.ds(pl.multiple_of(c * 16, 16), 16)
                for g in range(GROUPS + 1):
                    value = edge[0, g, pl.ds(c * 16 + (9 if a == 0 else 7), 16), :].astype(jnp.bfloat16)
                    spot(gathered, TERM, 3 - a, g, at, 2 if a == 0 else 0, value)

    pairs = band.shape[1] // (2 * PHASE)

    @pl.loop(0, CHUNKS)
    def _(chunk):
        at = pl.ds(pl.multiple_of(chunk * CHUNK, CHUNK), CHUNK)
        cells = gathered[:, :, at, TERM:].reshape(4 * GROUPS * CHUNK, TERM)
        for pair in range(pairs):
            lanes = slice(pair * 2 * PHASE, (pair + 1) * 2 * PHASE)
            sums = jnp.dot(cells, band[TERM:, lanes], preferred_element_type=jnp.float32)
            inv[chunk, :, :, :, lanes] = (1.0 / sums).reshape(4, GROUPS, CHUNK, 2 * PHASE)

    def halo_copy(slot):
        return pltpu.make_async_remote_copy(
            src_ref=halo_out.at[slot], dst_ref=halo_in.at[slot],
            send_sem=halo_send.at[slot], recv_sem=halo_recv.at[slot],
            device_id=left, device_id_type=MESH,
        )

    per_chunk = CHUNK * outer // (2 * LANES)
    home = block_here // per_chunk

    def out_copy(c, block, source):
        return pltpu.make_async_remote_copy(
            src_ref=staged.at[c, block], dst_ref=out_ref.at[source, c],
            send_sem=out_send.at[c, block], recv_sem=out_recv.at[c, source],
            device_id=owner(block), device_id_type=MESH,
        )

    def scale_copy(c, block, source):
        return pltpu.make_async_remote_copy(
            src_ref=factor.at[c, block // per_chunk], dst_ref=scale_ref.at[source, c],
            send_sem=scale_send.at[c, block], recv_sem=scale_recv.at[c, source],
            device_id=owner(block), device_id_type=MESH,
        )

    for c, (low_g, high_g, send, held) in enumerate(parts_of):
        @pl.loop(1, devices)
        def _(k):
            first_copy(c, k).wait()

        @pl.loop(low_g, high_g)
        def _(g):
            at = pl.ds(pl.multiple_of((g - low_g) * 16, 16), 16)
            parts = [(held[p, 0, at, :].astype(jnp.float32), held[p, 1, at, :].astype(jnp.float32)) for p in range(outer)]
            for k, (re, im) in enumerate(small_dft(parts)):
                to = slice(k % 8 * 16, (k % 8 + 1) * 16)
                cos = turn_ref[2, k : k + 1, :]
                sin = turn_ref[3, k : k + 1, :]
                mid[k // 8 * 8 + g, to, 0:LANES] = re * cos + im * sin
                mid[k // 8 * 8 + g, to, LANES : 2 * LANES] = im * cos - re * sin

        items = [(a, g) for g in range(low_g, high_g) for a in range(4)]
        for at_item in range(0, len(items), 2):
            two = items[at_item : at_item + 2]
            got = pair_dot(wide_ref[...], *[mid[a * 8 + g] for a, g in two])
            for one, (a, g) in enumerate(two):
                for term in range(2):
                    field = got[term * LANES : (term + 1) * LANES, one * LANES : (one + 1) * LANES]
                    value = jnp.exp((0.4 if term == 0 else 0.25) * field) * (lift if term == 0 else grip)[a, g]
                    if g == 0:
                        mask = lax.broadcasted_iota(jnp.int32, (LANES, LANES), 1) % TILE_LANES < R
                        sent = jnp.where(first & ~mask, 0.0, value)
                        value = jnp.where(first & mask, 0.0, value)
                        halo_out[a, term] = sent.astype(jnp.bfloat16)
                    spread(gathered, term * TERM, a, g, slice(None), value.astype(jnp.bfloat16))
                    if a in (0, 3):
                        moved = slice(9, 9 + LANES) if a == 0 else slice(7, 7 + LANES)
                        edge[term, g, 8 : 8 + LANES, :] = value
                        near = edge[term, g, moved, :].astype(jnp.bfloat16)
                        spot(gathered, term * TERM, 3 - a, g, slice(None), 2 if a == 0 else 0, near)
                        if g == 0:
                            edge_send[term, 8 : 8 + LANES, :] = sent
                            halo_out[4 if a == 0 else 5, term] = edge_send[term, moved, :].astype(jnp.bfloat16)
                if g == 0:
                    halo_copy(a).start()
                    if a in (0, 3):
                        halo_copy(4 if a == 0 else 5).start()

        if c == 1:
            for slot in range(6):
                halo_copy(slot).wait()
                for term in range(2):
                    value = halo_in[slot, term]
                    if slot < 4:
                        spread(gathered, term * TERM, slot, GROUPS, slice(None), value)
                    else:
                        to, shift = (3, 2) if slot == 4 else (0, 0)
                        spot(gathered, term * TERM, to, GROUPS, slice(None), shift, value)

        tiles = slice(c * 4, c * 4 + 4)

        @pl.loop(0, CHUNKS)
        def _(step):
            turn_by = jnp.where(step == 0, 2, jnp.where(step == 1, 1, jnp.where(step == 2, 3, 0)))
            chunk = lax.rem(home + turn_by, CHUNKS)
            at = pl.ds(pl.multiple_of(chunk * CHUNK, CHUNK), CHUNK)
            cells = gathered[:, tiles, at, :].reshape(16 * CHUNK, 2 * TERM)
            low = None
            for pair in range(pairs):
                lanes = slice(pair * 2 * PHASE, (pair + 1) * 2 * PHASE)
                ratio = jnp.dot(cells, band[:, lanes], preferred_element_type=jnp.float32)
                ratio = ratio * inv[chunk, :, tiles, :, lanes].reshape(16 * CHUNK, 2 * PHASE)
                least = jnp.minimum(ratio[:, 0:PHASE], ratio[:, PHASE:])
                low = least if low is None else jnp.minimum(low, least)
            largest = jnp.maximum(jnp.max(low), 1e-30)
            low = low.reshape(4, 4, 2, CHUNK // 2, LANES)
            for a in range(4):
                turned = swap8([low[a, g % 4, g // 4] for g in range(GROUPS)])
                for r in range(8):
                    natural[pl.ds(8 * a + r, CHUNK // 2, stride=32), :] = turned[r]
            spread_by = jnp.full((8, LANES), largest, jnp.float32)
            factor[c, chunk] = jnp.sqrt(spread_by) * (1.0 / 65535.0)
            upward = (65535.0 * lax.rsqrt(spread_by))[0:1, :]
            for piece in range(4):
                code = jnp.sqrt(natural[piece * LANES : (piece + 1) * LANES, :]) * upward + 0.5
                code = (code.astype(jnp.int32) - 32768).T.astype(jnp.int16)
                for upper in range(2):
                    block = chunk * per_chunk + upper * 2 + piece // 2
                    staged[c, block, :, piece % 2 * LANES : (piece % 2 + 1) * LANES] = code[upper * 64 : upper * 64 + 64]

            @pl.loop(0, per_chunk)
            def _(i):
                block = chunk * per_chunk + i

                @pl.when(block != block_here)
                def _():
                    out_copy(c, block, mine).start()
                    scale_copy(c, block, mine).start()

        out_ref[mine, c] = staged[c, block_here]
        scale_ref[mine, c] = factor[c, home]

    @pl.loop(1, group)
    def _(turned):
        block = lax.rem(block_here + turned, group)
        source = lax.rem(mine + turned, group)
        for c in range(2):
            out_copy(c, block, mine).wait_send()
            scale_copy(c, block, mine).wait_send()
            out_copy(c, block, source).wait_recv()
            scale_copy(c, block, source).wait_recv()


def whole_safety(noise, choices, headings, extents, library, row_count, cols):
    length = noise.shape[2]
    outer = length // LANES
    group = 2 * cols
    devices = group * row_count
    turns, wide = tables(length)
    vmem = pl.BlockSpec(memory_space=pltpu.VMEM)
    smem = pl.BlockSpec(memory_space=pltpu.SMEM)
    dma = pltpu.SemaphoreType.DMA
    f32, bf16 = jnp.float32, jnp.bfloat16
    early, late = SPLIT * 16, LANES - SPLIT * 16
    return pl.pallas_call(
        functools.partial(whole_kernel, (row_count, cols)),
        out_shape=[
            jax.ShapeDtypeStruct((group, 2, LANES // 2, 2 * LANES), jnp.int16),
            jax.ShapeDtypeStruct((group, 2, 8, LANES), f32),
        ],
        in_specs=[pl.BlockSpec(memory_space=pl.ANY), vmem, smem, smem, vmem, vmem, vmem],
        out_specs=[vmem, vmem],
        scratch_shapes=[
            pltpu.VMEM((outer, LANES, 2 * LANES), f32),
            pltpu.VMEM((2, length, LANES), f32),
            pltpu.VMEM((devices, 2, early, LANES), bf16),
            pltpu.VMEM((devices, 2, late, LANES), bf16),
            pltpu.VMEM((devices, 2, early, LANES), bf16),
            pltpu.VMEM((devices, 2, late, LANES), bf16),
            pltpu.VMEM((4, GROUPS, LANES, LANES), f32),
            pltpu.VMEM((4, GROUPS, LANES, LANES), f32),
            pltpu.VMEM((4, GROUPS, LANES, 2 * TERM), bf16),
            pltpu.VMEM((CHUNKS, 4, GROUPS, CHUNK, 8 * PHASE), f32),
            pltpu.VMEM((2 * TERM, 8 * PHASE), bf16),
            pltpu.VMEM((2, GROUPS + 1, LANES + 16, LANES), f32),
            pltpu.VMEM((2, LANES + 16, LANES), f32),
            pltpu.VMEM((6, 2, LANES, LANES), bf16),
            pltpu.VMEM((6, 2, LANES, LANES), bf16),
            pltpu.VMEM((length // CHUNKS // 2, LANES), f32),
            pltpu.VMEM((2, group, LANES // 2, 2 * LANES), jnp.int16),
            pltpu.VMEM((2, CHUNKS, 8, LANES), f32),
            pltpu.VMEM((row_count * cols, 16, LANES), jnp.int32),
            pltpu.VMEM((2, 8, LANES), jnp.int32),
            pltpu.SMEM((row_count * cols, 16, LANES), jnp.int32),
            dma((CHUNKS, 8)), dma((2, devices)), dma((2, devices)),
            dma((row_count * cols,)), dma((row_count * cols,)), dma, dma, dma,
            dma((6,)), dma((6,)), dma((2, group)), dma((2, group)), dma((2, group)), dma((2, group)),
        ],
        compiler_params=pltpu.CompilerParams(
            vmem_limit_bytes=62 << 20, collective_id=0, has_side_effects=True
        ),
    )(noise, choices, headings, extents, library, turns, wide)


def strip_body(noise, elevation_library, tile_choice_index, family_heading_index, family_extent_index):
    row_count, cols = lax.axis_size("row"), lax.axis_size("col")
    library = jnp.roll(elevation_library.transpose(0, 2, 1), R, axis=2)
    code, scale = whole_safety(
        noise, tile_choice_index, family_heading_index, family_extent_index, library, row_count, cols
    )
    root = (code.astype(jnp.float32) + 32768.0) * scale[:, :, 0:1, 0:1]
    return (root * root).reshape(-1, code.shape[3])


def chosen_body(noise, elevation_library, tile_choice_index, family_heading_index, family_extent_index):
    shape = (lax.axis_size("row"), lax.axis_size("col"), lax.axis_size("orient"))
    side_cells = noise.shape[2]
    fits = (
        shape == (2, 8, 2)
        and side_cells == 32 * LANES
        and elevation_library.shape[1] == LANES
        and tile_choice_index.shape == (16, 4)
        and family_heading_index.shape[0] == 4
    )
    chosen = strip_body if fits else body
    return chosen(noise, elevation_library, tile_choice_index, family_heading_index, family_extent_index)


def solution(mesh):
    placed = (P(None, ("row", "col"), None), P(), P("row", "col"), P("orient"), P("orient"))
    return jax.shard_map(
        chosen_body, mesh=mesh, in_specs=placed, out_specs=P("row", ("col", "orient")), check_vma=False
    )
```

```python
import functools
import math

import jax
import jax.numpy as jnp
import numpy as np
from jax import lax
from jax.experimental import pallas as pl
from jax.experimental.pallas import tpu as pltpu
from jax.sharding import PartitionSpec as P

R = 8
N_AZ = 36
NSIZE = 4
LANES = 128
TILE_ROWS = 8
TILE_LANES = 16
GROUPS = LANES // TILE_LANES
PHASE = TILE_ROWS * TILE_LANES
STEP_TILES = 8

nugget_share = 0.3
peak_share = 1024.0 / (2.0 * math.pi)
cutoff_ratio = 32.0


def amplitude(u_index, v_index, side_cells):
    wrap_u = jnp.minimum(u_index, side_cells - u_index).astype(jnp.float32)
    wrap_v = jnp.minimum(v_index, side_cells - v_index).astype(jnp.float32)
    cutoff = side_cells / cutoff_ratio
    scaled_u = wrap_u / cutoff
    scaled_v = wrap_v / cutoff
    grown = 1.0 + scaled_u * scaled_u + scaled_v * scaled_v
    spectrum = nugget_share + peak_share / (grown * jnp.sqrt(grown))
    return jnp.sqrt(spectrum) / side_cells


def ellipsoid(offset_u, offset_v, azimuth, size_index):
    heading = azimuth.astype(jnp.float32) * (math.pi / N_AZ)
    semi_axis = R * (size_index.astype(jnp.float32) + (1 + NSIZE)) / (2 * NSIZE)
    across = 0.6 * semi_axis
    slip_depth = 0.3 * semi_axis
    along = offset_u * jnp.cos(heading) + offset_v * jnp.sin(heading)
    lateral = offset_v * jnp.cos(heading) - offset_u * jnp.sin(heading)
    along_part = along / semi_axis
    lateral_part = lateral / across
    inside = 1.0 - along_part * along_part - lateral_part * lateral_part
    height = slip_depth * jnp.sqrt(jnp.maximum(inside, 0.0))
    base_share = jnp.clip(4.0 * inside, 0.0, 1.0)
    return (height, base_share)


def small_dft(parts):
    count = len(parts)
    if count == 1:
        return parts
    even = small_dft(parts[0::2])
    odd = small_dft(parts[1::2])
    low, high = [], []
    for k in range(count // 2):
        (a, b), (c, d) = even[k], odd[k]
        if k == 0:
            e, f = c, d
        elif 4 * k == count:
            e, f = d, -c
        else:
            cos = math.cos(2 * math.pi * k / count)
            sin = math.sin(2 * math.pi * k / count)
            e, f = c * cos + d * sin, d * cos - c * sin
        low.append((a + e, b + f))
        high.append((a - e, b - f))
    return low + high


def transform_kernel(planes, blocks, span, step, pad, in_ref, cos_ref, sin_ref, big_ref, small_ref, out_ref, mid, full):
    outer = cos_ref.shape[0]
    rows = mid.shape[1]
    unit = 16 if planes else 8

    @pl.loop(0, rows // unit)
    def _(block):
        at = pl.ds(pl.multiple_of(block * unit, unit), unit)
        parts = []
        for p in range(outer):
            if planes:
                parts.append((in_ref[p, 0, at, :].astype(jnp.float32), in_ref[p, 1, at, :].astype(jnp.float32)))
            else:
                lanes = slice(p * LANES, (p + 1) * LANES)
                parts.append((in_ref[0, at, lanes], in_ref[1, at, lanes]))
        for k, (re, im) in enumerate(small_dft(parts)):
            cos = cos_ref[k : k + 1, :]
            sin = sin_ref[k : k + 1, :]
            mid[k, at, 0:LANES] = re * cos + im * sin
            mid[k, at, LANES : 2 * LANES] = im * cos - re * sin

    if pad:
        edge = jnp.zeros((pad, rows), jnp.float32)
        for part in range(2):
            full[part, 0:pad, :] = edge
            full[part, pad + outer * LANES : 2 * pad + outer * LANES, :] = edge

    turned = (((1,), (1,)), ((), ()))
    dot = functools.partial(lax.dot_general, dimension_numbers=turned, preferred_element_type=jnp.float32)
    for k in range(outer):
        value = mid[k]
        high = value.astype(jnp.bfloat16)
        rest = (value - high.astype(jnp.float32)).astype(jnp.bfloat16)
        got = dot(big_ref[...], high) + dot(big_ref[...], rest) + dot(small_ref[...], high)
        full[0, pl.ds(pad + k, LANES, stride=outer), :] = got[0:LANES]
        full[1, pl.ds(pad + k, LANES, stride=outer), :] = got[LANES : 2 * LANES]

    @pl.loop(0, blocks)
    def _(block):
        at = pl.ds(pl.multiple_of(block * step, 8), span)
        for part in range(2):
            out_ref[block, part] = full[part, at, :].astype(jnp.bfloat16)


def transform(cells, planes, rows, length, blocks, pad):
    outer = length // LANES
    step = length // blocks
    span = step + 2 * pad
    k = np.arange(outer)[:, None]
    q = np.arange(LANES)
    turn = 2 * np.pi * k * q / length
    cos, sin = np.cos(turn).astype(np.float32), np.sin(turn).astype(np.float32)
    angle = 2 * np.pi * (q[:, None] * q % LANES) / LANES
    table = np.block([[np.cos(angle), np.sin(angle)], [-np.sin(angle), np.cos(angle)]]).astype(np.float32)
    big = table.astype(jnp.bfloat16)
    small = (table - big.astype(np.float32)).astype(jnp.bfloat16)
    vmem = pl.BlockSpec(memory_space=pltpu.VMEM)
    return pl.pallas_call(
        functools.partial(transform_kernel, planes, blocks, span, step, pad),
        out_shape=jax.ShapeDtypeStruct((blocks, 2, span, rows), jnp.bfloat16),
        in_specs=[vmem] * 5,
        out_specs=vmem,
        scratch_shapes=[
            pltpu.VMEM((outer, rows, 2 * LANES), jnp.float32),
            pltpu.VMEM((2, length + 2 * pad, rows), jnp.float32),
        ],
        compiler_params=pltpu.CompilerParams(vmem_limit_bytes=40 << 20),
    )(cells, cos, sin, big, small)


def swap_groups(cells):
    row = lax.broadcasted_iota(jnp.int32, cells.shape, 1)
    group = lax.broadcasted_iota(jnp.int32, cells.shape, 2) // TILE_LANES
    skewed = pltpu.roll(cells, 0, 2, stride=TILE_LANES, stride_axis=1)
    picked = jnp.take_along_axis(skewed, (group + row - 7) & 7, axis=1)
    level = pltpu.roll(picked, TILE_LANES, 2, stride=TILE_LANES, stride_axis=1)
    return jnp.take_along_axis(level, 7 - row, axis=1)


def gather_tiles(term_ref, swapped, gathered):
    tiles, across = gathered.shape[1:3]
    chunks = across // GROUPS

    @pl.when(pl.program_id(0) == 0)
    def _():
        @pl.loop(0, tiles // 2)
        def _(pair):
            at = pl.ds(pl.multiple_of(pair * 16, 16), 16)
            both = pl.ds(pair * 2, 2)
            for term in range(gathered.shape[0]):
                for chunk in range(chunks + 1):
                    cells = term_ref[term, at, chunk * LANES : (chunk + 1) * LANES].astype(jnp.float32)
                    turned = swap_groups(cells.reshape(2, TILE_ROWS, LANES))
                    swapped[:, chunk * GROUPS : (chunk + 1) * GROUPS, :] = turned
                gathered[term, both, :, 0:PHASE] = swapped[:, 0:across, :].astype(jnp.bfloat16)
                gathered[term, both, :, PHASE:] = swapped[:, 1 : across + 1, :].astype(jnp.bfloat16)


def column_sum(gathered, band_ref, lanes):
    terms, _, across, depth = gathered.shape
    tile = pl.program_id(0) * STEP_TILES
    pieces = [(term, shift) for term in range(terms) for shift in range(3)]
    left = [gathered[term, pl.ds(tile + shift, STEP_TILES)] for term, shift in pieces]
    left = [piece.reshape(STEP_TILES * across, depth) for piece in left]
    right = [band_ref[term, shift, :, lanes] for term, shift in pieces]
    return jnp.dot(
        jnp.concatenate(left, axis=1),
        jnp.concatenate(right, axis=0),
        preferred_element_type=jnp.float32,
    )


def driving_kernel(families, term_ref, band_ref, out_ref, swapped, gathered):
    gather_tiles(term_ref, swapped, gathered)
    for pair in range(families // 2):
        lanes = slice(pair * 2 * PHASE, (pair + 1) * 2 * PHASE)
        out_ref[:, lanes] = column_sum(gathered, band_ref, lanes)


def stability_kernel(families, term_ref, band_ref, drive_ref, out_ref, swapped, gathered):
    chunks = gathered.shape[2] // GROUPS
    gather_tiles(term_ref, swapped, gathered)
    low = None
    for pair in range(families // 2):
        lanes = slice(pair * 2 * PHASE, (pair + 1) * 2 * PHASE)
        ratio = column_sum(gathered, band_ref, lanes) / drive_ref[:, lanes]
        least = jnp.minimum(ratio[:, 0:PHASE], ratio[:, PHASE:])
        low = least if low is None else jnp.minimum(low, least)
    turned = swap_groups(low.reshape(STEP_TILES * chunks, TILE_ROWS, LANES))
    for side in range(STEP_TILES):
        for chunk in range(chunks):
            out_ref[side * 8 : side * 8 + 8, chunk * LANES : (chunk + 1) * LANES] = turned[side * chunks + chunk]


def tile_call(kernel, terms, band, height, width, out_shape, out_block, more=()):
    families = band.shape[-1] // PHASE
    across = width // TILE_LANES
    tiles = height // TILE_ROWS + 2
    count = terms.shape[0]
    work = 2 * (height // TILE_ROWS) * across * band.size
    return pl.pallas_call(
        functools.partial(kernel, families),
        grid=(height // (TILE_ROWS * STEP_TILES),),
        out_shape=jax.ShapeDtypeStruct(out_shape, jnp.float32),
        in_specs=[
            pl.BlockSpec(terms.shape, lambda i: (0, 0, 0), pipeline_mode=pl.Buffered(1)),
            pl.BlockSpec(band.shape, lambda i: (0, 0, 0, 0), pipeline_mode=pl.Buffered(1)),
        ]
        + [pl.BlockSpec((STEP_TILES * across, cells.shape[1]), lambda i: (i, 0)) for cells in more],
        out_specs=pl.BlockSpec(out_block, lambda i: (i, 0)),
        scratch_shapes=[
            pltpu.VMEM((2, across + GROUPS, LANES), jnp.float32),
            pltpu.VMEM((count, tiles, across, 2 * PHASE), jnp.bfloat16),
        ],
        compiler_params=pltpu.CompilerParams(vmem_limit_bytes=56 << 20),
        cost_estimate=pl.CostEstimate(flops=work, bytes_accessed=16 << 20, transcendentals=0),
    )(terms, band, *more)


def extended(cells, sides, width):
    for axis, dim in sides:
        ends = lax.axis_size(axis) - 1
        head = lax.slice_in_dim(cells, 0, width, axis=dim)
        tail = lax.slice_in_dim(cells, cells.shape[dim] - width, cells.shape[dim], axis=dim)
        before = lax.ppermute(tail, axis, [(i, i + 1) for i in range(ends)])
        after = lax.ppermute(head, axis, [(i + 1, i) for i in range(ends)])
        cells = jnp.concatenate([before, cells, after], axis=dim)
    return cells


def band_weights(headings, extents):
    shape = (3, 2, TILE_ROWS, TILE_LANES, TILE_ROWS, TILE_LANES)
    index = [lax.broadcasted_iota(jnp.int32, shape, axis) for axis in range(6)]
    offset_v = TILE_ROWS * index[0] + index[2] - R - index[4]
    offset_u = TILE_LANES * index[1] + index[3] - R - index[5]
    keep = (jnp.abs(offset_v) <= R) & (jnp.abs(offset_u) <= R)
    rows = 3 * 2 * PHASE

    def flat(cells):
        return cells.reshape(rows, 1, PHASE)

    heights, shares = ellipsoid(
        flat(offset_u.astype(jnp.float32)),
        flat(offset_v.astype(jnp.float32)),
        headings[None, :, None],
        extents[None, :, None],
    )
    keep = flat(keep)
    count = headings.shape[0]

    def whole(cells):
        return jnp.where(keep, cells, 0.0).astype(jnp.bfloat16).reshape(3, 2 * PHASE, count * PHASE)

    heights = whole(heights)
    return jnp.stack([whole(shares), heights])


def pick_tiles(library, index):
    def copy_kernel(index_ref, in_ref, out_ref):
        out_ref[...] = in_ref[...]

    block = (1,) + library.shape[1:]
    flat = index.reshape(-1)
    picked = pl.pallas_call(
        copy_kernel,
        out_shape=jax.ShapeDtypeStruct(flat.shape + library.shape[1:], library.dtype),
        grid_spec=pltpu.PrefetchScalarGridSpec(
            num_scalar_prefetch=1,
            grid=flat.shape,
            in_specs=[pl.BlockSpec(block, lambda i, index_ref: (index_ref[i], 0, 0))],
            out_specs=pl.BlockSpec(block, lambda i, index_ref: (i, 0, 0)),
        ),
    )(flat, library)
    return picked.reshape(index.shape + library.shape[1:])


def body(noise, elevation_library, tile_choice_index, family_heading_index, family_extent_index):
    side_cells = noise.shape[2]
    row_count = lax.axis_size("row")
    col_count = lax.axis_size("col")
    split = lax.axis_size("orient")
    row, col, side = (lax.axis_index(axis) for axis in ("row", "col", "orient"))
    devices = row_count * col_count * split
    lines = noise.shape[1] // split
    window_rows = side_cells // row_count
    window_columns = side_cells // (col_count * split)

    families = jnp.stack([family_heading_index, family_extent_index])
    held_families = [families]
    for turn in range(1, split):
        pairs = [(i, (i + turn) % split) for i in range(split)]
        held_families.append(lax.ppermute(families, "orient", pairs))
    families = jnp.concatenate(held_families, axis=1)
    choices = extended(tile_choice_index, (("row", 0), ("col", 1)), 1)

    own = lax.dynamic_slice_in_dim(noise, side * lines, lines, 1)
    first_line = lax.axis_index(("row", "col", "orient")) * lines
    v_index = first_line + lax.broadcasted_iota(jnp.int32, (lines, side_cells), 0)
    u_index = lax.broadcasted_iota(jnp.int32, (lines, side_cells), 1)
    weights = own * amplitude(u_index, v_index, side_cells)[None]
    spectrum = transform(weights, False, lines, side_cells, devices, 0)
    spectrum, choices, families = lax.optimization_barrier((spectrum, choices, families))
    held = lax.all_to_all(spectrum, ("row", "col", "orient"), split_axis=0, concat_axis=0, tiled=True)
    tall = window_columns + 2 * R
    wide = (window_rows // LANES + 1) * LANES
    spare = wide - window_rows - 2 * R
    tile_side = elevation_library.shape[1]
    tiles_x = window_rows // tile_side
    tiles_y = window_columns // tile_side
    first_y = col * split + side
    local = lax.dynamic_slice_in_dim(choices, side * tiles_y, tiles_y + 2, 1)
    slope = pick_tiles(elevation_library.transpose(0, 2, 1), local.T)
    slope = slope.transpose(0, 2, 1, 3).reshape((tiles_y + 2) * tile_side, (tiles_x + 2) * tile_side)
    edge = tile_side - R
    slope = slope[edge : edge + tall, edge : edge + wide]
    y = first_y * window_columns - R + lax.broadcasted_iota(jnp.int32, (tall, wide), 0)
    x = row * window_rows - R + lax.broadcasted_iota(jnp.int32, (tall, wide), 1)
    inside = (y >= 0) & (y < side_cells) & (x >= 0) & (x < side_cells)
    secant = jnp.sqrt(1.0 + slope * slope)
    lift = jnp.where(inside, 0.5 * secant, 0.0)
    grip = jnp.where(inside, 0.6 / secant, 0.0)
    drive = jnp.where(inside, slope / secant, 0.0).astype(jnp.bfloat16)
    band = band_weights(families[0], families[1])
    held, lift, grip, drive = lax.optimization_barrier((held, lift, grip, drive))
    positions = side_cells // devices
    per_block = LANES // lines
    held = held.reshape(side_cells // LANES, per_block, 2, positions, lines)
    held = held.transpose(0, 2, 3, 1, 4).reshape(side_cells // LANES, 2, positions, LANES)
    fields = transform(held, True, positions, side_cells, col_count * split, R)
    fields = lax.all_to_all(fields, ("col", "orient"), split_axis=0, concat_axis=0, tiled=True)
    across = window_rows // TILE_LANES
    driving = tile_call(
        driving_kernel,
        drive[None],
        band[1:],
        window_columns,
        window_rows,
        (window_columns // TILE_ROWS * across, band.shape[-1]),
        (STEP_TILES * across, band.shape[-1]),
    )
    fields, driving, band = lax.optimization_barrier((fields, driving, band))
    fields = fields.transpose(1, 2, 0, 3).reshape(2, tall, window_rows)
    ends = row_count - 1
    before = lax.ppermute(fields[:, :, window_rows - R :], "row", [(i, i + 1) for i in range(ends)])
    after = lax.ppermute(fields[:, :, :R], "row", [(i + 1, i) for i in range(ends)])
    fields = jnp.concatenate(
        [before, fields, after, jnp.zeros((2, tall, spare), fields.dtype)], axis=2
    ).astype(jnp.float32)

    cohesion = (jnp.exp(0.4 * fields[0]) * lift).astype(jnp.bfloat16)
    friction = (jnp.exp(0.25 * fields[1]) * grip).astype(jnp.bfloat16)
    safety = tile_call(
        stability_kernel,
        jnp.stack([cohesion, friction]),
        band,
        window_columns,
        window_rows,
        (window_columns, window_rows),
        (TILE_ROWS * STEP_TILES, window_rows),
        (driving,),
    )
    return safety.T


TURNED = (((1,), (1,)), ((), ()))
DOT = functools.partial(lax.dot_general, dimension_numbers=TURNED, preferred_element_type=jnp.float32)
MESH = pl.DeviceIdType.MESH
CHUNK = 32
CHUNKS = LANES // CHUNK
SPLIT = 6
TERM = 6 * LANES


def strip_of(row, col, side, cols):
    return row * (2 * cols) + col + side * (2 * cols - 1 - 2 * col)


def place_of(strip, cols):
    row = strip // (2 * cols)
    at = strip % (2 * cols)
    side = at // cols
    return row, at + side * (2 * cols - 1 - 2 * at), side


def tables(length):
    outer = length // LANES
    q = np.arange(LANES)
    turns = []
    for shift in (R, 0):
        turn = 2 * np.pi * (np.arange(outer)[:, None] - shift) * q / length
        turns += [np.cos(turn), np.sin(turn)]
    angle = 2 * np.pi * (q[:, None] * q % LANES) / LANES
    table = np.block([[np.cos(angle), np.sin(angle)], [-np.sin(angle), np.cos(angle)]]).astype(np.float32)
    big = table.astype(jnp.bfloat16)
    small = (table - big.astype(np.float32)).astype(jnp.bfloat16)
    u = np.arange(length)
    wrapped = np.minimum(u, length - u) / (length / cutoff_ratio)
    turns.append((wrapped * wrapped).reshape(outer, LANES))
    return np.stack(turns).astype(np.float32), np.concatenate([big, big, small], axis=1)


def swap8(cells):
    cells = [pltpu.roll(c, TILE_LANES * i, 1) if i else c for i, c in enumerate(cells)]
    group = lax.broadcasted_iota(jnp.int32, cells[0].shape, 1) // TILE_LANES
    for bit in (1, 2, 4):
        pick = (group & bit) != 0
        cells = [jnp.where(pick, cells[(i + bit) % GROUPS], cells[i]) for i in range(GROUPS)]
    out = []
    for i in range(GROUPS):
        c = cells[-i % GROUPS]
        out.append(pltpu.roll(c, LANES - TILE_LANES * i, 1) if i else c)
    return out


def pair_dot(wide, first, second):
    value = jnp.concatenate([first, second], axis=0)
    high = value.astype(jnp.bfloat16)
    rest = (value - high.astype(jnp.float32)).astype(jnp.bfloat16)
    return DOT(wide, jnp.concatenate([high, rest, high], axis=1))


def spread(into, base, a, g, at, value):
    for shift in range(3):
        to = a + 1 - shift
        if 0 <= to < 4:
            spot(into, base, to, g, at, shift, value)


def spot(into, base, to, g, at, shift, value):
    first = base + shift * 2 * LANES
    if g < GROUPS:
        into[to, g, at, first : first + LANES] = value
    if g > 0:
        into[to, g - 1, at, first + LANES : first + 2 * LANES] = value


def band_rows(family_ref, band, side):
    params = []
    for owner in range(2):
        both = family_ref[owner].astype(jnp.float32)
        heading = both[0:4] * (math.pi / N_AZ)
        semi_axis = R * (both[4:8] + (1 + NSIZE)) / (2 * NSIZE)
        params.append((jnp.cos(heading), jnp.sin(heading), 1.0 / semi_axis, 1.0 / (0.6 * semi_axis), 0.3 * semi_axis))
    shape = (16, LANES)
    lane = lax.broadcasted_iota(jnp.int32, shape, 1)
    row = lax.broadcasted_iota(jnp.int32, shape, 0)

    @pl.loop(0, TERM // 16)
    def _(block):
        offset_v = TILE_ROWS * (block // 16) + block % 8 - R - lane // TILE_LANES
        offset_u = TILE_LANES * (block // 8 % 2) - R + row - lane % TILE_LANES
        keep = (jnp.abs(offset_v) <= R) & (jnp.abs(offset_u) <= R)
        v = offset_v.astype(jnp.float32)
        u = offset_u.astype(jnp.float32)
        at = pl.multiple_of(block * 16, 16)
        for family in range(8):
            cos, sin, per_semi, per_across, slip_depth = [p[family % 4 : family % 4 + 1] for p in params[family // 4]]
            along = (u * cos + v * sin) * per_semi
            lateral = (v * cos - u * sin) * per_across
            inside = 1.0 - along * along - lateral * lateral
            height = slip_depth * jnp.sqrt(jnp.maximum(inside, 0.0))
            share = jnp.clip(4.0 * inside, 0.0, 1.0)
            lanes = slice(family * LANES, (family + 1) * LANES)
            band[pl.ds(at, 16), lanes] = jnp.where(keep, share, 0.0).astype(jnp.bfloat16)
            band[pl.ds(at + TERM, 16), lanes] = jnp.where(keep, height, 0.0).astype(jnp.bfloat16)


def whole_kernel(
    sizes, noise_any, choice_ref, heading_ref, extent_ref, lib_any, turn_ref, wide_ref,
    out_any,
    mid, full, send_a, send_b, held_a, held_b, lift, grip, gathered, inv, band, edge, edge_send, halo_out, halo_in,
    natural, staged, factor, code_in, scale_in, done, library, choice_in, family_in, choice_smem,
    noise_sem, first_send, first_recv, choice_send, choice_recv, family_send, family_recv, smem_sem,
    halo_send, halo_recv, out_send, out_recv, scale_send, scale_recv, library_sem, done_sem,
):
    row_count, cols = sizes
    row, col, side = (lax.axis_index(axis) for axis in ("row", "col", "orient"))
    devices = row_count * cols * 2
    group = cols * 2
    me = (row * cols + col) * 2 + side
    strip = strip_of(row, col, side, cols)
    mine = strip % group
    block_here = col * 2 + side
    plane = row * cols + col
    left = place_of(lax.rem(strip + devices - 1, devices), cols)
    outer = turn_ref.shape[1]

    def device(index):
        return index // group, index % group // 2, index % 2

    def owner(block):
        return row, block // 2, block % 2

    barrier = pltpu.get_barrier_semaphore()

    @pl.loop(1, devices)
    def _(k):
        pl.semaphore_signal(barrier, inc=1, device_id=device(lax.rem(me + k, devices)), device_id_type=MESH)

    def noise_copy(chunk, part, piece):
        lines = pl.ds(pl.multiple_of(side * LANES + chunk * CHUNK, CHUNK), CHUNK)
        return pltpu.make_async_copy(
            noise_any.at[part, lines, piece * 1024 : (piece + 1) * 1024],
            inv.at[0, part * 2 + piece // 2, piece % 2 * 4 + chunk],
            noise_sem.at[chunk, part * 4 + piece],
        )

    for chunk in range(CHUNKS):
        for part in range(2):
            for piece in range(4):
                noise_copy(chunk, part, piece).start()

    library_copy = pltpu.make_async_copy(lib_any, library, library_sem)
    library_copy.start()
    choice_in[plane] = jnp.zeros((8, LANES), jnp.int32)
    choice_in[plane, 0:4, 0:16] = choice_ref[...]
    which = lax.broadcasted_iota(jnp.int32, (8, LANES), 0)
    mixed = jnp.zeros((8, LANES), jnp.int32)
    for f in range(4):
        mixed = jnp.where(which == f, heading_ref[f], mixed)
        mixed = jnp.where(which == f + 4, extent_ref[f], mixed)
    family_in[side] = mixed

    for chunk in range(CHUNKS):
        for part in range(2):
            for piece in range(4):
                noise_copy(chunk, part, piece).wait()

        @pl.loop(0, CHUNK // 8)
        def _(block):
            at = pl.ds(pl.multiple_of(block * 8, 8), 8)
            line = me * LANES + chunk * CHUNK + block * 8 + lax.broadcasted_iota(jnp.int32, (8, LANES), 0)
            wrap_v = jnp.minimum(line, outer * LANES - line).astype(jnp.float32) * (cutoff_ratio / (outer * LANES))
            base = 1.0 + wrap_v * wrap_v
            parts = []
            for p in range(outer):
                root = lax.rsqrt(base + turn_ref[4, p : p + 1, :])
                spectrum = nugget_share + peak_share * (root * root * root)
                level = spectrum * lax.rsqrt(spectrum) * (1.0 / (outer * LANES))
                spot_at = (p // 16, p // 8 % 2 * 4 + chunk, at, slice(p % 8 * LANES, (p % 8 + 1) * LANES))
                parts.append((inv[(0,) + spot_at] * level, inv[(0, 2 + spot_at[0]) + spot_at[1:]] * level))
            turned = small_dft(parts)
            rows = pl.ds(pl.multiple_of(chunk * CHUNK + block * 8, 8), 8)
            for k in range(outer):
                re, im = turned[(k - R) % outer]
                cos = turn_ref[0, k : k + 1, :]
                sin = turn_ref[1, k : k + 1, :]
                mid[k, rows, 0:LANES] = re * cos + im * sin
                mid[k, rows, LANES : 2 * LANES] = im * cos - re * sin

    pl.semaphore_wait(barrier, devices - 1)

    def choice_copy(k):
        to = lax.rem(plane + k, row_count * cols)
        return pltpu.make_async_remote_copy(
            src_ref=choice_in.at[plane], dst_ref=choice_in.at[plane],
            send_sem=choice_send.at[k], recv_sem=choice_recv.at[k],
            device_id=(to // cols, to % cols, side), device_id_type=MESH,
        )

    def family_copy():
        return pltpu.make_async_remote_copy(
            src_ref=family_in.at[side], dst_ref=family_in.at[side], send_sem=family_send, recv_sem=family_recv,
            device_id=(row, col, 1 - side), device_id_type=MESH,
        )

    @pl.loop(1, row_count * cols)
    def _(k):
        choice_copy(k).start()

    family_copy().start()

    for k in range(0, outer, 2):
        got = pair_dot(wide_ref[...], mid[k], mid[k + 1])
        for part in range(2):
            for one in range(2):
                piece = got[part * LANES : (part + 1) * LANES, one * LANES : (one + 1) * LANES]
                full[part, pl.ds(k + one, LANES, stride=outer), :] = piece

    parts_of = ((0, SPLIT, send_a, held_a), (SPLIT, GROUPS, send_b, held_b))

    def partner(k):
        return me ^ (k % 2 * 8 + k // 2 % 8 + k // 16 * 16)

    def first_copy(c, k):
        to = partner(k)
        return pltpu.make_async_remote_copy(
            src_ref=parts_of[c][2].at[to], dst_ref=parts_of[c][3].at[me],
            send_sem=first_send.at[c, k], recv_sem=first_recv.at[c, k],
            device_id=device(to), device_id_type=MESH,
        )

    for c, (low_g, high_g, send, held) in enumerate(parts_of):
        count = (high_g - low_g) * 16

        def packed(to, into):
            to_strip = strip_of(*device(to), cols)
            at = pl.ds(pl.multiple_of(to_strip * LANES + low_g * 16, 16), count)
            for part in range(2):
                into[to, part] = full[part, at, :].astype(jnp.bfloat16)

        @pl.loop(1, devices)
        def _(k):
            packed(partner(k), send)
            first_copy(c, k).start()

        packed(me, held)

    family_copy().wait()
    band_rows(family_in, band, side)

    @pl.loop(1, row_count * cols)
    def _(k):
        choice_copy(k).wait()

    to_smem = pltpu.make_async_copy(choice_in, choice_smem, smem_sem)
    to_smem.start()
    to_smem.wait()
    library_copy.wait()

    @pl.loop(0, library.shape[0])
    def _(t):
        library[t] = pltpu.roll(library[t].T, R, 1)

    left_lanes = lax.broadcasted_iota(jnp.int32, (LANES, LANES), 1) < R

    def tile(shift, t):
        x = lax.rem(strip + devices + shift, devices)
        return library[choice_smem[x // 16 * cols + t // 4, t % 4, x % 16]]

    @pl.loop(0, outer)
    def _(t):
        at = pl.ds(pl.multiple_of(t * LANES, LANES), LANES)
        here = tile(0, t)
        full[0, at, :] = jnp.where(left_lanes, tile(-1, t), here)
        full[1, at, :] = jnp.where(left_lanes, here, tile(1, t))

    half = lax.broadcasted_iota(jnp.int32, (16, LANES), 1) % TILE_LANES < R
    first = strip == 0
    last = strip == devices - 1
    for side_rows in (slice(0, 8), slice(8 + LANES, 16 + LANES)):
        edge[:, :, side_rows, :] = jnp.zeros((2, GROUPS + 1, 8, LANES), jnp.float32)
        edge_send[:, side_rows, :] = jnp.zeros((2, 8, LANES), jnp.float32)

    for a in range(4):
        @pl.loop(0, 8)
        def _(c):
            at = pl.ds(pl.multiple_of(c * 16, 16), 16)
            for source in range(2):
                turned = swap8([full[source, pl.ds(c * 512 + 8 * a + r, 16, stride=32), :] for r in range(8)])
                for g in range(GROUPS) if source == 0 else (0,):
                    slope = turned[g]
                    square = 1.0 + slope * slope
                    inverse = lax.rsqrt(square)
                    drive = slope * inverse
                    tile_at = g
                    if source == 0:
                        lift[a, g, at, :] = 0.5 * square * inverse
                        grip[a, g, at, :] = 0.6 * inverse
                        if g == 0:
                            drive = jnp.where(half & first, 0.0, drive)
                    else:
                        tile_at = GROUPS
                        drive = jnp.where(last & ~half, 0.0, drive)
                    spread(gathered, TERM, a, tile_at, at, drive.astype(jnp.bfloat16))
                    if a in (0, 3):
                        edge[0, tile_at, pl.ds(pl.multiple_of(c * 16 + 8, 8), 16), :] = drive

        if a in (0, 3):
            @pl.loop(0, 8)
            def _(c):
                at = pl.ds(pl.multiple_of(c * 16, 16), 16)
                for g in range(GROUPS + 1):
                    value = edge[0, g, pl.ds(c * 16 + (9 if a == 0 else 7), 16), :].astype(jnp.bfloat16)
                    spot(gathered, TERM, 3 - a, g, at, 2 if a == 0 else 0, value)

    pairs = band.shape[1] // (2 * PHASE)

    @pl.loop(0, CHUNKS)
    def _(chunk):
        at = pl.ds(pl.multiple_of(chunk * CHUNK, CHUNK), CHUNK)
        cells = gathered[:, :, at, TERM:].reshape(4 * GROUPS * CHUNK, TERM)
        for pair in range(pairs):
            lanes = slice(pair * 2 * PHASE, (pair + 1) * 2 * PHASE)
            sums = jnp.dot(cells, band[TERM:, lanes], preferred_element_type=jnp.float32)
            inv[chunk, :, :, :, lanes] = (1.0 / sums).reshape(4, GROUPS, CHUNK, 2 * PHASE)

    def halo_copy(slot):
        return pltpu.make_async_remote_copy(
            src_ref=halo_out.at[slot], dst_ref=halo_in.at[slot],
            send_sem=halo_send.at[slot], recv_sem=halo_recv.at[slot],
            device_id=left, device_id_type=MESH,
        )

    per_chunk = CHUNK * outer // (2 * LANES)
    home = block_here // per_chunk

    def out_copy(c, block, source):
        return pltpu.make_async_remote_copy(
            src_ref=staged.at[c, block], dst_ref=code_in.at[source, c],
            send_sem=out_send.at[c, block], recv_sem=out_recv.at[c, source],
            device_id=owner(block), device_id_type=MESH,
        )

    def scale_copy(c, block, source):
        return pltpu.make_async_remote_copy(
            src_ref=factor.at[c, block // per_chunk], dst_ref=scale_in.at[source, c],
            send_sem=scale_send.at[c, block], recv_sem=scale_recv.at[c, source],
            device_id=owner(block), device_id_type=MESH,
        )

    for c, (low_g, high_g, send, held) in enumerate(parts_of):
        @pl.loop(1, devices)
        def _(k):
            first_copy(c, k).wait()

        @pl.loop(low_g, high_g)
        def _(g):
            at = pl.ds(pl.multiple_of((g - low_g) * 16, 16), 16)
            parts = [(held[p, 0, at, :].astype(jnp.float32), held[p, 1, at, :].astype(jnp.float32)) for p in range(outer)]
            for k, (re, im) in enumerate(small_dft(parts)):
                to = slice(k % 8 * 16, (k % 8 + 1) * 16)
                cos = turn_ref[2, k : k + 1, :]
                sin = turn_ref[3, k : k + 1, :]
                mid[k // 8 * 8 + g, to, 0:LANES] = re * cos + im * sin
                mid[k // 8 * 8 + g, to, LANES : 2 * LANES] = im * cos - re * sin

        items = [(a, g) for g in range(low_g, high_g) for a in range(4)]
        for at_item in range(0, len(items), 2):
            two = items[at_item : at_item + 2]
            got = pair_dot(wide_ref[...], *[mid[a * 8 + g] for a, g in two])
            for one, (a, g) in enumerate(two):
                for term in range(2):
                    field = got[term * LANES : (term + 1) * LANES, one * LANES : (one + 1) * LANES]
                    value = jnp.exp((0.4 if term == 0 else 0.25) * field) * (lift if term == 0 else grip)[a, g]
                    if g == 0:
                        mask = lax.broadcasted_iota(jnp.int32, (LANES, LANES), 1) % TILE_LANES < R
                        sent = jnp.where(first & ~mask, 0.0, value)
                        value = jnp.where(first & mask, 0.0, value)
                        halo_out[a, term] = sent.astype(jnp.bfloat16)
                    spread(gathered, term * TERM, a, g, slice(None), value.astype(jnp.bfloat16))
                    if a in (0, 3):
                        moved = slice(9, 9 + LANES) if a == 0 else slice(7, 7 + LANES)
                        edge[term, g, 8 : 8 + LANES, :] = value
                        near = edge[term, g, moved, :].astype(jnp.bfloat16)
                        spot(gathered, term * TERM, 3 - a, g, slice(None), 2 if a == 0 else 0, near)
                        if g == 0:
                            edge_send[term, 8 : 8 + LANES, :] = sent
                            halo_out[4 if a == 0 else 5, term] = edge_send[term, moved, :].astype(jnp.bfloat16)
                if g == 0:
                    halo_copy(a).start()
                    if a in (0, 3):
                        halo_copy(4 if a == 0 else 5).start()

        if c == 1:
            for slot in range(6):
                halo_copy(slot).wait()
                for term in range(2):
                    value = halo_in[slot, term]
                    if slot < 4:
                        spread(gathered, term * TERM, slot, GROUPS, slice(None), value)
                    else:
                        to, shift = (3, 2) if slot == 4 else (0, 0)
                        spot(gathered, term * TERM, to, GROUPS, slice(None), shift, value)

        tiles = slice(c * 4, c * 4 + 4)

        @pl.loop(0, CHUNKS)
        def _(step):
            chunk = home ^ jnp.where(step < 2, step + 2, 3 - step)
            at = pl.ds(pl.multiple_of(chunk * CHUNK, CHUNK), CHUNK)
            cells = gathered[:, tiles, at, :].reshape(16 * CHUNK, 2 * TERM)
            low = None
            for pair in range(pairs):
                lanes = slice(pair * 2 * PHASE, (pair + 1) * 2 * PHASE)
                ratio = jnp.dot(cells, band[:, lanes], preferred_element_type=jnp.float32)
                ratio = ratio * inv[chunk, :, tiles, :, lanes].reshape(16 * CHUNK, 2 * PHASE)
                least = jnp.minimum(ratio[:, 0:PHASE], ratio[:, PHASE:])
                low = least if low is None else jnp.minimum(low, least)
            largest = jnp.maximum(jnp.max(low), 1e-30)
            low = low.reshape(4, 4, 2, CHUNK // 2, LANES)
            for a in range(4):
                turned = swap8([low[a, g % 4, g // 4] for g in range(GROUPS)])
                for r in range(8):
                    natural[pl.ds(8 * a + r, CHUNK // 2, stride=32), :] = turned[r]
            spread_by = jnp.full((8, LANES), largest, jnp.float32)
            factor[c, chunk] = jnp.sqrt(spread_by) * (1.0 / 65535.0)
            upward = (65535.0 * lax.rsqrt(spread_by))[0:1, :]
            for piece in range(4):
                code = jnp.sqrt(natural[piece * LANES : (piece + 1) * LANES, :]) * upward + 0.5
                code = (code.astype(jnp.int32) - 32768).T.astype(jnp.int16)
                for upper in range(2):
                    block = chunk * per_chunk + upper * 2 + piece // 2
                    staged[c, block, :, piece % 2 * LANES : (piece % 2 + 1) * LANES] = code[upper * 64 : upper * 64 + 64]

            @pl.loop(0, per_chunk)
            def _(i):
                block = chunk * per_chunk + i

                @pl.when(block != block_here)
                def _():
                    out_copy(c, block, mine).start()
                    scale_copy(c, block, mine).start()

    def done_copy(c, source):
        rows = pl.ds(pl.multiple_of(source * LANES + c * 64, 64), 64)
        return pltpu.make_async_copy(done.at[source, c], out_any.at[rows], done_sem.at[c, source])

    def finish(c, source, code, scale):
        root = (code.astype(jnp.float32) + 32768.0) * scale[0:1, 0:1]
        done[source, c] = root * root
        done_copy(c, source).start()

    for c in range(2):
        finish(c, mine, staged[c, block_here], factor[c, home])

        @pl.loop(0, group)
        def _(at):
            away = at // 4
            block = (home ^ jnp.where(away < 2, away + 2, 3 - away)) * 4 + at % 4
            source = strip_of(0, block // 2, block % 2, cols)

            @pl.when(block != block_here)
            def _():
                out_copy(c, block, source).wait_recv()
                scale_copy(c, block, source).wait_recv()
                finish(c, source, code_in[source, c], scale_in[source, c])

    @pl.loop(1, group)
    def _(turned):
        block = lax.rem(block_here + turned, group)
        for c in range(2):
            out_copy(c, block, mine).wait_send()
            scale_copy(c, block, mine).wait_send()

    @pl.loop(0, group)
    def _(source):
        for c in range(2):
            done_copy(c, source).wait()


def whole_safety(noise, choices, headings, extents, library, row_count, cols):
    length = noise.shape[2]
    outer = length // LANES
    group = 2 * cols
    devices = group * row_count
    turns, wide = tables(length)
    vmem = pl.BlockSpec(memory_space=pltpu.VMEM)
    smem = pl.BlockSpec(memory_space=pltpu.SMEM)
    dma = pltpu.SemaphoreType.DMA
    f32, bf16 = jnp.float32, jnp.bfloat16
    early, late = SPLIT * 16, LANES - SPLIT * 16
    return pl.pallas_call(
        functools.partial(whole_kernel, (row_count, cols)),
        out_shape=jax.ShapeDtypeStruct((group * LANES, 2 * LANES), f32),
        in_specs=[pl.BlockSpec(memory_space=pl.ANY), vmem, smem, smem, pl.BlockSpec(memory_space=pl.ANY), vmem, vmem],
        out_specs=pl.BlockSpec(memory_space=pl.ANY),
        scratch_shapes=[
            pltpu.VMEM((outer, LANES, 2 * LANES), f32),
            pltpu.VMEM((2, length, LANES), f32),
            pltpu.VMEM((devices, 2, early, LANES), bf16),
            pltpu.VMEM((devices, 2, late, LANES), bf16),
            pltpu.VMEM((devices, 2, early, LANES), bf16),
            pltpu.VMEM((devices, 2, late, LANES), bf16),
            pltpu.VMEM((4, GROUPS, LANES, LANES), f32),
            pltpu.VMEM((4, GROUPS, LANES, LANES), f32),
            pltpu.VMEM((4, GROUPS, LANES, 2 * TERM), bf16),
            pltpu.VMEM((CHUNKS, 4, GROUPS, CHUNK, 8 * PHASE), f32),
            pltpu.VMEM((2 * TERM, 8 * PHASE), bf16),
            pltpu.VMEM((2, GROUPS + 1, LANES + 16, LANES), f32),
            pltpu.VMEM((2, LANES + 16, LANES), f32),
            pltpu.VMEM((6, 2, LANES, LANES), bf16),
            pltpu.VMEM((6, 2, LANES, LANES), bf16),
            pltpu.VMEM((length // CHUNKS // 2, LANES), f32),
            pltpu.VMEM((2, group, LANES // 2, 2 * LANES), jnp.int16),
            pltpu.VMEM((2, CHUNKS, 8, LANES), f32),
            pltpu.VMEM((group, 2, LANES // 2, 2 * LANES), jnp.int16),
            pltpu.VMEM((group, 2, 8, LANES), f32),
            pltpu.VMEM((group, 2, LANES // 2, 2 * LANES), f32),
            pltpu.VMEM(library.shape, f32),
            pltpu.VMEM((row_count * cols, 8, LANES), jnp.int32),
            pltpu.VMEM((2, 8, LANES), jnp.int32),
            pltpu.SMEM((row_count * cols, 8, LANES), jnp.int32),
            dma((CHUNKS, 8)), dma((2, devices)), dma((2, devices)),
            dma((row_count * cols,)), dma((row_count * cols,)), dma, dma, dma,
            dma((6,)), dma((6,)), dma((2, group)), dma((2, group)), dma((2, group)), dma((2, group)), dma, dma((2, group)),
        ],
        compiler_params=pltpu.CompilerParams(
            vmem_limit_bytes=62 << 20, collective_id=0, has_side_effects=True
        ),
    )(noise, choices, headings, extents, library, turns, wide)


def strip_body(noise, elevation_library, tile_choice_index, family_heading_index, family_extent_index):
    row_count, cols = lax.axis_size("row"), lax.axis_size("col")
    return whole_safety(
        noise, tile_choice_index.T, family_heading_index, family_extent_index, elevation_library, row_count, cols
    )


def chosen_body(noise, elevation_library, tile_choice_index, family_heading_index, family_extent_index):
    shape = (lax.axis_size("row"), lax.axis_size("col"), lax.axis_size("orient"))
    side_cells = noise.shape[2]
    fits = (
        shape == (2, 8, 2)
        and side_cells == 32 * LANES
        and elevation_library.shape[1] == LANES
        and tile_choice_index.shape == (16, 4)
        and family_heading_index.shape[0] == 4
    )
    chosen = strip_body if fits else body
    return chosen(noise, elevation_library, tile_choice_index, family_heading_index, family_extent_index)


def solution(mesh):
    placed = (P(None, ("row", "col"), None), P(), P("row", "col"), P("orient"), P("orient"))
    return jax.shard_map(
        chosen_body, mesh=mesh, in_specs=placed, out_specs=P("row", ("col", "orient")), check_vma=False
    )
```

```python
import functools
import math

import jax
import jax.numpy as jnp
import numpy as np
from jax import lax
from jax.experimental import pallas as pl
from jax.experimental.pallas import tpu as pltpu
from jax.sharding import PartitionSpec as P

R = 8
N_AZ = 36
NSIZE = 4
LANES = 128
TILE_ROWS = 8
TILE_LANES = 16
GROUPS = LANES // TILE_LANES
PHASE = TILE_ROWS * TILE_LANES
STEP_TILES = 8

nugget_share = 0.3
peak_share = 1024.0 / (2.0 * math.pi)
cutoff_ratio = 32.0


def amplitude(u_index, v_index, side_cells):
    wrap_u = jnp.minimum(u_index, side_cells - u_index).astype(jnp.float32)
    wrap_v = jnp.minimum(v_index, side_cells - v_index).astype(jnp.float32)
    cutoff = side_cells / cutoff_ratio
    scaled_u = wrap_u / cutoff
    scaled_v = wrap_v / cutoff
    grown = 1.0 + scaled_u * scaled_u + scaled_v * scaled_v
    spectrum = nugget_share + peak_share / (grown * jnp.sqrt(grown))
    return jnp.sqrt(spectrum) / side_cells


def ellipsoid(offset_u, offset_v, azimuth, size_index):
    heading = azimuth.astype(jnp.float32) * (math.pi / N_AZ)
    semi_axis = R * (size_index.astype(jnp.float32) + (1 + NSIZE)) / (2 * NSIZE)
    across = 0.6 * semi_axis
    slip_depth = 0.3 * semi_axis
    along = offset_u * jnp.cos(heading) + offset_v * jnp.sin(heading)
    lateral = offset_v * jnp.cos(heading) - offset_u * jnp.sin(heading)
    along_part = along / semi_axis
    lateral_part = lateral / across
    inside = 1.0 - along_part * along_part - lateral_part * lateral_part
    height = slip_depth * jnp.sqrt(jnp.maximum(inside, 0.0))
    base_share = jnp.clip(4.0 * inside, 0.0, 1.0)
    return (height, base_share)


def small_dft(parts):
    count = len(parts)
    if count == 1:
        return parts
    even = small_dft(parts[0::2])
    odd = small_dft(parts[1::2])
    low, high = [], []
    for k in range(count // 2):
        (a, b), (c, d) = even[k], odd[k]
        if k == 0:
            e, f = c, d
        elif 4 * k == count:
            e, f = d, -c
        else:
            cos = math.cos(2 * math.pi * k / count)
            sin = math.sin(2 * math.pi * k / count)
            e, f = c * cos + d * sin, d * cos - c * sin
        low.append((a + e, b + f))
        high.append((a - e, b - f))
    return low + high


def transform_kernel(planes, blocks, span, step, pad, in_ref, cos_ref, sin_ref, big_ref, small_ref, out_ref, mid, full):
    outer = cos_ref.shape[0]
    rows = mid.shape[1]
    unit = 16 if planes else 8

    @pl.loop(0, rows // unit)
    def _(block):
        at = pl.ds(pl.multiple_of(block * unit, unit), unit)
        parts = []
        for p in range(outer):
            if planes:
                parts.append((in_ref[p, 0, at, :].astype(jnp.float32), in_ref[p, 1, at, :].astype(jnp.float32)))
            else:
                lanes = slice(p * LANES, (p + 1) * LANES)
                parts.append((in_ref[0, at, lanes], in_ref[1, at, lanes]))
        for k, (re, im) in enumerate(small_dft(parts)):
            cos = cos_ref[k : k + 1, :]
            sin = sin_ref[k : k + 1, :]
            mid[k, at, 0:LANES] = re * cos + im * sin
            mid[k, at, LANES : 2 * LANES] = im * cos - re * sin

    if pad:
        edge = jnp.zeros((pad, rows), jnp.float32)
        for part in range(2):
            full[part, 0:pad, :] = edge
            full[part, pad + outer * LANES : 2 * pad + outer * LANES, :] = edge

    turned = (((1,), (1,)), ((), ()))
    dot = functools.partial(lax.dot_general, dimension_numbers=turned, preferred_element_type=jnp.float32)
    for k in range(outer):
        value = mid[k]
        high = value.astype(jnp.bfloat16)
        rest = (value - high.astype(jnp.float32)).astype(jnp.bfloat16)
        got = dot(big_ref[...], high) + dot(big_ref[...], rest) + dot(small_ref[...], high)
        full[0, pl.ds(pad + k, LANES, stride=outer), :] = got[0:LANES]
        full[1, pl.ds(pad + k, LANES, stride=outer), :] = got[LANES : 2 * LANES]

    @pl.loop(0, blocks)
    def _(block):
        at = pl.ds(pl.multiple_of(block * step, 8), span)
        for part in range(2):
            out_ref[block, part] = full[part, at, :].astype(jnp.bfloat16)


def transform(cells, planes, rows, length, blocks, pad):
    outer = length // LANES
    step = length // blocks
    span = step + 2 * pad
    k = np.arange(outer)[:, None]
    q = np.arange(LANES)
    turn = 2 * np.pi * k * q / length
    cos, sin = np.cos(turn).astype(np.float32), np.sin(turn).astype(np.float32)
    angle = 2 * np.pi * (q[:, None] * q % LANES) / LANES
    table = np.block([[np.cos(angle), np.sin(angle)], [-np.sin(angle), np.cos(angle)]]).astype(np.float32)
    big = table.astype(jnp.bfloat16)
    small = (table - big.astype(np.float32)).astype(jnp.bfloat16)
    vmem = pl.BlockSpec(memory_space=pltpu.VMEM)
    return pl.pallas_call(
        functools.partial(transform_kernel, planes, blocks, span, step, pad),
        out_shape=jax.ShapeDtypeStruct((blocks, 2, span, rows), jnp.bfloat16),
        in_specs=[vmem] * 5,
        out_specs=vmem,
        scratch_shapes=[
            pltpu.VMEM((outer, rows, 2 * LANES), jnp.float32),
            pltpu.VMEM((2, length + 2 * pad, rows), jnp.float32),
        ],
        compiler_params=pltpu.CompilerParams(vmem_limit_bytes=40 << 20),
    )(cells, cos, sin, big, small)


def swap_groups(cells):
    row = lax.broadcasted_iota(jnp.int32, cells.shape, 1)
    group = lax.broadcasted_iota(jnp.int32, cells.shape, 2) // TILE_LANES
    skewed = pltpu.roll(cells, 0, 2, stride=TILE_LANES, stride_axis=1)
    picked = jnp.take_along_axis(skewed, (group + row - 7) & 7, axis=1)
    level = pltpu.roll(picked, TILE_LANES, 2, stride=TILE_LANES, stride_axis=1)
    return jnp.take_along_axis(level, 7 - row, axis=1)


def gather_tiles(term_ref, swapped, gathered):
    tiles, across = gathered.shape[1:3]
    chunks = across // GROUPS

    @pl.when(pl.program_id(0) == 0)
    def _():
        @pl.loop(0, tiles // 2)
        def _(pair):
            at = pl.ds(pl.multiple_of(pair * 16, 16), 16)
            both = pl.ds(pair * 2, 2)
            for term in range(gathered.shape[0]):
                for chunk in range(chunks + 1):
                    cells = term_ref[term, at, chunk * LANES : (chunk + 1) * LANES].astype(jnp.float32)
                    turned = swap_groups(cells.reshape(2, TILE_ROWS, LANES))
                    swapped[:, chunk * GROUPS : (chunk + 1) * GROUPS, :] = turned
                gathered[term, both, :, 0:PHASE] = swapped[:, 0:across, :].astype(jnp.bfloat16)
                gathered[term, both, :, PHASE:] = swapped[:, 1 : across + 1, :].astype(jnp.bfloat16)


def column_sum(gathered, band_ref, lanes):
    terms, _, across, depth = gathered.shape
    tile = pl.program_id(0) * STEP_TILES
    pieces = [(term, shift) for term in range(terms) for shift in range(3)]
    left = [gathered[term, pl.ds(tile + shift, STEP_TILES)] for term, shift in pieces]
    left = [piece.reshape(STEP_TILES * across, depth) for piece in left]
    right = [band_ref[term, shift, :, lanes] for term, shift in pieces]
    return jnp.dot(
        jnp.concatenate(left, axis=1),
        jnp.concatenate(right, axis=0),
        preferred_element_type=jnp.float32,
    )


def driving_kernel(families, term_ref, band_ref, out_ref, swapped, gathered):
    gather_tiles(term_ref, swapped, gathered)
    for pair in range(families // 2):
        lanes = slice(pair * 2 * PHASE, (pair + 1) * 2 * PHASE)
        out_ref[:, lanes] = column_sum(gathered, band_ref, lanes)


def stability_kernel(families, term_ref, band_ref, drive_ref, out_ref, swapped, gathered):
    chunks = gathered.shape[2] // GROUPS
    gather_tiles(term_ref, swapped, gathered)
    low = None
    for pair in range(families // 2):
        lanes = slice(pair * 2 * PHASE, (pair + 1) * 2 * PHASE)
        ratio = column_sum(gathered, band_ref, lanes) / drive_ref[:, lanes]
        least = jnp.minimum(ratio[:, 0:PHASE], ratio[:, PHASE:])
        low = least if low is None else jnp.minimum(low, least)
    turned = swap_groups(low.reshape(STEP_TILES * chunks, TILE_ROWS, LANES))
    for side in range(STEP_TILES):
        for chunk in range(chunks):
            out_ref[side * 8 : side * 8 + 8, chunk * LANES : (chunk + 1) * LANES] = turned[side * chunks + chunk]


def tile_call(kernel, terms, band, height, width, out_shape, out_block, more=()):
    families = band.shape[-1] // PHASE
    across = width // TILE_LANES
    tiles = height // TILE_ROWS + 2
    count = terms.shape[0]
    work = 2 * (height // TILE_ROWS) * across * band.size
    return pl.pallas_call(
        functools.partial(kernel, families),
        grid=(height // (TILE_ROWS * STEP_TILES),),
        out_shape=jax.ShapeDtypeStruct(out_shape, jnp.float32),
        in_specs=[
            pl.BlockSpec(terms.shape, lambda i: (0, 0, 0), pipeline_mode=pl.Buffered(1)),
            pl.BlockSpec(band.shape, lambda i: (0, 0, 0, 0), pipeline_mode=pl.Buffered(1)),
        ]
        + [pl.BlockSpec((STEP_TILES * across, cells.shape[1]), lambda i: (i, 0)) for cells in more],
        out_specs=pl.BlockSpec(out_block, lambda i: (i, 0)),
        scratch_shapes=[
            pltpu.VMEM((2, across + GROUPS, LANES), jnp.float32),
            pltpu.VMEM((count, tiles, across, 2 * PHASE), jnp.bfloat16),
        ],
        compiler_params=pltpu.CompilerParams(vmem_limit_bytes=56 << 20),
        cost_estimate=pl.CostEstimate(flops=work, bytes_accessed=16 << 20, transcendentals=0),
    )(terms, band, *more)


def extended(cells, sides, width):
    for axis, dim in sides:
        ends = lax.axis_size(axis) - 1
        head = lax.slice_in_dim(cells, 0, width, axis=dim)
        tail = lax.slice_in_dim(cells, cells.shape[dim] - width, cells.shape[dim], axis=dim)
        before = lax.ppermute(tail, axis, [(i, i + 1) for i in range(ends)])
        after = lax.ppermute(head, axis, [(i + 1, i) for i in range(ends)])
        cells = jnp.concatenate([before, cells, after], axis=dim)
    return cells


def band_weights(headings, extents):
    shape = (3, 2, TILE_ROWS, TILE_LANES, TILE_ROWS, TILE_LANES)
    index = [lax.broadcasted_iota(jnp.int32, shape, axis) for axis in range(6)]
    offset_v = TILE_ROWS * index[0] + index[2] - R - index[4]
    offset_u = TILE_LANES * index[1] + index[3] - R - index[5]
    keep = (jnp.abs(offset_v) <= R) & (jnp.abs(offset_u) <= R)
    rows = 3 * 2 * PHASE

    def flat(cells):
        return cells.reshape(rows, 1, PHASE)

    heights, shares = ellipsoid(
        flat(offset_u.astype(jnp.float32)),
        flat(offset_v.astype(jnp.float32)),
        headings[None, :, None],
        extents[None, :, None],
    )
    keep = flat(keep)
    count = headings.shape[0]

    def whole(cells):
        return jnp.where(keep, cells, 0.0).astype(jnp.bfloat16).reshape(3, 2 * PHASE, count * PHASE)

    heights = whole(heights)
    return jnp.stack([whole(shares), heights])


def pick_tiles(library, index):
    def copy_kernel(index_ref, in_ref, out_ref):
        out_ref[...] = in_ref[...]

    block = (1,) + library.shape[1:]
    flat = index.reshape(-1)
    picked = pl.pallas_call(
        copy_kernel,
        out_shape=jax.ShapeDtypeStruct(flat.shape + library.shape[1:], library.dtype),
        grid_spec=pltpu.PrefetchScalarGridSpec(
            num_scalar_prefetch=1,
            grid=flat.shape,
            in_specs=[pl.BlockSpec(block, lambda i, index_ref: (index_ref[i], 0, 0))],
            out_specs=pl.BlockSpec(block, lambda i, index_ref: (i, 0, 0)),
        ),
    )(flat, library)
    return picked.reshape(index.shape + library.shape[1:])


def body(noise, elevation_library, tile_choice_index, family_heading_index, family_extent_index):
    side_cells = noise.shape[2]
    row_count = lax.axis_size("row")
    col_count = lax.axis_size("col")
    split = lax.axis_size("orient")
    row, col, side = (lax.axis_index(axis) for axis in ("row", "col", "orient"))
    devices = row_count * col_count * split
    lines = noise.shape[1] // split
    window_rows = side_cells // row_count
    window_columns = side_cells // (col_count * split)

    families = jnp.stack([family_heading_index, family_extent_index])
    held_families = [families]
    for turn in range(1, split):
        pairs = [(i, (i + turn) % split) for i in range(split)]
        held_families.append(lax.ppermute(families, "orient", pairs))
    families = jnp.concatenate(held_families, axis=1)
    choices = extended(tile_choice_index, (("row", 0), ("col", 1)), 1)

    own = lax.dynamic_slice_in_dim(noise, side * lines, lines, 1)
    first_line = lax.axis_index(("row", "col", "orient")) * lines
    v_index = first_line + lax.broadcasted_iota(jnp.int32, (lines, side_cells), 0)
    u_index = lax.broadcasted_iota(jnp.int32, (lines, side_cells), 1)
    weights = own * amplitude(u_index, v_index, side_cells)[None]
    spectrum = transform(weights, False, lines, side_cells, devices, 0)
    spectrum, choices, families = lax.optimization_barrier((spectrum, choices, families))
    held = lax.all_to_all(spectrum, ("row", "col", "orient"), split_axis=0, concat_axis=0, tiled=True)
    tall = window_columns + 2 * R
    wide = (window_rows // LANES + 1) * LANES
    spare = wide - window_rows - 2 * R
    tile_side = elevation_library.shape[1]
    tiles_x = window_rows // tile_side
    tiles_y = window_columns // tile_side
    first_y = col * split + side
    local = lax.dynamic_slice_in_dim(choices, side * tiles_y, tiles_y + 2, 1)
    slope = pick_tiles(elevation_library.transpose(0, 2, 1), local.T)
    slope = slope.transpose(0, 2, 1, 3).reshape((tiles_y + 2) * tile_side, (tiles_x + 2) * tile_side)
    edge = tile_side - R
    slope = slope[edge : edge + tall, edge : edge + wide]
    y = first_y * window_columns - R + lax.broadcasted_iota(jnp.int32, (tall, wide), 0)
    x = row * window_rows - R + lax.broadcasted_iota(jnp.int32, (tall, wide), 1)
    inside = (y >= 0) & (y < side_cells) & (x >= 0) & (x < side_cells)
    secant = jnp.sqrt(1.0 + slope * slope)
    lift = jnp.where(inside, 0.5 * secant, 0.0)
    grip = jnp.where(inside, 0.6 / secant, 0.0)
    drive = jnp.where(inside, slope / secant, 0.0).astype(jnp.bfloat16)
    band = band_weights(families[0], families[1])
    held, lift, grip, drive = lax.optimization_barrier((held, lift, grip, drive))
    positions = side_cells // devices
    per_block = LANES // lines
    held = held.reshape(side_cells // LANES, per_block, 2, positions, lines)
    held = held.transpose(0, 2, 3, 1, 4).reshape(side_cells // LANES, 2, positions, LANES)
    fields = transform(held, True, positions, side_cells, col_count * split, R)
    fields = lax.all_to_all(fields, ("col", "orient"), split_axis=0, concat_axis=0, tiled=True)
    across = window_rows // TILE_LANES
    driving = tile_call(
        driving_kernel,
        drive[None],
        band[1:],
        window_columns,
        window_rows,
        (window_columns // TILE_ROWS * across, band.shape[-1]),
        (STEP_TILES * across, band.shape[-1]),
    )
    fields, driving, band = lax.optimization_barrier((fields, driving, band))
    fields = fields.transpose(1, 2, 0, 3).reshape(2, tall, window_rows)
    ends = row_count - 1
    before = lax.ppermute(fields[:, :, window_rows - R :], "row", [(i, i + 1) for i in range(ends)])
    after = lax.ppermute(fields[:, :, :R], "row", [(i + 1, i) for i in range(ends)])
    fields = jnp.concatenate(
        [before, fields, after, jnp.zeros((2, tall, spare), fields.dtype)], axis=2
    ).astype(jnp.float32)

    cohesion = (jnp.exp(0.4 * fields[0]) * lift).astype(jnp.bfloat16)
    friction = (jnp.exp(0.25 * fields[1]) * grip).astype(jnp.bfloat16)
    safety = tile_call(
        stability_kernel,
        jnp.stack([cohesion, friction]),
        band,
        window_columns,
        window_rows,
        (window_columns, window_rows),
        (TILE_ROWS * STEP_TILES, window_rows),
        (driving,),
    )
    return safety.T


TURNED = (((1,), (1,)), ((), ()))
DOT = functools.partial(lax.dot_general, dimension_numbers=TURNED, preferred_element_type=jnp.float32)
MESH = pl.DeviceIdType.MESH
CHUNK = 32
CHUNKS = LANES // CHUNK
SPLIT = 6
TERM = 6 * LANES


def strip_of(row, col, side, cols):
    return row * (2 * cols) + col + side * (2 * cols - 1 - 2 * col)


def place_of(strip, cols):
    row = strip // (2 * cols)
    at = strip % (2 * cols)
    side = at // cols
    return row, at + side * (2 * cols - 1 - 2 * at), side


def tables(length):
    outer = length // LANES
    q = np.arange(LANES)
    turns = []
    for shift in (R, 0):
        turn = 2 * np.pi * (np.arange(outer)[:, None] - shift) * q / length
        turns += [np.cos(turn), np.sin(turn)]
    angle = 2 * np.pi * (q[:, None] * q % LANES) / LANES
    table = np.block([[np.cos(angle), np.sin(angle)], [-np.sin(angle), np.cos(angle)]]).astype(np.float32)
    big = table.astype(jnp.bfloat16)
    small = (table - big.astype(np.float32)).astype(jnp.bfloat16)
    u = np.arange(length)
    wrapped = np.minimum(u, length - u) / (length / cutoff_ratio)
    turns.append((wrapped * wrapped).reshape(outer, LANES))
    return np.stack(turns).astype(np.float32), np.concatenate([big, big, small], axis=1)


def swap8(cells):
    cells = [pltpu.roll(c, TILE_LANES * i, 1) if i else c for i, c in enumerate(cells)]
    group = lax.broadcasted_iota(jnp.int32, cells[0].shape, 1) // TILE_LANES
    for bit in (1, 2, 4):
        pick = (group & bit) != 0
        cells = [jnp.where(pick, cells[(i + bit) % GROUPS], cells[i]) for i in range(GROUPS)]
    out = []
    for i in range(GROUPS):
        c = cells[-i % GROUPS]
        out.append(pltpu.roll(c, LANES - TILE_LANES * i, 1) if i else c)
    return out


def pair_dot(wide, first, second):
    value = jnp.concatenate([first, second], axis=0)
    high = value.astype(jnp.bfloat16)
    rest = (value - high.astype(jnp.float32)).astype(jnp.bfloat16)
    return DOT(wide, jnp.concatenate([high, rest, high], axis=1))


def spread(into, base, a, g, at, value):
    for shift in range(3):
        to = a + 1 - shift
        if 0 <= to < 4:
            spot(into, base, to, g, at, shift, value)


def spot(into, base, to, g, at, shift, value):
    first = base + shift * 2 * LANES
    if g < GROUPS:
        into[to, g, at, first : first + LANES] = value
    if g > 0:
        into[to, g - 1, at, first + LANES : first + 2 * LANES] = value


def band_rows(family_ref, band, side):
    params = []
    for owner in range(2):
        both = family_ref[owner].astype(jnp.float32)
        heading = both[0:4] * (math.pi / N_AZ)
        semi_axis = R * (both[4:8] + (1 + NSIZE)) / (2 * NSIZE)
        params.append((jnp.cos(heading), jnp.sin(heading), 1.0 / semi_axis, 1.0 / (0.6 * semi_axis), 0.3 * semi_axis))
    shape = (16, LANES)
    lane = lax.broadcasted_iota(jnp.int32, shape, 1)
    row = lax.broadcasted_iota(jnp.int32, shape, 0)

    @pl.loop(0, TERM // 16)
    def _(block):
        offset_v = TILE_ROWS * (block // 16) + block % 8 - R - lane // TILE_LANES
        offset_u = TILE_LANES * (block // 8 % 2) - R + row - lane % TILE_LANES
        keep = (jnp.abs(offset_v) <= R) & (jnp.abs(offset_u) <= R)
        v = offset_v.astype(jnp.float32)
        u = offset_u.astype(jnp.float32)
        at = pl.multiple_of(block * 16, 16)
        for family in range(8):
            cos, sin, per_semi, per_across, slip_depth = [p[family % 4 : family % 4 + 1] for p in params[family // 4]]
            along = (u * cos + v * sin) * per_semi
            lateral = (v * cos - u * sin) * per_across
            inside = 1.0 - along * along - lateral * lateral
            height = slip_depth * jnp.sqrt(jnp.maximum(inside, 0.0))
            share = jnp.clip(4.0 * inside, 0.0, 1.0)
            lanes = slice(family * LANES, (family + 1) * LANES)
            band[pl.ds(at, 16), lanes] = jnp.where(keep, share, 0.0).astype(jnp.bfloat16)
            band[pl.ds(at + TERM, 16), lanes] = jnp.where(keep, height, 0.0).astype(jnp.bfloat16)


def whole_kernel(
    sizes, noise_any, choice_ref, heading_ref, extent_ref, lib_any, turn_ref, wide_ref,
    out_any,
    mid, full, send_a, send_b, held_a, held_b, lift, grip, gathered, inv, band, edge, edge_send, halo_out, halo_in,
    natural, staged, factor, code_in, scale_in, done, library, choice_in, family_in, choice_smem,
    noise_sem, first_send, first_recv, choice_send, choice_recv, family_send, family_recv, smem_sem,
    halo_send, halo_recv, out_send, out_recv, scale_send, scale_recv, library_sem, done_sem,
):
    row_count, cols = sizes
    row, col, side = (lax.axis_index(axis) for axis in ("row", "col", "orient"))
    devices = row_count * cols * 2
    group = cols * 2
    me = (row * cols + col) * 2 + side
    strip = strip_of(row, col, side, cols)
    mine = strip % group
    block_here = col * 2 + side
    plane = row * cols + col
    left = place_of(lax.rem(strip + devices - 1, devices), cols)
    outer = turn_ref.shape[1]

    def device(index):
        return index // group, index % group // 2, index % 2

    def owner(block):
        return row, block // 2, block % 2

    barrier = pltpu.get_barrier_semaphore()

    @pl.loop(1, devices)
    def _(k):
        pl.semaphore_signal(barrier, inc=1, device_id=device(lax.rem(me + k, devices)), device_id_type=MESH)

    def noise_copy(chunk, part, piece):
        lines = pl.ds(pl.multiple_of(side * LANES + chunk * CHUNK, CHUNK), CHUNK)
        return pltpu.make_async_copy(
            noise_any.at[part, lines, piece * 1024 : (piece + 1) * 1024],
            inv.at[0, part * 2 + piece // 2, piece % 2 * 4 + chunk],
            noise_sem.at[chunk, part * 4 + piece],
        )

    for chunk in range(CHUNKS):
        for part in range(2):
            for piece in range(4):
                noise_copy(chunk, part, piece).start()

    library_copy = pltpu.make_async_copy(lib_any, library, library_sem)
    library_copy.start()
    choice_in[plane] = jnp.zeros((8, LANES), jnp.int32)
    choice_in[plane, 0:4, 0:16] = choice_ref[...]
    which = lax.broadcasted_iota(jnp.int32, (8, LANES), 0)
    mixed = jnp.zeros((8, LANES), jnp.int32)
    for f in range(4):
        mixed = jnp.where(which == f, heading_ref[f], mixed)
        mixed = jnp.where(which == f + 4, extent_ref[f], mixed)
    family_in[side] = mixed

    for chunk in range(CHUNKS):
        for part in range(2):
            for piece in range(4):
                noise_copy(chunk, part, piece).wait()

        @pl.loop(0, CHUNK // 8)
        def _(block):
            at = pl.ds(pl.multiple_of(block * 8, 8), 8)
            line = me * LANES + chunk * CHUNK + block * 8 + lax.broadcasted_iota(jnp.int32, (8, LANES), 0)
            wrap_v = jnp.minimum(line, outer * LANES - line).astype(jnp.float32) * (cutoff_ratio / (outer * LANES))
            base = 1.0 + wrap_v * wrap_v
            parts = []
            for p in range(outer):
                root = lax.rsqrt(base + turn_ref[4, p : p + 1, :])
                spectrum = nugget_share + peak_share * (root * root * root)
                level = spectrum * lax.rsqrt(spectrum) * (1.0 / (outer * LANES))
                spot_at = (p // 16, p // 8 % 2 * 4 + chunk, at, slice(p % 8 * LANES, (p % 8 + 1) * LANES))
                parts.append((inv[(0,) + spot_at] * level, inv[(0, 2 + spot_at[0]) + spot_at[1:]] * level))
            turned = small_dft(parts)
            rows = pl.ds(pl.multiple_of(chunk * CHUNK + block * 8, 8), 8)
            for k in range(outer):
                re, im = turned[(k - R) % outer]
                cos = turn_ref[0, k : k + 1, :]
                sin = turn_ref[1, k : k + 1, :]
                mid[k, rows, 0:LANES] = re * cos + im * sin
                mid[k, rows, LANES : 2 * LANES] = im * cos - re * sin

    pl.semaphore_wait(barrier, devices - 1)

    def choice_copy(k):
        to = lax.rem(plane + k, row_count * cols)
        return pltpu.make_async_remote_copy(
            src_ref=choice_in.at[plane], dst_ref=choice_in.at[plane],
            send_sem=choice_send.at[k], recv_sem=choice_recv.at[k],
            device_id=(to // cols, to % cols, side), device_id_type=MESH,
        )

    def family_copy():
        return pltpu.make_async_remote_copy(
            src_ref=family_in.at[side], dst_ref=family_in.at[side], send_sem=family_send, recv_sem=family_recv,
            device_id=(row, col, 1 - side), device_id_type=MESH,
        )

    @pl.loop(1, row_count * cols)
    def _(k):
        choice_copy(k).start()

    family_copy().start()

    for k in range(0, outer, 2):
        got = pair_dot(wide_ref[...], mid[k], mid[k + 1])
        for part in range(2):
            for one in range(2):
                piece = got[part * LANES : (part + 1) * LANES, one * LANES : (one + 1) * LANES]
                full[part, pl.ds(k + one, LANES, stride=outer), :] = piece

    parts_of = ((0, SPLIT, send_a, held_a), (SPLIT, GROUPS, send_b, held_b))

    def partner(k):
        return me ^ (k % 2 * 8 + k // 2 % 8 + k // 16 * 16)

    def first_copy(c, k):
        to = partner(k)
        return pltpu.make_async_remote_copy(
            src_ref=parts_of[c][2].at[to], dst_ref=parts_of[c][3].at[me],
            send_sem=first_send.at[c, k], recv_sem=first_recv.at[c, k],
            device_id=device(to), device_id_type=MESH,
        )

    for c, (low_g, high_g, send, held) in enumerate(parts_of):
        count = (high_g - low_g) * 16

        def packed(to, into):
            to_strip = strip_of(*device(to), cols)
            at = pl.ds(pl.multiple_of(to_strip * LANES + low_g * 16, 16), count)
            for part in range(2):
                into[to, part] = full[part, at, :].astype(jnp.bfloat16)

        @pl.loop(1, devices)
        def _(k):
            packed(partner(k), send)
            first_copy(c, k).start()

        packed(me, held)

    family_copy().wait()
    band_rows(family_in, band, side)

    @pl.loop(1, row_count * cols)
    def _(k):
        choice_copy(k).wait()

    to_smem = pltpu.make_async_copy(choice_in, choice_smem, smem_sem)
    to_smem.start()
    to_smem.wait()
    library_copy.wait()

    @pl.loop(0, library.shape[0])
    def _(t):
        library[t] = pltpu.roll(library[t].T, R, 1)

    left_lanes = lax.broadcasted_iota(jnp.int32, (LANES, LANES), 1) < R

    def tile(shift, t):
        x = lax.rem(strip + devices + shift, devices)
        return library[choice_smem[x // 16 * cols + t // 4, t % 4, x % 16]]

    @pl.loop(0, outer)
    def _(t):
        at = pl.ds(pl.multiple_of(t * LANES, LANES), LANES)
        here = tile(0, t)
        full[0, at, :] = jnp.where(left_lanes, tile(-1, t), here)
        full[1, at, :] = jnp.where(left_lanes, here, tile(1, t))

    half = lax.broadcasted_iota(jnp.int32, (16, LANES), 1) % TILE_LANES < R
    first = strip == 0
    last = strip == devices - 1
    for side_rows in (slice(0, 8), slice(8 + LANES, 16 + LANES)):
        edge[:, :, side_rows, :] = jnp.zeros((2, GROUPS + 1, 8, LANES), jnp.float32)
        edge_send[:, side_rows, :] = jnp.zeros((2, 8, LANES), jnp.float32)

    for a in range(4):
        @pl.loop(0, 8)
        def _(c):
            at = pl.ds(pl.multiple_of(c * 16, 16), 16)
            for source in range(2):
                turned = swap8([full[source, pl.ds(c * 512 + 8 * a + r, 16, stride=32), :] for r in range(8)])
                for g in range(GROUPS) if source == 0 else (0,):
                    slope = turned[g]
                    square = 1.0 + slope * slope
                    inverse = lax.rsqrt(square)
                    drive = slope * inverse
                    tile_at = g
                    if source == 0:
                        lift[a, g, at, :] = 0.5 * square * inverse
                        grip[a, g, at, :] = 0.6 * inverse
                        if g == 0:
                            drive = jnp.where(half & first, 0.0, drive)
                    else:
                        tile_at = GROUPS
                        drive = jnp.where(last & ~half, 0.0, drive)
                    spread(gathered, TERM, a, tile_at, at, drive.astype(jnp.bfloat16))
                    if a in (0, 3):
                        edge[0, tile_at, pl.ds(pl.multiple_of(c * 16 + 8, 8), 16), :] = drive

        if a in (0, 3):
            @pl.loop(0, 8)
            def _(c):
                at = pl.ds(pl.multiple_of(c * 16, 16), 16)
                for g in range(GROUPS + 1):
                    value = edge[0, g, pl.ds(c * 16 + (9 if a == 0 else 7), 16), :].astype(jnp.bfloat16)
                    spot(gathered, TERM, 3 - a, g, at, 2 if a == 0 else 0, value)

    pairs = band.shape[1] // (2 * PHASE)

    @pl.loop(0, CHUNKS)
    def _(chunk):
        at = pl.ds(pl.multiple_of(chunk * CHUNK, CHUNK), CHUNK)
        cells = gathered[:, :, at, TERM:].reshape(4 * GROUPS * CHUNK, TERM)
        for pair in range(pairs):
            lanes = slice(pair * 2 * PHASE, (pair + 1) * 2 * PHASE)
            sums = jnp.dot(cells, band[TERM:, lanes], preferred_element_type=jnp.float32)
            inv[chunk, :, :, :, lanes] = (1.0 / sums).reshape(4, GROUPS, CHUNK, 2 * PHASE)

    def halo_copy(slot):
        return pltpu.make_async_remote_copy(
            src_ref=halo_out.at[slot], dst_ref=halo_in.at[slot],
            send_sem=halo_send.at[slot], recv_sem=halo_recv.at[slot],
            device_id=left, device_id_type=MESH,
        )

    per_chunk = CHUNK * outer // (2 * LANES)
    home = block_here // per_chunk

    def out_copy(c, block, source):
        return pltpu.make_async_remote_copy(
            src_ref=staged.at[c, block], dst_ref=code_in.at[source, c],
            send_sem=out_send.at[c, block], recv_sem=out_recv.at[c, source],
            device_id=owner(block), device_id_type=MESH,
        )

    def scale_copy(c, block, source):
        return pltpu.make_async_remote_copy(
            src_ref=factor.at[c, block // (2 * per_chunk)], dst_ref=scale_in.at[source, c],
            send_sem=scale_send.at[c, block], recv_sem=scale_recv.at[c, source],
            device_id=owner(block), device_id_type=MESH,
        )

    for c, (low_g, high_g, send, held) in enumerate(parts_of):
        @pl.loop(1, devices)
        def _(k):
            first_copy(c, k).wait()

        @pl.loop(low_g, high_g)
        def _(g):
            at = pl.ds(pl.multiple_of((g - low_g) * 16, 16), 16)
            parts = [(held[p, 0, at, :].astype(jnp.float32), held[p, 1, at, :].astype(jnp.float32)) for p in range(outer)]
            for k, (re, im) in enumerate(small_dft(parts)):
                to = slice(k % 8 * 16, (k % 8 + 1) * 16)
                cos = turn_ref[2, k : k + 1, :]
                sin = turn_ref[3, k : k + 1, :]
                mid[k // 8 * 8 + g, to, 0:LANES] = re * cos + im * sin
                mid[k // 8 * 8 + g, to, LANES : 2 * LANES] = im * cos - re * sin

        items = [(a, g) for g in range(low_g, high_g) for a in range(4)]
        for at_item in range(0, len(items), 2):
            two = items[at_item : at_item + 2]
            got = pair_dot(wide_ref[...], *[mid[a * 8 + g] for a, g in two])
            for one, (a, g) in enumerate(two):
                for term in range(2):
                    field = got[term * LANES : (term + 1) * LANES, one * LANES : (one + 1) * LANES]
                    value = jnp.exp((0.4 if term == 0 else 0.25) * field) * (lift if term == 0 else grip)[a, g]
                    if g == 0:
                        mask = lax.broadcasted_iota(jnp.int32, (LANES, LANES), 1) % TILE_LANES < R
                        sent = jnp.where(first & ~mask, 0.0, value)
                        value = jnp.where(first & mask, 0.0, value)
                        halo_out[a, term] = sent.astype(jnp.bfloat16)
                    spread(gathered, term * TERM, a, g, slice(None), value.astype(jnp.bfloat16))
                    if a in (0, 3):
                        moved = slice(9, 9 + LANES) if a == 0 else slice(7, 7 + LANES)
                        edge[term, g, 8 : 8 + LANES, :] = value
                        near = edge[term, g, moved, :].astype(jnp.bfloat16)
                        spot(gathered, term * TERM, 3 - a, g, slice(None), 2 if a == 0 else 0, near)
                        if g == 0:
                            edge_send[term, 8 : 8 + LANES, :] = sent
                            halo_out[4 if a == 0 else 5, term] = edge_send[term, moved, :].astype(jnp.bfloat16)
                if g == 0:
                    halo_copy(a).start()
                    if a in (0, 3):
                        halo_copy(4 if a == 0 else 5).start()

        if c == 1:
            for slot in range(6):
                halo_copy(slot).wait()
                for term in range(2):
                    value = halo_in[slot, term]
                    if slot < 4:
                        spread(gathered, term * TERM, slot, GROUPS, slice(None), value)
                    else:
                        to, shift = (3, 2) if slot == 4 else (0, 0)
                        spot(gathered, term * TERM, to, GROUPS, slice(None), shift, value)

        tiles = slice(c * 4, c * 4 + 4)

        @pl.loop(0, 2)
        def _(step):
            half_at = (home // 2) ^ (1 - step)
            cells = []
            for q in range(2):
                at = pl.ds(pl.multiple_of((half_at * 2 + q) * CHUNK, CHUNK), CHUNK)
                cells.append(gathered[:, tiles, at, :].reshape(16 * CHUNK, 2 * TERM))
            cells = jnp.concatenate(cells, axis=0)
            low = None
            for pair in range(pairs):
                lanes = slice(pair * 2 * PHASE, (pair + 1) * 2 * PHASE)
                ratio = jnp.dot(cells, band[:, lanes], preferred_element_type=jnp.float32)
                ratio = ratio * inv[pl.ds(half_at * 2, 2), :, tiles, :, lanes].reshape(32 * CHUNK, 2 * PHASE)
                least = jnp.minimum(ratio[:, 0:PHASE], ratio[:, PHASE:])
                low = least if low is None else jnp.minimum(low, least)
            largest = jnp.max(jnp.max(low, axis=0, keepdims=True), axis=1, keepdims=True)
            largest = jnp.broadcast_to(jnp.maximum(largest, 1e-30), (8, LANES))
            factor[c, half_at] = jnp.sqrt(largest) * (1.0 / 65535.0)
            upward = (65535.0 * lax.rsqrt(largest))[0:1, :]
            low = low.reshape(2, 4, 4, 2, CHUNK // 2, LANES)
            for q in range(2):
                for a in range(4):
                    turned = swap8([low[q, a, g % 4, g // 4] for g in range(GROUPS)])
                    for r in range(8):
                        code = jnp.sqrt(turned[r]) * upward + 0.5
                        natural[q, pl.ds(8 * a + r, CHUNK // 2, stride=32), :] = code
                for piece in range(4):
                    code = natural[q, piece * LANES : (piece + 1) * LANES, :]
                    code = (code.astype(jnp.int32) - 32768).T.astype(jnp.int16)
                    for upper in range(2):
                        block = (half_at * 2 + q) * per_chunk + upper * 2 + piece // 2
                        staged[c, block, :, piece % 2 * LANES : (piece % 2 + 1) * LANES] = code[upper * 64 : upper * 64 + 64]

            @pl.loop(0, 2 * per_chunk)
            def _(i):
                block = half_at * 2 * per_chunk + (i ^ (per_chunk * (1 - home % 2)))

                @pl.when(block != block_here)
                def _():
                    out_copy(c, block, mine).start()
                    scale_copy(c, block, mine).start()

    def done_copy(c, source):
        rows = pl.ds(pl.multiple_of(source * LANES + c * 64, 64), 64)
        return pltpu.make_async_copy(done.at[source, c], out_any.at[rows], done_sem.at[c, source])

    def finish(c, source, code, scale):
        root = (code.astype(jnp.float32) + 32768.0) * scale[0:1, 0:1]
        done[source, c] = root * root
        done_copy(c, source).start()

    for c in range(2):
        finish(c, mine, staged[c, block_here], factor[c, home // 2])

        @pl.loop(0, group)
        def _(at):
            block = (home ^ (3 - at // per_chunk)) * per_chunk + at % per_chunk
            source = strip_of(0, block // 2, block % 2, cols)

            @pl.when(block != block_here)
            def _():
                out_copy(c, block, source).wait_recv()
                scale_copy(c, block, source).wait_recv()
                finish(c, source, code_in[source, c], scale_in[source, c])

    @pl.loop(1, group)
    def _(turned):
        block = lax.rem(block_here + turned, group)
        for c in range(2):
            out_copy(c, block, mine).wait_send()
            scale_copy(c, block, mine).wait_send()

    @pl.loop(0, group)
    def _(source):
        for c in range(2):
            done_copy(c, source).wait()


def whole_safety(noise, choices, headings, extents, library, row_count, cols):
    length = noise.shape[2]
    outer = length // LANES
    group = 2 * cols
    devices = group * row_count
    turns, wide = tables(length)
    vmem = pl.BlockSpec(memory_space=pltpu.VMEM)
    smem = pl.BlockSpec(memory_space=pltpu.SMEM)
    dma = pltpu.SemaphoreType.DMA
    f32, bf16 = jnp.float32, jnp.bfloat16
    early, late = SPLIT * 16, LANES - SPLIT * 16
    return pl.pallas_call(
        functools.partial(whole_kernel, (row_count, cols)),
        out_shape=jax.ShapeDtypeStruct((group * LANES, 2 * LANES), f32),
        in_specs=[pl.BlockSpec(memory_space=pl.ANY), vmem, smem, smem, pl.BlockSpec(memory_space=pl.ANY), vmem, vmem],
        out_specs=pl.BlockSpec(memory_space=pl.ANY),
        scratch_shapes=[
            pltpu.VMEM((outer, LANES, 2 * LANES), f32),
            pltpu.VMEM((2, length, LANES), f32),
            pltpu.VMEM((devices, 2, early, LANES), bf16),
            pltpu.VMEM((devices, 2, late, LANES), bf16),
            pltpu.VMEM((devices, 2, early, LANES), bf16),
            pltpu.VMEM((devices, 2, late, LANES), bf16),
            pltpu.VMEM((4, GROUPS, LANES, LANES), f32),
            pltpu.VMEM((4, GROUPS, LANES, LANES), f32),
            pltpu.VMEM((4, GROUPS, LANES, 2 * TERM), bf16),
            pltpu.VMEM((CHUNKS, 4, GROUPS, CHUNK, 8 * PHASE), f32),
            pltpu.VMEM((2 * TERM, 8 * PHASE), bf16),
            pltpu.VMEM((2, GROUPS + 1, LANES + 16, LANES), f32),
            pltpu.VMEM((2, LANES + 16, LANES), f32),
            pltpu.VMEM((6, 2, LANES, LANES), bf16),
            pltpu.VMEM((6, 2, LANES, LANES), bf16),
            pltpu.VMEM((2, length // CHUNKS // 2, LANES), f32),
            pltpu.VMEM((2, group, LANES // 2, 2 * LANES), jnp.int16),
            pltpu.VMEM((2, 2, 8, LANES), f32),
            pltpu.VMEM((group, 2, LANES // 2, 2 * LANES), jnp.int16),
            pltpu.VMEM((group, 2, 8, LANES), f32),
            pltpu.VMEM((group, 2, LANES // 2, 2 * LANES), f32),
            pltpu.VMEM(library.shape, f32),
            pltpu.VMEM((row_count * cols, 8, LANES), jnp.int32),
            pltpu.VMEM((2, 8, LANES), jnp.int32),
            pltpu.SMEM((row_count * cols, 8, LANES), jnp.int32),
            dma((CHUNKS, 8)), dma((2, devices)), dma((2, devices)),
            dma((row_count * cols,)), dma((row_count * cols,)), dma, dma, dma,
            dma((6,)), dma((6,)), dma((2, group)), dma((2, group)), dma((2, group)), dma((2, group)), dma, dma((2, group)),
        ],
        compiler_params=pltpu.CompilerParams(
            vmem_limit_bytes=62 << 20, collective_id=0, has_side_effects=True
        ),
    )(noise, choices, headings, extents, library, turns, wide)


def strip_body(noise, elevation_library, tile_choice_index, family_heading_index, family_extent_index):
    row_count, cols = lax.axis_size("row"), lax.axis_size("col")
    return whole_safety(
        noise, tile_choice_index.T, family_heading_index, family_extent_index, elevation_library, row_count, cols
    )


def chosen_body(noise, elevation_library, tile_choice_index, family_heading_index, family_extent_index):
    shape = (lax.axis_size("row"), lax.axis_size("col"), lax.axis_size("orient"))
    side_cells = noise.shape[2]
    fits = (
        shape == (2, 8, 2)
        and side_cells == 32 * LANES
        and elevation_library.shape[1] == LANES
        and tile_choice_index.shape == (16, 4)
        and family_heading_index.shape[0] == 4
    )
    chosen = strip_body if fits else body
    return chosen(noise, elevation_library, tile_choice_index, family_heading_index, family_extent_index)


def solution(mesh):
    placed = (P(None, ("row", "col"), None), P(), P("row", "col"), P("orient"), P("orient"))
    return jax.shard_map(
        chosen_body, mesh=mesh, in_specs=placed, out_specs=P("row", ("col", "orient")), check_vma=False
    )
```

```python
import functools
import math

import jax
import jax.numpy as jnp
import numpy as np
from jax import lax
from jax.experimental import pallas as pl
from jax.experimental.pallas import tpu as pltpu
from jax.sharding import PartitionSpec as P

R = 8
N_AZ = 36
NSIZE = 4
LANES = 128
TILE_ROWS = 8
TILE_LANES = 16
GROUPS = LANES // TILE_LANES
PHASE = TILE_ROWS * TILE_LANES
STEP_TILES = 8

nugget_share = 0.3
peak_share = 1024.0 / (2.0 * math.pi)
cutoff_ratio = 32.0


def amplitude(u_index, v_index, side_cells):
    wrap_u = jnp.minimum(u_index, side_cells - u_index).astype(jnp.float32)
    wrap_v = jnp.minimum(v_index, side_cells - v_index).astype(jnp.float32)
    cutoff = side_cells / cutoff_ratio
    scaled_u = wrap_u / cutoff
    scaled_v = wrap_v / cutoff
    grown = 1.0 + scaled_u * scaled_u + scaled_v * scaled_v
    spectrum = nugget_share + peak_share / (grown * jnp.sqrt(grown))
    return jnp.sqrt(spectrum) / side_cells


def ellipsoid(offset_u, offset_v, azimuth, size_index):
    heading = azimuth.astype(jnp.float32) * (math.pi / N_AZ)
    semi_axis = R * (size_index.astype(jnp.float32) + (1 + NSIZE)) / (2 * NSIZE)
    across = 0.6 * semi_axis
    slip_depth = 0.3 * semi_axis
    along = offset_u * jnp.cos(heading) + offset_v * jnp.sin(heading)
    lateral = offset_v * jnp.cos(heading) - offset_u * jnp.sin(heading)
    along_part = along / semi_axis
    lateral_part = lateral / across
    inside = 1.0 - along_part * along_part - lateral_part * lateral_part
    height = slip_depth * jnp.sqrt(jnp.maximum(inside, 0.0))
    base_share = jnp.clip(4.0 * inside, 0.0, 1.0)
    return (height, base_share)


def small_dft(parts):
    count = len(parts)
    if count == 1:
        return parts
    even = small_dft(parts[0::2])
    odd = small_dft(parts[1::2])
    low, high = [], []
    for k in range(count // 2):
        (a, b), (c, d) = even[k], odd[k]
        if k == 0:
            e, f = c, d
        elif 4 * k == count:
            e, f = d, -c
        else:
            cos = math.cos(2 * math.pi * k / count)
            sin = math.sin(2 * math.pi * k / count)
            e, f = c * cos + d * sin, d * cos - c * sin
        low.append((a + e, b + f))
        high.append((a - e, b - f))
    return low + high


def transform_kernel(planes, blocks, span, step, pad, in_ref, cos_ref, sin_ref, big_ref, small_ref, out_ref, mid, full):
    outer = cos_ref.shape[0]
    rows = mid.shape[1]
    unit = 16 if planes else 8

    @pl.loop(0, rows // unit)
    def _(block):
        at = pl.ds(pl.multiple_of(block * unit, unit), unit)
        parts = []
        for p in range(outer):
            if planes:
                parts.append((in_ref[p, 0, at, :].astype(jnp.float32), in_ref[p, 1, at, :].astype(jnp.float32)))
            else:
                lanes = slice(p * LANES, (p + 1) * LANES)
                parts.append((in_ref[0, at, lanes], in_ref[1, at, lanes]))
        for k, (re, im) in enumerate(small_dft(parts)):
            cos = cos_ref[k : k + 1, :]
            sin = sin_ref[k : k + 1, :]
            mid[k, at, 0:LANES] = re * cos + im * sin
            mid[k, at, LANES : 2 * LANES] = im * cos - re * sin

    if pad:
        edge = jnp.zeros((pad, rows), jnp.float32)
        for part in range(2):
            full[part, 0:pad, :] = edge
            full[part, pad + outer * LANES : 2 * pad + outer * LANES, :] = edge

    turned = (((1,), (1,)), ((), ()))
    dot = functools.partial(lax.dot_general, dimension_numbers=turned, preferred_element_type=jnp.float32)
    for k in range(outer):
        value = mid[k]
        high = value.astype(jnp.bfloat16)
        rest = (value - high.astype(jnp.float32)).astype(jnp.bfloat16)
        got = dot(big_ref[...], high) + dot(big_ref[...], rest) + dot(small_ref[...], high)
        full[0, pl.ds(pad + k, LANES, stride=outer), :] = got[0:LANES]
        full[1, pl.ds(pad + k, LANES, stride=outer), :] = got[LANES : 2 * LANES]

    @pl.loop(0, blocks)
    def _(block):
        at = pl.ds(pl.multiple_of(block * step, 8), span)
        for part in range(2):
            out_ref[block, part] = full[part, at, :].astype(jnp.bfloat16)


def transform(cells, planes, rows, length, blocks, pad):
    outer = length // LANES
    step = length // blocks
    span = step + 2 * pad
    k = np.arange(outer)[:, None]
    q = np.arange(LANES)
    turn = 2 * np.pi * k * q / length
    cos, sin = np.cos(turn).astype(np.float32), np.sin(turn).astype(np.float32)
    angle = 2 * np.pi * (q[:, None] * q % LANES) / LANES
    table = np.block([[np.cos(angle), np.sin(angle)], [-np.sin(angle), np.cos(angle)]]).astype(np.float32)
    big = table.astype(jnp.bfloat16)
    small = (table - big.astype(np.float32)).astype(jnp.bfloat16)
    vmem = pl.BlockSpec(memory_space=pltpu.VMEM)
    return pl.pallas_call(
        functools.partial(transform_kernel, planes, blocks, span, step, pad),
        out_shape=jax.ShapeDtypeStruct((blocks, 2, span, rows), jnp.bfloat16),
        in_specs=[vmem] * 5,
        out_specs=vmem,
        scratch_shapes=[
            pltpu.VMEM((outer, rows, 2 * LANES), jnp.float32),
            pltpu.VMEM((2, length + 2 * pad, rows), jnp.float32),
        ],
        compiler_params=pltpu.CompilerParams(vmem_limit_bytes=40 << 20),
    )(cells, cos, sin, big, small)


def swap_groups(cells):
    row = lax.broadcasted_iota(jnp.int32, cells.shape, 1)
    group = lax.broadcasted_iota(jnp.int32, cells.shape, 2) // TILE_LANES
    skewed = pltpu.roll(cells, 0, 2, stride=TILE_LANES, stride_axis=1)
    picked = jnp.take_along_axis(skewed, (group + row - 7) & 7, axis=1)
    level = pltpu.roll(picked, TILE_LANES, 2, stride=TILE_LANES, stride_axis=1)
    return jnp.take_along_axis(level, 7 - row, axis=1)


def gather_tiles(term_ref, swapped, gathered):
    tiles, across = gathered.shape[1:3]
    chunks = across // GROUPS

    @pl.when(pl.program_id(0) == 0)
    def _():
        @pl.loop(0, tiles // 2)
        def _(pair):
            at = pl.ds(pl.multiple_of(pair * 16, 16), 16)
            both = pl.ds(pair * 2, 2)
            for term in range(gathered.shape[0]):
                for chunk in range(chunks + 1):
                    cells = term_ref[term, at, chunk * LANES : (chunk + 1) * LANES].astype(jnp.float32)
                    turned = swap_groups(cells.reshape(2, TILE_ROWS, LANES))
                    swapped[:, chunk * GROUPS : (chunk + 1) * GROUPS, :] = turned
                gathered[term, both, :, 0:PHASE] = swapped[:, 0:across, :].astype(jnp.bfloat16)
                gathered[term, both, :, PHASE:] = swapped[:, 1 : across + 1, :].astype(jnp.bfloat16)


def column_sum(gathered, band_ref, lanes):
    terms, _, across, depth = gathered.shape
    tile = pl.program_id(0) * STEP_TILES
    pieces = [(term, shift) for term in range(terms) for shift in range(3)]
    left = [gathered[term, pl.ds(tile + shift, STEP_TILES)] for term, shift in pieces]
    left = [piece.reshape(STEP_TILES * across, depth) for piece in left]
    right = [band_ref[term, shift, :, lanes] for term, shift in pieces]
    return jnp.dot(
        jnp.concatenate(left, axis=1),
        jnp.concatenate(right, axis=0),
        preferred_element_type=jnp.float32,
    )


def driving_kernel(families, term_ref, band_ref, out_ref, swapped, gathered):
    gather_tiles(term_ref, swapped, gathered)
    for pair in range(families // 2):
        lanes = slice(pair * 2 * PHASE, (pair + 1) * 2 * PHASE)
        out_ref[:, lanes] = column_sum(gathered, band_ref, lanes)


def stability_kernel(families, term_ref, band_ref, drive_ref, out_ref, swapped, gathered):
    chunks = gathered.shape[2] // GROUPS
    gather_tiles(term_ref, swapped, gathered)
    low = None
    for pair in range(families // 2):
        lanes = slice(pair * 2 * PHASE, (pair + 1) * 2 * PHASE)
        ratio = column_sum(gathered, band_ref, lanes) / drive_ref[:, lanes]
        least = jnp.minimum(ratio[:, 0:PHASE], ratio[:, PHASE:])
        low = least if low is None else jnp.minimum(low, least)
    turned = swap_groups(low.reshape(STEP_TILES * chunks, TILE_ROWS, LANES))
    for side in range(STEP_TILES):
        for chunk in range(chunks):
            out_ref[side * 8 : side * 8 + 8, chunk * LANES : (chunk + 1) * LANES] = turned[side * chunks + chunk]


def tile_call(kernel, terms, band, height, width, out_shape, out_block, more=()):
    families = band.shape[-1] // PHASE
    across = width // TILE_LANES
    tiles = height // TILE_ROWS + 2
    count = terms.shape[0]
    work = 2 * (height // TILE_ROWS) * across * band.size
    return pl.pallas_call(
        functools.partial(kernel, families),
        grid=(height // (TILE_ROWS * STEP_TILES),),
        out_shape=jax.ShapeDtypeStruct(out_shape, jnp.float32),
        in_specs=[
            pl.BlockSpec(terms.shape, lambda i: (0, 0, 0), pipeline_mode=pl.Buffered(1)),
            pl.BlockSpec(band.shape, lambda i: (0, 0, 0, 0), pipeline_mode=pl.Buffered(1)),
        ]
        + [pl.BlockSpec((STEP_TILES * across, cells.shape[1]), lambda i: (i, 0)) for cells in more],
        out_specs=pl.BlockSpec(out_block, lambda i: (i, 0)),
        scratch_shapes=[
            pltpu.VMEM((2, across + GROUPS, LANES), jnp.float32),
            pltpu.VMEM((count, tiles, across, 2 * PHASE), jnp.bfloat16),
        ],
        compiler_params=pltpu.CompilerParams(vmem_limit_bytes=56 << 20),
        cost_estimate=pl.CostEstimate(flops=work, bytes_accessed=16 << 20, transcendentals=0),
    )(terms, band, *more)


def extended(cells, sides, width):
    for axis, dim in sides:
        ends = lax.axis_size(axis) - 1
        head = lax.slice_in_dim(cells, 0, width, axis=dim)
        tail = lax.slice_in_dim(cells, cells.shape[dim] - width, cells.shape[dim], axis=dim)
        before = lax.ppermute(tail, axis, [(i, i + 1) for i in range(ends)])
        after = lax.ppermute(head, axis, [(i + 1, i) for i in range(ends)])
        cells = jnp.concatenate([before, cells, after], axis=dim)
    return cells


def band_weights(headings, extents):
    shape = (3, 2, TILE_ROWS, TILE_LANES, TILE_ROWS, TILE_LANES)
    index = [lax.broadcasted_iota(jnp.int32, shape, axis) for axis in range(6)]
    offset_v = TILE_ROWS * index[0] + index[2] - R - index[4]
    offset_u = TILE_LANES * index[1] + index[3] - R - index[5]
    keep = (jnp.abs(offset_v) <= R) & (jnp.abs(offset_u) <= R)
    rows = 3 * 2 * PHASE

    def flat(cells):
        return cells.reshape(rows, 1, PHASE)

    heights, shares = ellipsoid(
        flat(offset_u.astype(jnp.float32)),
        flat(offset_v.astype(jnp.float32)),
        headings[None, :, None],
        extents[None, :, None],
    )
    keep = flat(keep)
    count = headings.shape[0]

    def whole(cells):
        return jnp.where(keep, cells, 0.0).astype(jnp.bfloat16).reshape(3, 2 * PHASE, count * PHASE)

    heights = whole(heights)
    return jnp.stack([whole(shares), heights])


def pick_tiles(library, index):
    def copy_kernel(index_ref, in_ref, out_ref):
        out_ref[...] = in_ref[...]

    block = (1,) + library.shape[1:]
    flat = index.reshape(-1)
    picked = pl.pallas_call(
        copy_kernel,
        out_shape=jax.ShapeDtypeStruct(flat.shape + library.shape[1:], library.dtype),
        grid_spec=pltpu.PrefetchScalarGridSpec(
            num_scalar_prefetch=1,
            grid=flat.shape,
            in_specs=[pl.BlockSpec(block, lambda i, index_ref: (index_ref[i], 0, 0))],
            out_specs=pl.BlockSpec(block, lambda i, index_ref: (i, 0, 0)),
        ),
    )(flat, library)
    return picked.reshape(index.shape + library.shape[1:])


def body(noise, elevation_library, tile_choice_index, family_heading_index, family_extent_index):
    side_cells = noise.shape[2]
    row_count = lax.axis_size("row")
    col_count = lax.axis_size("col")
    split = lax.axis_size("orient")
    row, col, side = (lax.axis_index(axis) for axis in ("row", "col", "orient"))
    devices = row_count * col_count * split
    lines = noise.shape[1] // split
    window_rows = side_cells // row_count
    window_columns = side_cells // (col_count * split)

    families = jnp.stack([family_heading_index, family_extent_index])
    held_families = [families]
    for turn in range(1, split):
        pairs = [(i, (i + turn) % split) for i in range(split)]
        held_families.append(lax.ppermute(families, "orient", pairs))
    families = jnp.concatenate(held_families, axis=1)
    choices = extended(tile_choice_index, (("row", 0), ("col", 1)), 1)

    own = lax.dynamic_slice_in_dim(noise, side * lines, lines, 1)
    first_line = lax.axis_index(("row", "col", "orient")) * lines
    v_index = first_line + lax.broadcasted_iota(jnp.int32, (lines, side_cells), 0)
    u_index = lax.broadcasted_iota(jnp.int32, (lines, side_cells), 1)
    weights = own * amplitude(u_index, v_index, side_cells)[None]
    spectrum = transform(weights, False, lines, side_cells, devices, 0)
    spectrum, choices, families = lax.optimization_barrier((spectrum, choices, families))
    held = lax.all_to_all(spectrum, ("row", "col", "orient"), split_axis=0, concat_axis=0, tiled=True)
    tall = window_columns + 2 * R
    wide = (window_rows // LANES + 1) * LANES
    spare = wide - window_rows - 2 * R
    tile_side = elevation_library.shape[1]
    tiles_x = window_rows // tile_side
    tiles_y = window_columns // tile_side
    first_y = col * split + side
    local = lax.dynamic_slice_in_dim(choices, side * tiles_y, tiles_y + 2, 1)
    slope = pick_tiles(elevation_library.transpose(0, 2, 1), local.T)
    slope = slope.transpose(0, 2, 1, 3).reshape((tiles_y + 2) * tile_side, (tiles_x + 2) * tile_side)
    edge = tile_side - R
    slope = slope[edge : edge + tall, edge : edge + wide]
    y = first_y * window_columns - R + lax.broadcasted_iota(jnp.int32, (tall, wide), 0)
    x = row * window_rows - R + lax.broadcasted_iota(jnp.int32, (tall, wide), 1)
    inside = (y >= 0) & (y < side_cells) & (x >= 0) & (x < side_cells)
    secant = jnp.sqrt(1.0 + slope * slope)
    lift = jnp.where(inside, 0.5 * secant, 0.0)
    grip = jnp.where(inside, 0.6 / secant, 0.0)
    drive = jnp.where(inside, slope / secant, 0.0).astype(jnp.bfloat16)
    band = band_weights(families[0], families[1])
    held, lift, grip, drive = lax.optimization_barrier((held, lift, grip, drive))
    positions = side_cells // devices
    per_block = LANES // lines
    held = held.reshape(side_cells // LANES, per_block, 2, positions, lines)
    held = held.transpose(0, 2, 3, 1, 4).reshape(side_cells // LANES, 2, positions, LANES)
    fields = transform(held, True, positions, side_cells, col_count * split, R)
    fields = lax.all_to_all(fields, ("col", "orient"), split_axis=0, concat_axis=0, tiled=True)
    across = window_rows // TILE_LANES
    driving = tile_call(
        driving_kernel,
        drive[None],
        band[1:],
        window_columns,
        window_rows,
        (window_columns // TILE_ROWS * across, band.shape[-1]),
        (STEP_TILES * across, band.shape[-1]),
    )
    fields, driving, band = lax.optimization_barrier((fields, driving, band))
    fields = fields.transpose(1, 2, 0, 3).reshape(2, tall, window_rows)
    ends = row_count - 1
    before = lax.ppermute(fields[:, :, window_rows - R :], "row", [(i, i + 1) for i in range(ends)])
    after = lax.ppermute(fields[:, :, :R], "row", [(i + 1, i) for i in range(ends)])
    fields = jnp.concatenate(
        [before, fields, after, jnp.zeros((2, tall, spare), fields.dtype)], axis=2
    ).astype(jnp.float32)

    cohesion = (jnp.exp(0.4 * fields[0]) * lift).astype(jnp.bfloat16)
    friction = (jnp.exp(0.25 * fields[1]) * grip).astype(jnp.bfloat16)
    safety = tile_call(
        stability_kernel,
        jnp.stack([cohesion, friction]),
        band,
        window_columns,
        window_rows,
        (window_columns, window_rows),
        (TILE_ROWS * STEP_TILES, window_rows),
        (driving,),
    )
    return safety.T


TURNED = (((1,), (1,)), ((), ()))
DOT = functools.partial(lax.dot_general, dimension_numbers=TURNED, preferred_element_type=jnp.float32)
MESH = pl.DeviceIdType.MESH
CHUNK = 32
CHUNKS = LANES // CHUNK
SPLIT = 6
TERM = 6 * LANES


def strip_of(row, col, side, cols):
    return row * (2 * cols) + col + side * (2 * cols - 1 - 2 * col)


def place_of(strip, cols):
    row = strip // (2 * cols)
    at = strip % (2 * cols)
    side = at // cols
    return row, at + side * (2 * cols - 1 - 2 * at), side


def tables(length):
    outer = length // LANES
    q = np.arange(LANES)
    turns = []
    for shift in (R, 0):
        turn = 2 * np.pi * (np.arange(outer)[:, None] - shift) * q / length
        turns += [np.cos(turn), np.sin(turn)]
    angle = 2 * np.pi * (q[:, None] * q % LANES) / LANES
    table = np.block([[np.cos(angle), np.sin(angle)], [-np.sin(angle), np.cos(angle)]]).astype(np.float32)
    big = table.astype(jnp.bfloat16)
    small = (table - big.astype(np.float32)).astype(jnp.bfloat16)
    u = np.arange(length)
    wrapped = np.minimum(u, length - u) / (length / cutoff_ratio)
    turns.append((wrapped * wrapped).reshape(outer, LANES))
    return np.stack(turns).astype(np.float32), np.concatenate([big, big, small], axis=1)


def swap8(cells):
    cells = [pltpu.roll(c, TILE_LANES * i, 1) if i else c for i, c in enumerate(cells)]
    group = lax.broadcasted_iota(jnp.int32, cells[0].shape, 1) // TILE_LANES
    for bit in (1, 2, 4):
        pick = (group & bit) != 0
        cells = [jnp.where(pick, cells[(i + bit) % GROUPS], cells[i]) for i in range(GROUPS)]
    out = []
    for i in range(GROUPS):
        c = cells[-i % GROUPS]
        out.append(pltpu.roll(c, LANES - TILE_LANES * i, 1) if i else c)
    return out


def pair_dot(wide, first, second):
    value = jnp.concatenate([first, second], axis=0)
    high = value.astype(jnp.bfloat16)
    rest = (value - high.astype(jnp.float32)).astype(jnp.bfloat16)
    return DOT(wide, jnp.concatenate([high, rest, high], axis=1))


def spread(into, base, a, g, at, value):
    for shift in range(3):
        to = a + 1 - shift
        if 0 <= to < 4:
            spot(into, base, to, g, at, shift, value)


def spot(into, base, to, g, at, shift, value):
    first = base + shift * 2 * LANES
    if g < GROUPS:
        into[to, g, at, first : first + LANES] = value
    if g > 0:
        into[to, g - 1, at, first + LANES : first + 2 * LANES] = value


def band_rows(family_ref, band, side):
    params = []
    for owner in range(2):
        both = family_ref[owner].astype(jnp.float32)
        heading = both[0:4] * (math.pi / N_AZ)
        semi_axis = R * (both[4:8] + (1 + NSIZE)) / (2 * NSIZE)
        params.append((jnp.cos(heading), jnp.sin(heading), 1.0 / semi_axis, 1.0 / (0.6 * semi_axis), 0.3 * semi_axis))
    shape = (16, LANES)
    lane = lax.broadcasted_iota(jnp.int32, shape, 1)
    row = lax.broadcasted_iota(jnp.int32, shape, 0)

    @pl.loop(0, TERM // 16)
    def _(block):
        offset_v = TILE_ROWS * (block // 16) + block % 8 - R - lane // TILE_LANES
        offset_u = TILE_LANES * (block // 8 % 2) - R + row - lane % TILE_LANES
        keep = (jnp.abs(offset_v) <= R) & (jnp.abs(offset_u) <= R)
        v = offset_v.astype(jnp.float32)
        u = offset_u.astype(jnp.float32)
        at = pl.multiple_of(block * 16, 16)
        for family in range(8):
            cos, sin, per_semi, per_across, slip_depth = [p[family % 4 : family % 4 + 1] for p in params[family // 4]]
            along = (u * cos + v * sin) * per_semi
            lateral = (v * cos - u * sin) * per_across
            inside = 1.0 - along * along - lateral * lateral
            height = slip_depth * jnp.sqrt(jnp.maximum(inside, 0.0))
            share = jnp.clip(4.0 * inside, 0.0, 1.0)
            lanes = slice(family * LANES, (family + 1) * LANES)
            band[pl.ds(at, 16), lanes] = jnp.where(keep, share, 0.0).astype(jnp.bfloat16)
            band[pl.ds(at + TERM, 16), lanes] = jnp.where(keep, height, 0.0).astype(jnp.bfloat16)


def whole_kernel(
    sizes, noise_any, choice_any, heading_any, extent_any, lib_any, turn_any, wide_any,
    out_any,
    mid, full, send_a, send_b, held_a, held_b, lift, grip, gathered, inv, band, edge, edge_send, halo_out, halo_in,
    natural, staged, factor, code_in, scale_in, done, library, choice_in, family_in, choice_smem, choice_ref, heading_ref, extent_ref, turn_ref, wide_ref,
    noise_sem, first_send, first_recv, choice_send, choice_recv, family_send, family_recv, smem_sem,
    halo_send, halo_recv, out_send, out_recv, scale_send, scale_recv, library_sem, done_sem, entry_sem,
):
    row_count, cols = sizes
    row, col, side = (lax.axis_index(axis) for axis in ("row", "col", "orient"))
    devices = row_count * cols * 2
    group = cols * 2
    me = (row * cols + col) * 2 + side
    strip = strip_of(row, col, side, cols)
    mine = strip % group
    block_here = col * 2 + side
    plane = row * cols + col
    left = place_of(lax.rem(strip + devices - 1, devices), cols)
    outer = turn_any.shape[1]

    def device(index):
        return index // group, index % group // 2, index % 2

    def owner(block):
        return row, block // 2, block % 2

    barrier = pltpu.get_barrier_semaphore()

    @pl.loop(1, devices)
    def _(k):
        pl.semaphore_signal(barrier, inc=1, device_id=device(lax.rem(me + k, devices)), device_id_type=MESH)

    def noise_copy(chunk, part, piece):
        lines = pl.ds(pl.multiple_of(side * LANES + chunk * CHUNK, CHUNK), CHUNK)
        return pltpu.make_async_copy(
            noise_any.at[part, lines, piece * 1024 : (piece + 1) * 1024],
            inv.at[0, part * 2 + piece // 2, piece % 2 * 4 + chunk],
            noise_sem.at[chunk, part * 4 + piece],
        )

    entries = [(turn_any, turn_ref), (choice_any, choice_ref), (heading_any, heading_ref), (extent_any, extent_ref)]
    entries = [pltpu.make_async_copy(a, b, entry_sem.at[i]) for i, (a, b) in enumerate(entries + [(wide_any, wide_ref)])]
    entries[0].start()
    for chunk in range(CHUNKS):
        for part in range(2):
            for piece in range(4):
                noise_copy(chunk, part, piece).start()

    for entry in entries[1:]:
        entry.start()
    library_copy = pltpu.make_async_copy(lib_any, library, library_sem)
    library_copy.start()
    entries[0].wait()
    for chunk in range(CHUNKS):
        for part in range(2):
            for piece in range(4):
                noise_copy(chunk, part, piece).wait()

        @pl.loop(0, CHUNK // 8)
        def _(block):
            at = pl.ds(pl.multiple_of(block * 8, 8), 8)
            line = me * LANES + chunk * CHUNK + block * 8 + lax.broadcasted_iota(jnp.int32, (8, LANES), 0)
            wrap_v = jnp.minimum(line, outer * LANES - line).astype(jnp.float32) * (cutoff_ratio / (outer * LANES))
            base = 1.0 + wrap_v * wrap_v
            parts = []
            for p in range(outer):
                root = lax.rsqrt(base + turn_ref[4, p : p + 1, :])
                spectrum = nugget_share + peak_share * (root * root * root)
                level = spectrum * lax.rsqrt(spectrum) * (1.0 / (outer * LANES))
                spot_at = (p // 16, p // 8 % 2 * 4 + chunk, at, slice(p % 8 * LANES, (p % 8 + 1) * LANES))
                parts.append((inv[(0,) + spot_at] * level, inv[(0, 2 + spot_at[0]) + spot_at[1:]] * level))
            turned = small_dft(parts)
            rows = pl.ds(pl.multiple_of(chunk * CHUNK + block * 8, 8), 8)
            for k in range(outer):
                re, im = turned[(k - R) % outer]
                cos = turn_ref[0, k : k + 1, :]
                sin = turn_ref[1, k : k + 1, :]
                mid[k, rows, 0:LANES] = re * cos + im * sin
                mid[k, rows, LANES : 2 * LANES] = im * cos - re * sin

    for entry in entries[1:]:
        entry.wait()
    choice_in[plane] = jnp.zeros((8, LANES), jnp.int32)
    choice_in[plane, 0:4, 0:16] = choice_ref[...]
    which = lax.broadcasted_iota(jnp.int32, (8, LANES), 0)
    mixed = jnp.zeros((8, LANES), jnp.int32)
    for f in range(4):
        mixed = jnp.where(which == f, heading_ref[f], mixed)
        mixed = jnp.where(which == f + 4, extent_ref[f], mixed)
    family_in[side] = mixed
    pl.semaphore_wait(barrier, devices - 1)

    def choice_copy(k):
        to = lax.rem(plane + k, row_count * cols)
        return pltpu.make_async_remote_copy(
            src_ref=choice_in.at[plane], dst_ref=choice_in.at[plane],
            send_sem=choice_send.at[k], recv_sem=choice_recv.at[k],
            device_id=(to // cols, to % cols, side), device_id_type=MESH,
        )

    def family_copy():
        return pltpu.make_async_remote_copy(
            src_ref=family_in.at[side], dst_ref=family_in.at[side], send_sem=family_send, recv_sem=family_recv,
            device_id=(row, col, 1 - side), device_id_type=MESH,
        )

    @pl.loop(1, row_count * cols)
    def _(k):
        choice_copy(k).start()

    family_copy().start()

    for k in range(0, outer, 2):
        got = pair_dot(wide_ref[...], mid[k], mid[k + 1])
        for part in range(2):
            for one in range(2):
                piece = got[part * LANES : (part + 1) * LANES, one * LANES : (one + 1) * LANES]
                full[part, pl.ds(k + one, LANES, stride=outer), :] = piece

    parts_of = ((0, SPLIT, send_a, held_a), (SPLIT, GROUPS, send_b, held_b))

    def partner(k):
        return me ^ (k % 2 * 8 + k // 2 % 8 + k // 16 * 16)

    def first_copy(c, k):
        to = partner(k)
        return pltpu.make_async_remote_copy(
            src_ref=parts_of[c][2].at[to], dst_ref=parts_of[c][3].at[me],
            send_sem=first_send.at[c, k], recv_sem=first_recv.at[c, k],
            device_id=device(to), device_id_type=MESH,
        )

    for c, (low_g, high_g, send, held) in enumerate(parts_of):
        count = (high_g - low_g) * 16

        def packed(to, into):
            to_strip = strip_of(*device(to), cols)
            at = pl.ds(pl.multiple_of(to_strip * LANES + low_g * 16, 16), count)
            for part in range(2):
                into[to, part] = full[part, at, :].astype(jnp.bfloat16)

        @pl.loop(1, devices)
        def _(k):
            packed(partner(k), send)
            first_copy(c, k).start()

        packed(me, held)

    family_copy().wait()
    band_rows(family_in, band, side)

    @pl.loop(1, row_count * cols)
    def _(k):
        choice_copy(k).wait()

    to_smem = pltpu.make_async_copy(choice_in, choice_smem, smem_sem)
    to_smem.start()
    to_smem.wait()
    library_copy.wait()

    @pl.loop(0, library.shape[0])
    def _(t):
        library[t] = pltpu.roll(library[t].T, R, 1)

    left_lanes = lax.broadcasted_iota(jnp.int32, (LANES, LANES), 1) < R

    def tile(shift, t):
        x = lax.rem(strip + devices + shift, devices)
        return library[choice_smem[x // 16 * cols + t // 4, t % 4, x % 16]]

    @pl.loop(0, outer)
    def _(t):
        at = pl.ds(pl.multiple_of(t * LANES, LANES), LANES)
        here = tile(0, t)
        full[0, at, :] = jnp.where(left_lanes, tile(-1, t), here)
        full[1, at, :] = jnp.where(left_lanes, here, tile(1, t))

    half = lax.broadcasted_iota(jnp.int32, (16, LANES), 1) % TILE_LANES < R
    first = strip == 0
    last = strip == devices - 1
    for side_rows in (slice(0, 8), slice(8 + LANES, 16 + LANES)):
        edge[:, :, side_rows, :] = jnp.zeros((2, GROUPS + 1, 8, LANES), jnp.float32)
        edge_send[:, side_rows, :] = jnp.zeros((2, 8, LANES), jnp.float32)

    for a in range(4):
        @pl.loop(0, 8)
        def _(c):
            at = pl.ds(pl.multiple_of(c * 16, 16), 16)
            for source in range(2):
                turned = swap8([full[source, pl.ds(c * 512 + 8 * a + r, 16, stride=32), :] for r in range(8)])
                for g in range(GROUPS) if source == 0 else (0,):
                    slope = turned[g]
                    square = 1.0 + slope * slope
                    inverse = lax.rsqrt(square)
                    drive = slope * inverse
                    tile_at = g
                    if source == 0:
                        lift[a, g, at, :] = 0.5 * square * inverse
                        grip[a, g, at, :] = 0.6 * inverse
                        if g == 0:
                            drive = jnp.where(half & first, 0.0, drive)
                    else:
                        tile_at = GROUPS
                        drive = jnp.where(last & ~half, 0.0, drive)
                    spread(gathered, TERM, a, tile_at, at, drive.astype(jnp.bfloat16))
                    if a in (0, 3):
                        edge[0, tile_at, pl.ds(pl.multiple_of(c * 16 + 8, 8), 16), :] = drive

        if a in (0, 3):
            @pl.loop(0, 8)
            def _(c):
                at = pl.ds(pl.multiple_of(c * 16, 16), 16)
                for g in range(GROUPS + 1):
                    value = edge[0, g, pl.ds(c * 16 + (9 if a == 0 else 7), 16), :].astype(jnp.bfloat16)
                    spot(gathered, TERM, 3 - a, g, at, 2 if a == 0 else 0, value)

    pairs = band.shape[1] // (2 * PHASE)

    @pl.loop(0, CHUNKS)
    def _(chunk):
        at = pl.ds(pl.multiple_of(chunk * CHUNK, CHUNK), CHUNK)
        cells = gathered[:, :, at, TERM:].reshape(4 * GROUPS * CHUNK, TERM)
        for pair in range(pairs):
            lanes = slice(pair * 2 * PHASE, (pair + 1) * 2 * PHASE)
            sums = jnp.dot(cells, band[TERM:, lanes], preferred_element_type=jnp.float32)
            inv[chunk, :, :, :, lanes] = (1.0 / sums).reshape(4, GROUPS, CHUNK, 2 * PHASE)

    def halo_copy(slot):
        return pltpu.make_async_remote_copy(
            src_ref=halo_out.at[slot], dst_ref=halo_in.at[slot],
            send_sem=halo_send.at[slot], recv_sem=halo_recv.at[slot],
            device_id=left, device_id_type=MESH,
        )

    per_chunk = CHUNK * outer // (2 * LANES)
    home = block_here // per_chunk

    def out_copy(c, block, source):
        return pltpu.make_async_remote_copy(
            src_ref=staged.at[c, block], dst_ref=code_in.at[source, c],
            send_sem=out_send.at[c, block], recv_sem=out_recv.at[c, source],
            device_id=owner(block), device_id_type=MESH,
        )

    def scale_copy(c, block, source):
        return pltpu.make_async_remote_copy(
            src_ref=factor.at[c, block // (2 * per_chunk)], dst_ref=scale_in.at[source, c],
            send_sem=scale_send.at[c, block], recv_sem=scale_recv.at[c, source],
            device_id=owner(block), device_id_type=MESH,
        )

    for c, (low_g, high_g, send, held) in enumerate(parts_of):
        @pl.loop(1, devices)
        def _(k):
            first_copy(c, k).wait()

        @pl.loop(low_g, high_g)
        def _(g):
            at = pl.ds(pl.multiple_of((g - low_g) * 16, 16), 16)
            parts = [(held[p, 0, at, :].astype(jnp.float32), held[p, 1, at, :].astype(jnp.float32)) for p in range(outer)]
            for k, (re, im) in enumerate(small_dft(parts)):
                to = slice(k % 8 * 16, (k % 8 + 1) * 16)
                cos = turn_ref[2, k : k + 1, :]
                sin = turn_ref[3, k : k + 1, :]
                mid[k // 8 * 8 + g, to, 0:LANES] = re * cos + im * sin
                mid[k // 8 * 8 + g, to, LANES : 2 * LANES] = im * cos - re * sin

        items = [(a, g) for g in range(low_g, high_g) for a in range(4)]
        for at_item in range(0, len(items), 2):
            two = items[at_item : at_item + 2]
            got = pair_dot(wide_ref[...], *[mid[a * 8 + g] for a, g in two])
            for one, (a, g) in enumerate(two):
                for term in range(2):
                    field = got[term * LANES : (term + 1) * LANES, one * LANES : (one + 1) * LANES]
                    value = jnp.exp((0.4 if term == 0 else 0.25) * field) * (lift if term == 0 else grip)[a, g]
                    if g == 0:
                        mask = lax.broadcasted_iota(jnp.int32, (LANES, LANES), 1) % TILE_LANES < R
                        sent = jnp.where(first & ~mask, 0.0, value)
                        value = jnp.where(first & mask, 0.0, value)
                        halo_out[a, term] = sent.astype(jnp.bfloat16)
                    spread(gathered, term * TERM, a, g, slice(None), value.astype(jnp.bfloat16))
                    if a in (0, 3):
                        moved = slice(9, 9 + LANES) if a == 0 else slice(7, 7 + LANES)
                        edge[term, g, 8 : 8 + LANES, :] = value
                        near = edge[term, g, moved, :].astype(jnp.bfloat16)
                        spot(gathered, term * TERM, 3 - a, g, slice(None), 2 if a == 0 else 0, near)
                        if g == 0:
                            edge_send[term, 8 : 8 + LANES, :] = sent
                            halo_out[4 if a == 0 else 5, term] = edge_send[term, moved, :].astype(jnp.bfloat16)
                if g == 0:
                    halo_copy(a).start()
                    if a in (0, 3):
                        halo_copy(4 if a == 0 else 5).start()

        if c == 1:
            for slot in range(6):
                halo_copy(slot).wait()
                for term in range(2):
                    value = halo_in[slot, term]
                    if slot < 4:
                        spread(gathered, term * TERM, slot, GROUPS, slice(None), value)
                    else:
                        to, shift = (3, 2) if slot == 4 else (0, 0)
                        spot(gathered, term * TERM, to, GROUPS, slice(None), shift, value)

        tiles = slice(c * 4, c * 4 + 4)

        @pl.loop(0, 2)
        def _(step):
            half_at = (home // 2) ^ (1 - step)
            cells = []
            for q in range(2):
                at = pl.ds(pl.multiple_of((half_at * 2 + q) * CHUNK, CHUNK), CHUNK)
                cells.append(gathered[:, tiles, at, :].reshape(16 * CHUNK, 2 * TERM))
            cells = jnp.concatenate(cells, axis=0)
            low = None
            for pair in range(pairs):
                lanes = slice(pair * 2 * PHASE, (pair + 1) * 2 * PHASE)
                ratio = jnp.dot(cells, band[:, lanes], preferred_element_type=jnp.float32)
                ratio = ratio * inv[pl.ds(half_at * 2, 2), :, tiles, :, lanes].reshape(32 * CHUNK, 2 * PHASE)
                least = jnp.minimum(ratio[:, 0:PHASE], ratio[:, PHASE:])
                low = least if low is None else jnp.minimum(low, least)
            largest = jnp.max(jnp.max(low, axis=0, keepdims=True), axis=1, keepdims=True)
            largest = jnp.broadcast_to(jnp.maximum(largest, 1e-30), (8, LANES))
            factor[c, half_at] = jnp.sqrt(largest) * (1.0 / 65535.0)
            upward = (65535.0 * lax.rsqrt(largest))[0:1, :]
            low = low.reshape(2, 4, 4, 2, CHUNK // 2, LANES)
            for q in range(2):
                for a in range(4):
                    turned = swap8([low[q, a, g % 4, g // 4] for g in range(GROUPS)])
                    for r in range(8):
                        code = jnp.sqrt(turned[r]) * upward + 0.5
                        natural[q, pl.ds(8 * a + r, CHUNK // 2, stride=32), :] = code
                for piece in range(4):
                    code = natural[q, piece * LANES : (piece + 1) * LANES, :]
                    code = (code.astype(jnp.int32) - 32768).T.astype(jnp.int16)
                    for upper in range(2):
                        block = (half_at * 2 + q) * per_chunk + upper * 2 + piece // 2
                        staged[c, block, :, piece % 2 * LANES : (piece % 2 + 1) * LANES] = code[upper * 64 : upper * 64 + 64]

            @pl.loop(0, 2 * per_chunk)
            def _(i):
                block = half_at * 2 * per_chunk + (i ^ (per_chunk * (1 - home % 2)))

                @pl.when(block != block_here)
                def _():
                    out_copy(c, block, mine).start()
                    scale_copy(c, block, mine).start()

    def done_copy(c, source):
        rows = pl.ds(pl.multiple_of(source * LANES + c * 64, 64), 64)
        return pltpu.make_async_copy(done.at[source, c], out_any.at[rows], done_sem.at[c, source])

    def finish(c, source, code, scale):
        root = (code.astype(jnp.float32) + 32768.0) * scale[0:1, 0:1]
        done[source, c] = root * root
        done_copy(c, source).start()

    for c in range(2):
        finish(c, mine, staged[c, block_here], factor[c, home // 2])

        @pl.loop(0, group)
        def _(at):
            block = (home ^ (3 - at // per_chunk)) * per_chunk + at % per_chunk
            source = strip_of(0, block // 2, block % 2, cols)

            @pl.when(block != block_here)
            def _():
                out_copy(c, block, source).wait_recv()
                scale_copy(c, block, source).wait_recv()
                finish(c, source, code_in[source, c], scale_in[source, c])

    @pl.loop(1, group)
    def _(turned):
        block = lax.rem(block_here + turned, group)
        for c in range(2):
            out_copy(c, block, mine).wait_send()
            scale_copy(c, block, mine).wait_send()

    @pl.loop(0, group)
    def _(source):
        for c in range(2):
            done_copy(c, source).wait()


def whole_safety(noise, choices, headings, extents, library, row_count, cols):
    length = noise.shape[2]
    outer = length // LANES
    group = 2 * cols
    devices = group * row_count
    turns, wide = tables(length)
    dma = pltpu.SemaphoreType.DMA
    f32, bf16 = jnp.float32, jnp.bfloat16
    early, late = SPLIT * 16, LANES - SPLIT * 16
    return pl.pallas_call(
        functools.partial(whole_kernel, (row_count, cols)),
        out_shape=jax.ShapeDtypeStruct((group * LANES, 2 * LANES), f32),
        in_specs=[pl.BlockSpec(memory_space=pl.ANY)] * 7,
        out_specs=pl.BlockSpec(memory_space=pl.ANY),
        scratch_shapes=[
            pltpu.VMEM((outer, LANES, 2 * LANES), f32),
            pltpu.VMEM((2, length, LANES), f32),
            pltpu.VMEM((devices, 2, early, LANES), bf16),
            pltpu.VMEM((devices, 2, late, LANES), bf16),
            pltpu.VMEM((devices, 2, early, LANES), bf16),
            pltpu.VMEM((devices, 2, late, LANES), bf16),
            pltpu.VMEM((4, GROUPS, LANES, LANES), f32),
            pltpu.VMEM((4, GROUPS, LANES, LANES), f32),
            pltpu.VMEM((4, GROUPS, LANES, 2 * TERM), bf16),
            pltpu.VMEM((CHUNKS, 4, GROUPS, CHUNK, 8 * PHASE), f32),
            pltpu.VMEM((2 * TERM, 8 * PHASE), bf16),
            pltpu.VMEM((2, GROUPS + 1, LANES + 16, LANES), f32),
            pltpu.VMEM((2, LANES + 16, LANES), f32),
            pltpu.VMEM((6, 2, LANES, LANES), bf16),
            pltpu.VMEM((6, 2, LANES, LANES), bf16),
            pltpu.VMEM((2, length // CHUNKS // 2, LANES), f32),
            pltpu.VMEM((2, group, LANES // 2, 2 * LANES), jnp.int16),
            pltpu.VMEM((2, 2, 8, LANES), f32),
            pltpu.VMEM((group, 2, LANES // 2, 2 * LANES), jnp.int16),
            pltpu.VMEM((group, 2, 8, LANES), f32),
            pltpu.VMEM((group, 2, LANES // 2, 2 * LANES), f32),
            pltpu.VMEM(library.shape, f32),
            pltpu.VMEM((row_count * cols, 8, LANES), jnp.int32),
            pltpu.VMEM((2, 8, LANES), jnp.int32),
            pltpu.SMEM((row_count * cols, 8, LANES), jnp.int32),
            pltpu.VMEM(choices.shape, jnp.int32),
            pltpu.SMEM(headings.shape, jnp.int32),
            pltpu.SMEM(extents.shape, jnp.int32),
            pltpu.VMEM(turns.shape, f32),
            pltpu.VMEM(wide.shape, bf16),
            dma((CHUNKS, 8)), dma((2, devices)), dma((2, devices)),
            dma((row_count * cols,)), dma((row_count * cols,)), dma, dma, dma,
            dma((6,)), dma((6,)), dma((2, group)), dma((2, group)), dma((2, group)), dma((2, group)), dma, dma((2, group)), dma((5,)),
        ],
        compiler_params=pltpu.CompilerParams(
            vmem_limit_bytes=62 << 20, collective_id=0, has_side_effects=True
        ),
    )(noise, choices, headings, extents, library, turns, wide)


def strip_body(noise, elevation_library, tile_choice_index, family_heading_index, family_extent_index):
    row_count, cols = lax.axis_size("row"), lax.axis_size("col")
    return whole_safety(
        noise, tile_choice_index.T, family_heading_index, family_extent_index, elevation_library, row_count, cols
    )


def chosen_body(noise, elevation_library, tile_choice_index, family_heading_index, family_extent_index):
    shape = (lax.axis_size("row"), lax.axis_size("col"), lax.axis_size("orient"))
    side_cells = noise.shape[2]
    fits = (
        shape == (2, 8, 2)
        and side_cells == 32 * LANES
        and elevation_library.shape[1] == LANES
        and tile_choice_index.shape == (16, 4)
        and family_heading_index.shape[0] == 4
    )
    chosen = strip_body if fits else body
    return chosen(noise, elevation_library, tile_choice_index, family_heading_index, family_extent_index)


def solution(mesh):
    placed = (P(None, ("row", "col"), None), P(), P("row", "col"), P("orient"), P("orient"))
    return jax.shard_map(
        chosen_body, mesh=mesh, in_specs=placed, out_specs=P("row", ("col", "orient")), check_vma=False
    )
```

```python
import functools
import math

import jax
import jax.numpy as jnp
import numpy as np
from jax import lax
from jax.experimental import pallas as pl
from jax.experimental.pallas import tpu as pltpu
from jax.sharding import PartitionSpec as P

R = 8
N_AZ = 36
NSIZE = 4
LANES = 128
TILE_ROWS = 8
TILE_LANES = 16
GROUPS = LANES // TILE_LANES
PHASE = TILE_ROWS * TILE_LANES
STEP_TILES = 8

nugget_share = 0.3
peak_share = 1024.0 / (2.0 * math.pi)
cutoff_ratio = 32.0


def amplitude(u_index, v_index, side_cells):
    wrap_u = jnp.minimum(u_index, side_cells - u_index).astype(jnp.float32)
    wrap_v = jnp.minimum(v_index, side_cells - v_index).astype(jnp.float32)
    cutoff = side_cells / cutoff_ratio
    scaled_u = wrap_u / cutoff
    scaled_v = wrap_v / cutoff
    grown = 1.0 + scaled_u * scaled_u + scaled_v * scaled_v
    spectrum = nugget_share + peak_share / (grown * jnp.sqrt(grown))
    return jnp.sqrt(spectrum) / side_cells


def ellipsoid(offset_u, offset_v, azimuth, size_index):
    heading = azimuth.astype(jnp.float32) * (math.pi / N_AZ)
    semi_axis = R * (size_index.astype(jnp.float32) + (1 + NSIZE)) / (2 * NSIZE)
    across = 0.6 * semi_axis
    slip_depth = 0.3 * semi_axis
    along = offset_u * jnp.cos(heading) + offset_v * jnp.sin(heading)
    lateral = offset_v * jnp.cos(heading) - offset_u * jnp.sin(heading)
    along_part = along / semi_axis
    lateral_part = lateral / across
    inside = 1.0 - along_part * along_part - lateral_part * lateral_part
    height = slip_depth * jnp.sqrt(jnp.maximum(inside, 0.0))
    base_share = jnp.clip(4.0 * inside, 0.0, 1.0)
    return (height, base_share)


def small_dft(parts):
    count = len(parts)
    if count == 1:
        return parts
    even = small_dft(parts[0::2])
    odd = small_dft(parts[1::2])
    low, high = [], []
    for k in range(count // 2):
        (a, b), (c, d) = even[k], odd[k]
        if k == 0:
            e, f = c, d
        elif 4 * k == count:
            e, f = d, -c
        else:
            cos = math.cos(2 * math.pi * k / count)
            sin = math.sin(2 * math.pi * k / count)
            e, f = c * cos + d * sin, d * cos - c * sin
        low.append((a + e, b + f))
        high.append((a - e, b - f))
    return low + high


def transform_kernel(planes, blocks, span, step, pad, in_ref, cos_ref, sin_ref, big_ref, small_ref, out_ref, mid, full):
    outer = cos_ref.shape[0]
    rows = mid.shape[1]
    unit = 16 if planes else 8

    @pl.loop(0, rows // unit)
    def _(block):
        at = pl.ds(pl.multiple_of(block * unit, unit), unit)
        parts = []
        for p in range(outer):
            if planes:
                parts.append((in_ref[p, 0, at, :].astype(jnp.float32), in_ref[p, 1, at, :].astype(jnp.float32)))
            else:
                lanes = slice(p * LANES, (p + 1) * LANES)
                parts.append((in_ref[0, at, lanes], in_ref[1, at, lanes]))
        for k, (re, im) in enumerate(small_dft(parts)):
            cos = cos_ref[k : k + 1, :]
            sin = sin_ref[k : k + 1, :]
            mid[k, at, 0:LANES] = re * cos + im * sin
            mid[k, at, LANES : 2 * LANES] = im * cos - re * sin

    if pad:
        edge = jnp.zeros((pad, rows), jnp.float32)
        for part in range(2):
            full[part, 0:pad, :] = edge
            full[part, pad + outer * LANES : 2 * pad + outer * LANES, :] = edge

    turned = (((1,), (1,)), ((), ()))
    dot = functools.partial(lax.dot_general, dimension_numbers=turned, preferred_element_type=jnp.float32)
    for k in range(outer):
        value = mid[k]
        high = value.astype(jnp.bfloat16)
        rest = (value - high.astype(jnp.float32)).astype(jnp.bfloat16)
        got = dot(big_ref[...], high) + dot(big_ref[...], rest) + dot(small_ref[...], high)
        full[0, pl.ds(pad + k, LANES, stride=outer), :] = got[0:LANES]
        full[1, pl.ds(pad + k, LANES, stride=outer), :] = got[LANES : 2 * LANES]

    @pl.loop(0, blocks)
    def _(block):
        at = pl.ds(pl.multiple_of(block * step, 8), span)
        for part in range(2):
            out_ref[block, part] = full[part, at, :].astype(jnp.bfloat16)


def transform(cells, planes, rows, length, blocks, pad):
    outer = length // LANES
    step = length // blocks
    span = step + 2 * pad
    k = np.arange(outer)[:, None]
    q = np.arange(LANES)
    turn = 2 * np.pi * k * q / length
    cos, sin = np.cos(turn).astype(np.float32), np.sin(turn).astype(np.float32)
    angle = 2 * np.pi * (q[:, None] * q % LANES) / LANES
    table = np.block([[np.cos(angle), np.sin(angle)], [-np.sin(angle), np.cos(angle)]]).astype(np.float32)
    big = table.astype(jnp.bfloat16)
    small = (table - big.astype(np.float32)).astype(jnp.bfloat16)
    vmem = pl.BlockSpec(memory_space=pltpu.VMEM)
    return pl.pallas_call(
        functools.partial(transform_kernel, planes, blocks, span, step, pad),
        out_shape=jax.ShapeDtypeStruct((blocks, 2, span, rows), jnp.bfloat16),
        in_specs=[vmem] * 5,
        out_specs=vmem,
        scratch_shapes=[
            pltpu.VMEM((outer, rows, 2 * LANES), jnp.float32),
            pltpu.VMEM((2, length + 2 * pad, rows), jnp.float32),
        ],
        compiler_params=pltpu.CompilerParams(vmem_limit_bytes=40 << 20),
    )(cells, cos, sin, big, small)


def swap_groups(cells):
    row = lax.broadcasted_iota(jnp.int32, cells.shape, 1)
    group = lax.broadcasted_iota(jnp.int32, cells.shape, 2) // TILE_LANES
    skewed = pltpu.roll(cells, 0, 2, stride=TILE_LANES, stride_axis=1)
    picked = jnp.take_along_axis(skewed, (group + row - 7) & 7, axis=1)
    level = pltpu.roll(picked, TILE_LANES, 2, stride=TILE_LANES, stride_axis=1)
    return jnp.take_along_axis(level, 7 - row, axis=1)


def gather_tiles(term_ref, swapped, gathered):
    tiles, across = gathered.shape[1:3]
    chunks = across // GROUPS

    @pl.when(pl.program_id(0) == 0)
    def _():
        @pl.loop(0, tiles // 2)
        def _(pair):
            at = pl.ds(pl.multiple_of(pair * 16, 16), 16)
            both = pl.ds(pair * 2, 2)
            for term in range(gathered.shape[0]):
                for chunk in range(chunks + 1):
                    cells = term_ref[term, at, chunk * LANES : (chunk + 1) * LANES].astype(jnp.float32)
                    turned = swap_groups(cells.reshape(2, TILE_ROWS, LANES))
                    swapped[:, chunk * GROUPS : (chunk + 1) * GROUPS, :] = turned
                gathered[term, both, :, 0:PHASE] = swapped[:, 0:across, :].astype(jnp.bfloat16)
                gathered[term, both, :, PHASE:] = swapped[:, 1 : across + 1, :].astype(jnp.bfloat16)


def column_sum(gathered, band_ref, lanes):
    terms, _, across, depth = gathered.shape
    tile = pl.program_id(0) * STEP_TILES
    pieces = [(term, shift) for term in range(terms) for shift in range(3)]
    left = [gathered[term, pl.ds(tile + shift, STEP_TILES)] for term, shift in pieces]
    left = [piece.reshape(STEP_TILES * across, depth) for piece in left]
    right = [band_ref[term, shift, :, lanes] for term, shift in pieces]
    return jnp.dot(
        jnp.concatenate(left, axis=1),
        jnp.concatenate(right, axis=0),
        preferred_element_type=jnp.float32,
    )


def driving_kernel(families, term_ref, band_ref, out_ref, swapped, gathered):
    gather_tiles(term_ref, swapped, gathered)
    for pair in range(families // 2):
        lanes = slice(pair * 2 * PHASE, (pair + 1) * 2 * PHASE)
        out_ref[:, lanes] = column_sum(gathered, band_ref, lanes)


def stability_kernel(families, term_ref, band_ref, drive_ref, out_ref, swapped, gathered):
    chunks = gathered.shape[2] // GROUPS
    gather_tiles(term_ref, swapped, gathered)
    low = None
    for pair in range(families // 2):
        lanes = slice(pair * 2 * PHASE, (pair + 1) * 2 * PHASE)
        ratio = column_sum(gathered, band_ref, lanes) / drive_ref[:, lanes]
        least = jnp.minimum(ratio[:, 0:PHASE], ratio[:, PHASE:])
        low = least if low is None else jnp.minimum(low, least)
    turned = swap_groups(low.reshape(STEP_TILES * chunks, TILE_ROWS, LANES))
    for side in range(STEP_TILES):
        for chunk in range(chunks):
            out_ref[side * 8 : side * 8 + 8, chunk * LANES : (chunk + 1) * LANES] = turned[side * chunks + chunk]


def tile_call(kernel, terms, band, height, width, out_shape, out_block, more=()):
    families = band.shape[-1] // PHASE
    across = width // TILE_LANES
    tiles = height // TILE_ROWS + 2
    count = terms.shape[0]
    work = 2 * (height // TILE_ROWS) * across * band.size
    return pl.pallas_call(
        functools.partial(kernel, families),
        grid=(height // (TILE_ROWS * STEP_TILES),),
        out_shape=jax.ShapeDtypeStruct(out_shape, jnp.float32),
        in_specs=[
            pl.BlockSpec(terms.shape, lambda i: (0, 0, 0), pipeline_mode=pl.Buffered(1)),
            pl.BlockSpec(band.shape, lambda i: (0, 0, 0, 0), pipeline_mode=pl.Buffered(1)),
        ]
        + [pl.BlockSpec((STEP_TILES * across, cells.shape[1]), lambda i: (i, 0)) for cells in more],
        out_specs=pl.BlockSpec(out_block, lambda i: (i, 0)),
        scratch_shapes=[
            pltpu.VMEM((2, across + GROUPS, LANES), jnp.float32),
            pltpu.VMEM((count, tiles, across, 2 * PHASE), jnp.bfloat16),
        ],
        compiler_params=pltpu.CompilerParams(vmem_limit_bytes=56 << 20),
        cost_estimate=pl.CostEstimate(flops=work, bytes_accessed=16 << 20, transcendentals=0),
    )(terms, band, *more)


def extended(cells, sides, width):
    for axis, dim in sides:
        ends = lax.axis_size(axis) - 1
        head = lax.slice_in_dim(cells, 0, width, axis=dim)
        tail = lax.slice_in_dim(cells, cells.shape[dim] - width, cells.shape[dim], axis=dim)
        before = lax.ppermute(tail, axis, [(i, i + 1) for i in range(ends)])
        after = lax.ppermute(head, axis, [(i + 1, i) for i in range(ends)])
        cells = jnp.concatenate([before, cells, after], axis=dim)
    return cells


def band_weights(headings, extents):
    shape = (3, 2, TILE_ROWS, TILE_LANES, TILE_ROWS, TILE_LANES)
    index = [lax.broadcasted_iota(jnp.int32, shape, axis) for axis in range(6)]
    offset_v = TILE_ROWS * index[0] + index[2] - R - index[4]
    offset_u = TILE_LANES * index[1] + index[3] - R - index[5]
    keep = (jnp.abs(offset_v) <= R) & (jnp.abs(offset_u) <= R)
    rows = 3 * 2 * PHASE

    def flat(cells):
        return cells.reshape(rows, 1, PHASE)

    heights, shares = ellipsoid(
        flat(offset_u.astype(jnp.float32)),
        flat(offset_v.astype(jnp.float32)),
        headings[None, :, None],
        extents[None, :, None],
    )
    keep = flat(keep)
    count = headings.shape[0]

    def whole(cells):
        return jnp.where(keep, cells, 0.0).astype(jnp.bfloat16).reshape(3, 2 * PHASE, count * PHASE)

    heights = whole(heights)
    return jnp.stack([whole(shares), heights])


def pick_tiles(library, index):
    def copy_kernel(index_ref, in_ref, out_ref):
        out_ref[...] = in_ref[...]

    block = (1,) + library.shape[1:]
    flat = index.reshape(-1)
    picked = pl.pallas_call(
        copy_kernel,
        out_shape=jax.ShapeDtypeStruct(flat.shape + library.shape[1:], library.dtype),
        grid_spec=pltpu.PrefetchScalarGridSpec(
            num_scalar_prefetch=1,
            grid=flat.shape,
            in_specs=[pl.BlockSpec(block, lambda i, index_ref: (index_ref[i], 0, 0))],
            out_specs=pl.BlockSpec(block, lambda i, index_ref: (i, 0, 0)),
        ),
    )(flat, library)
    return picked.reshape(index.shape + library.shape[1:])


def body(noise, elevation_library, tile_choice_index, family_heading_index, family_extent_index):
    side_cells = noise.shape[2]
    row_count = lax.axis_size("row")
    col_count = lax.axis_size("col")
    split = lax.axis_size("orient")
    row, col, side = (lax.axis_index(axis) for axis in ("row", "col", "orient"))
    devices = row_count * col_count * split
    lines = noise.shape[1] // split
    window_rows = side_cells // row_count
    window_columns = side_cells // (col_count * split)

    families = jnp.stack([family_heading_index, family_extent_index])
    held_families = [families]
    for turn in range(1, split):
        pairs = [(i, (i + turn) % split) for i in range(split)]
        held_families.append(lax.ppermute(families, "orient", pairs))
    families = jnp.concatenate(held_families, axis=1)
    choices = extended(tile_choice_index, (("row", 0), ("col", 1)), 1)

    own = lax.dynamic_slice_in_dim(noise, side * lines, lines, 1)
    first_line = lax.axis_index(("row", "col", "orient")) * lines
    v_index = first_line + lax.broadcasted_iota(jnp.int32, (lines, side_cells), 0)
    u_index = lax.broadcasted_iota(jnp.int32, (lines, side_cells), 1)
    weights = own * amplitude(u_index, v_index, side_cells)[None]
    spectrum = transform(weights, False, lines, side_cells, devices, 0)
    spectrum, choices, families = lax.optimization_barrier((spectrum, choices, families))
    held = lax.all_to_all(spectrum, ("row", "col", "orient"), split_axis=0, concat_axis=0, tiled=True)
    tall = window_columns + 2 * R
    wide = (window_rows // LANES + 1) * LANES
    spare = wide - window_rows - 2 * R
    tile_side = elevation_library.shape[1]
    tiles_x = window_rows // tile_side
    tiles_y = window_columns // tile_side
    first_y = col * split + side
    local = lax.dynamic_slice_in_dim(choices, side * tiles_y, tiles_y + 2, 1)
    slope = pick_tiles(elevation_library.transpose(0, 2, 1), local.T)
    slope = slope.transpose(0, 2, 1, 3).reshape((tiles_y + 2) * tile_side, (tiles_x + 2) * tile_side)
    edge = tile_side - R
    slope = slope[edge : edge + tall, edge : edge + wide]
    y = first_y * window_columns - R + lax.broadcasted_iota(jnp.int32, (tall, wide), 0)
    x = row * window_rows - R + lax.broadcasted_iota(jnp.int32, (tall, wide), 1)
    inside = (y >= 0) & (y < side_cells) & (x >= 0) & (x < side_cells)
    secant = jnp.sqrt(1.0 + slope * slope)
    lift = jnp.where(inside, 0.5 * secant, 0.0)
    grip = jnp.where(inside, 0.6 / secant, 0.0)
    drive = jnp.where(inside, slope / secant, 0.0).astype(jnp.bfloat16)
    band = band_weights(families[0], families[1])
    held, lift, grip, drive = lax.optimization_barrier((held, lift, grip, drive))
    positions = side_cells // devices
    per_block = LANES // lines
    held = held.reshape(side_cells // LANES, per_block, 2, positions, lines)
    held = held.transpose(0, 2, 3, 1, 4).reshape(side_cells // LANES, 2, positions, LANES)
    fields = transform(held, True, positions, side_cells, col_count * split, R)
    fields = lax.all_to_all(fields, ("col", "orient"), split_axis=0, concat_axis=0, tiled=True)
    across = window_rows // TILE_LANES
    driving = tile_call(
        driving_kernel,
        drive[None],
        band[1:],
        window_columns,
        window_rows,
        (window_columns // TILE_ROWS * across, band.shape[-1]),
        (STEP_TILES * across, band.shape[-1]),
    )
    fields, driving, band = lax.optimization_barrier((fields, driving, band))
    fields = fields.transpose(1, 2, 0, 3).reshape(2, tall, window_rows)
    ends = row_count - 1
    before = lax.ppermute(fields[:, :, window_rows - R :], "row", [(i, i + 1) for i in range(ends)])
    after = lax.ppermute(fields[:, :, :R], "row", [(i + 1, i) for i in range(ends)])
    fields = jnp.concatenate(
        [before, fields, after, jnp.zeros((2, tall, spare), fields.dtype)], axis=2
    ).astype(jnp.float32)

    cohesion = (jnp.exp(0.4 * fields[0]) * lift).astype(jnp.bfloat16)
    friction = (jnp.exp(0.25 * fields[1]) * grip).astype(jnp.bfloat16)
    safety = tile_call(
        stability_kernel,
        jnp.stack([cohesion, friction]),
        band,
        window_columns,
        window_rows,
        (window_columns, window_rows),
        (TILE_ROWS * STEP_TILES, window_rows),
        (driving,),
    )
    return safety.T


TURNED = (((1,), (1,)), ((), ()))
DOT = functools.partial(lax.dot_general, dimension_numbers=TURNED, preferred_element_type=jnp.float32)
MESH = pl.DeviceIdType.MESH
CHUNK = 32
CHUNKS = LANES // CHUNK
SPLIT = 6
TERM = 6 * LANES


def strip_of(row, col, side, cols):
    return row * (2 * cols) + col + side * (2 * cols - 1 - 2 * col)


def place_of(strip, cols):
    row = strip // (2 * cols)
    at = strip % (2 * cols)
    side = at // cols
    return row, at + side * (2 * cols - 1 - 2 * at), side


def tables(length):
    outer = length // LANES
    q = np.arange(LANES)
    turns = []
    for shift in (R, 0):
        turn = 2 * np.pi * (np.arange(outer)[:, None] - shift) * q / length
        turns += [np.cos(turn), np.sin(turn)]
    angle = 2 * np.pi * (q[:, None] * q % LANES) / LANES
    table = np.block([[np.cos(angle), np.sin(angle)], [-np.sin(angle), np.cos(angle)]]).astype(np.float32)
    big = table.astype(jnp.bfloat16)
    small = (table - big.astype(np.float32)).astype(jnp.bfloat16)
    u = np.arange(length)
    wrapped = np.minimum(u, length - u) / (length / cutoff_ratio)
    turns.append((wrapped * wrapped).reshape(outer, LANES))
    return np.stack(turns).astype(np.float32), np.concatenate([big, big, small], axis=1)


def swap8(cells):
    cells = [pltpu.roll(c, TILE_LANES * i, 1) if i else c for i, c in enumerate(cells)]
    group = lax.broadcasted_iota(jnp.int32, cells[0].shape, 1) // TILE_LANES
    for bit in (1, 2, 4):
        pick = (group & bit) != 0
        cells = [jnp.where(pick, cells[(i + bit) % GROUPS], cells[i]) for i in range(GROUPS)]
    out = []
    for i in range(GROUPS):
        c = cells[-i % GROUPS]
        out.append(pltpu.roll(c, LANES - TILE_LANES * i, 1) if i else c)
    return out


def pair_dot(wide, first, second):
    value = jnp.concatenate([first, second], axis=0)
    high = value.astype(jnp.bfloat16)
    rest = (value - high.astype(jnp.float32)).astype(jnp.bfloat16)
    return DOT(wide, jnp.concatenate([high, rest, high], axis=1))


def spread(into, base, a, g, at, value):
    for shift in range(3):
        to = a + 1 - shift
        if 0 <= to < 4:
            spot(into, base, to, g, at, shift, value)


def spot(into, base, to, g, at, shift, value):
    first = base + shift * 2 * LANES
    if g < GROUPS:
        into[to, g, at, first : first + LANES] = value
    if g > 0:
        into[to, g - 1, at, first + LANES : first + 2 * LANES] = value


def band_rows(family_ref, band, side):
    params = []
    for owner in range(2):
        both = family_ref[owner].astype(jnp.float32)
        heading = both[0:4] * (math.pi / N_AZ)
        semi_axis = R * (both[4:8] + (1 + NSIZE)) / (2 * NSIZE)
        params.append((jnp.cos(heading), jnp.sin(heading), 1.0 / semi_axis, 1.0 / (0.6 * semi_axis), 0.3 * semi_axis))
    shape = (16, LANES)
    lane = lax.broadcasted_iota(jnp.int32, shape, 1)
    row = lax.broadcasted_iota(jnp.int32, shape, 0)

    @pl.loop(0, TERM // 16)
    def _(block):
        offset_v = TILE_ROWS * (block // 16) + block % 8 - R - lane // TILE_LANES
        offset_u = TILE_LANES * (block // 8 % 2) - R + row - lane % TILE_LANES
        keep = (jnp.abs(offset_v) <= R) & (jnp.abs(offset_u) <= R)
        v = offset_v.astype(jnp.float32)
        u = offset_u.astype(jnp.float32)
        at = pl.multiple_of(block * 16, 16)
        for family in range(8):
            cos, sin, per_semi, per_across, slip_depth = [p[family % 4 : family % 4 + 1] for p in params[family // 4]]
            along = (u * cos + v * sin) * per_semi
            lateral = (v * cos - u * sin) * per_across
            inside = 1.0 - along * along - lateral * lateral
            height = slip_depth * jnp.sqrt(jnp.maximum(inside, 0.0))
            share = jnp.clip(4.0 * inside, 0.0, 1.0)
            lanes = slice(family * LANES, (family + 1) * LANES)
            band[pl.ds(at, 16), lanes] = jnp.where(keep, share, 0.0).astype(jnp.bfloat16)
            band[pl.ds(at + TERM, 16), lanes] = jnp.where(keep, height, 0.0).astype(jnp.bfloat16)


def whole_kernel(
    sizes, noise_any, choice_any, heading_any, extent_any, lib_any, turn_any, wide_any,
    out_any,
    mid, full, send_a, send_b, held_a, held_b, lift, grip, gathered, inv, band, edge, edge_send, halo_out, halo_in,
    natural, staged, factor, code_in, scale_in, done, library, choice_in, family_in, choice_smem, choice_ref, heading_ref, extent_ref, turn_ref, wide_ref,
    noise_sem, first_send, first_recv, choice_send, choice_recv, family_send, family_recv, smem_sem,
    halo_send, halo_recv, out_send, out_recv, scale_send, scale_recv, library_sem, done_sem, entry_sem,
):
    row_count, cols = sizes
    row, col, side = (lax.axis_index(axis) for axis in ("row", "col", "orient"))
    devices = row_count * cols * 2
    group = cols * 2
    me = (row * cols + col) * 2 + side
    strip = strip_of(row, col, side, cols)
    mine = strip % group
    block_here = col * 2 + side
    plane = row * cols + col
    left = place_of(lax.rem(strip + devices - 1, devices), cols)
    outer = turn_any.shape[1]

    def device(index):
        return index // group, index % group // 2, index % 2

    def owner(block):
        return row, block // 2, block % 2

    barrier = pltpu.get_barrier_semaphore()

    @pl.loop(1, devices)
    def _(k):
        pl.semaphore_signal(barrier, inc=1, device_id=device(lax.rem(me + k, devices)), device_id_type=MESH)

    def noise_copy(chunk, part, piece):
        lines = pl.ds(pl.multiple_of(side * LANES + chunk * CHUNK, CHUNK), CHUNK)
        return pltpu.make_async_copy(
            noise_any.at[part, lines, piece * 1024 : (piece + 1) * 1024],
            inv.at[0, part * 2 + piece // 2, piece % 2 * 4 + chunk],
            noise_sem.at[chunk, part * 4 + piece],
        )

    entries = [(turn_any, turn_ref), (choice_any, choice_ref), (heading_any, heading_ref), (extent_any, extent_ref)]
    entries = [pltpu.make_async_copy(a, b, entry_sem.at[i]) for i, (a, b) in enumerate(entries + [(wide_any, wide_ref)])]
    entries[0].start()
    for chunk in range(CHUNKS):
        for part in range(2):
            for piece in range(4):
                noise_copy(chunk, part, piece).start()

    for entry in entries[1:]:
        entry.start()
    library_copy = pltpu.make_async_copy(lib_any, library, library_sem)
    library_copy.start()
    entries[0].wait()
    for chunk in range(CHUNKS):
        for part in range(2):
            for piece in range(4):
                noise_copy(chunk, part, piece).wait()

        @pl.loop(0, CHUNK // 8)
        def _(block):
            at = pl.ds(pl.multiple_of(block * 8, 8), 8)
            line = me * LANES + chunk * CHUNK + block * 8 + lax.broadcasted_iota(jnp.int32, (8, LANES), 0)
            wrap_v = jnp.minimum(line, outer * LANES - line).astype(jnp.float32) * (cutoff_ratio / (outer * LANES))
            base = 1.0 + wrap_v * wrap_v
            parts = []
            for p in range(outer):
                root = lax.rsqrt(base + turn_ref[4, p : p + 1, :])
                spectrum = nugget_share + peak_share * (root * root * root)
                level = spectrum * lax.rsqrt(spectrum) * (1.0 / (outer * LANES))
                spot_at = (p // 16, p // 8 % 2 * 4 + chunk, at, slice(p % 8 * LANES, (p % 8 + 1) * LANES))
                parts.append((inv[(0,) + spot_at] * level, inv[(0, 2 + spot_at[0]) + spot_at[1:]] * level))
            turned = small_dft(parts)
            rows = pl.ds(pl.multiple_of(chunk * CHUNK + block * 8, 8), 8)
            for k in range(outer):
                re, im = turned[(k - R) % outer]
                cos = turn_ref[0, k : k + 1, :]
                sin = turn_ref[1, k : k + 1, :]
                mid[k, rows, 0:LANES] = re * cos + im * sin
                mid[k, rows, LANES : 2 * LANES] = im * cos - re * sin

    for entry in entries[1:]:
        entry.wait()
    choice_in[plane] = jnp.zeros((8, LANES), jnp.int32)
    choice_in[plane, 0:4, 0:16] = choice_ref[...]
    which = lax.broadcasted_iota(jnp.int32, (8, LANES), 0)
    mixed = jnp.zeros((8, LANES), jnp.int32)
    for f in range(4):
        mixed = jnp.where(which == f, heading_ref[f], mixed)
        mixed = jnp.where(which == f + 4, extent_ref[f], mixed)
    family_in[side] = mixed
    pl.semaphore_wait(barrier, devices - 1)

    def choice_copy(k):
        to = lax.rem(plane + k, row_count * cols)
        return pltpu.make_async_remote_copy(
            src_ref=choice_in.at[plane], dst_ref=choice_in.at[plane],
            send_sem=choice_send.at[k], recv_sem=choice_recv.at[k],
            device_id=(to // cols, to % cols, side), device_id_type=MESH,
        )

    def family_copy():
        return pltpu.make_async_remote_copy(
            src_ref=family_in.at[side], dst_ref=family_in.at[side], send_sem=family_send, recv_sem=family_recv,
            device_id=(row, col, 1 - side), device_id_type=MESH,
        )

    @pl.loop(1, row_count * cols)
    def _(k):
        choice_copy(k).start()

    family_copy().start()

    for k in range(0, outer, 2):
        high = jnp.concatenate([mid[k], mid[k + 1]], axis=0).astype(jnp.bfloat16)
        got = DOT(wide_ref[:, 2 * LANES :], jnp.concatenate([high, high], axis=1))
        for part in range(2):
            for one in range(2):
                piece = got[part * LANES : (part + 1) * LANES, one * LANES : (one + 1) * LANES]
                full[part, pl.ds(k + one, LANES, stride=outer), :] = piece

    parts_of = ((0, SPLIT, send_a, held_a), (SPLIT, GROUPS, send_b, held_b))

    def partner(k):
        return me ^ (k % 2 * 8 + k // 2 % 8 + k // 16 * 16)

    def first_copy(c, k):
        to = partner(k)
        return pltpu.make_async_remote_copy(
            src_ref=parts_of[c][2].at[to], dst_ref=parts_of[c][3].at[me],
            send_sem=first_send.at[c, k], recv_sem=first_recv.at[c, k],
            device_id=device(to), device_id_type=MESH,
        )

    for c, (low_g, high_g, send, held) in enumerate(parts_of):
        count = (high_g - low_g) * 16

        def packed(to, into):
            to_strip = strip_of(*device(to), cols)
            at = pl.ds(pl.multiple_of(to_strip * LANES + low_g * 16, 16), count)
            for part in range(2):
                into[to, part] = full[part, at, :].astype(jnp.bfloat16)

        @pl.loop(1, devices)
        def _(k):
            packed(partner(k), send)
            first_copy(c, k).start()

        packed(me, held)

    family_copy().wait()
    band_rows(family_in, band, side)

    @pl.loop(1, row_count * cols)
    def _(k):
        choice_copy(k).wait()

    to_smem = pltpu.make_async_copy(choice_in, choice_smem, smem_sem)
    to_smem.start()
    to_smem.wait()
    library_copy.wait()

    @pl.loop(0, library.shape[0])
    def _(t):
        library[t] = pltpu.roll(library[t].T, R, 1)

    left_lanes = lax.broadcasted_iota(jnp.int32, (LANES, LANES), 1) < R

    def tile(shift, t):
        x = lax.rem(strip + devices + shift, devices)
        return library[choice_smem[x // 16 * cols + t // 4, t % 4, x % 16]]

    @pl.loop(0, outer)
    def _(t):
        at = pl.ds(pl.multiple_of(t * LANES, LANES), LANES)
        here = tile(0, t)
        full[0, at, :] = jnp.where(left_lanes, tile(-1, t), here)
        full[1, at, :] = jnp.where(left_lanes, here, tile(1, t))

    half = lax.broadcasted_iota(jnp.int32, (16, LANES), 1) % TILE_LANES < R
    first = strip == 0
    last = strip == devices - 1
    for side_rows in (slice(0, 8), slice(8 + LANES, 16 + LANES)):
        edge[:, :, side_rows, :] = jnp.zeros((2, GROUPS + 1, 8, LANES), jnp.float32)
        edge_send[:, side_rows, :] = jnp.zeros((2, 8, LANES), jnp.float32)

    for a in range(4):
        @pl.loop(0, 8)
        def _(c):
            at = pl.ds(pl.multiple_of(c * 16, 16), 16)
            for source in range(2):
                turned = swap8([full[source, pl.ds(c * 512 + 8 * a + r, 16, stride=32), :] for r in range(8)])
                for g in range(GROUPS) if source == 0 else (0,):
                    slope = turned[g]
                    square = 1.0 + slope * slope
                    inverse = lax.rsqrt(square)
                    drive = slope * inverse
                    tile_at = g
                    if source == 0:
                        lift[a, g, at, :] = 0.5 * square * inverse
                        grip[a, g, at, :] = 0.6 * inverse
                        if g == 0:
                            drive = jnp.where(half & first, 0.0, drive)
                    else:
                        tile_at = GROUPS
                        drive = jnp.where(last & ~half, 0.0, drive)
                    spread(gathered, TERM, a, tile_at, at, drive.astype(jnp.bfloat16))
                    if a in (0, 3):
                        edge[0, tile_at, pl.ds(pl.multiple_of(c * 16 + 8, 8), 16), :] = drive

        if a in (0, 3):
            @pl.loop(0, 8)
            def _(c):
                at = pl.ds(pl.multiple_of(c * 16, 16), 16)
                for g in range(GROUPS + 1):
                    value = edge[0, g, pl.ds(c * 16 + (9 if a == 0 else 7), 16), :].astype(jnp.bfloat16)
                    spot(gathered, TERM, 3 - a, g, at, 2 if a == 0 else 0, value)

    pairs = band.shape[1] // (2 * PHASE)

    @pl.loop(0, CHUNKS)
    def _(chunk):
        at = pl.ds(pl.multiple_of(chunk * CHUNK, CHUNK), CHUNK)
        cells = gathered[:, :, at, TERM:].reshape(4 * GROUPS * CHUNK, TERM)
        for pair in range(pairs):
            lanes = slice(pair * 2 * PHASE, (pair + 1) * 2 * PHASE)
            sums = jnp.dot(cells, band[TERM:, lanes], preferred_element_type=jnp.float32)
            inv[chunk, :, :, :, lanes] = (1.0 / sums).reshape(4, GROUPS, CHUNK, 2 * PHASE)

    def halo_copy(slot):
        return pltpu.make_async_remote_copy(
            src_ref=halo_out.at[slot], dst_ref=halo_in.at[slot],
            send_sem=halo_send.at[slot], recv_sem=halo_recv.at[slot],
            device_id=left, device_id_type=MESH,
        )

    per_chunk = CHUNK * outer // (2 * LANES)
    home = block_here // per_chunk

    def out_copy(c, block, source):
        return pltpu.make_async_remote_copy(
            src_ref=staged.at[c, block], dst_ref=code_in.at[source, c],
            send_sem=out_send.at[c, block], recv_sem=out_recv.at[c, source],
            device_id=owner(block), device_id_type=MESH,
        )

    def scale_copy(c, block, source):
        return pltpu.make_async_remote_copy(
            src_ref=factor.at[c, block // (2 * per_chunk)], dst_ref=scale_in.at[source, c],
            send_sem=scale_send.at[c, block], recv_sem=scale_recv.at[c, source],
            device_id=owner(block), device_id_type=MESH,
        )

    for c, (low_g, high_g, send, held) in enumerate(parts_of):
        @pl.loop(1, devices)
        def _(k):
            first_copy(c, k).wait()

        @pl.loop(low_g, high_g)
        def _(g):
            at = pl.ds(pl.multiple_of((g - low_g) * 16, 16), 16)
            parts = [(held[p, 0, at, :].astype(jnp.float32), held[p, 1, at, :].astype(jnp.float32)) for p in range(outer)]
            for k, (re, im) in enumerate(small_dft(parts)):
                to = slice(k % 8 * 16, (k % 8 + 1) * 16)
                cos = turn_ref[2, k : k + 1, :]
                sin = turn_ref[3, k : k + 1, :]
                mid[k // 8 * 8 + g, to, 0:LANES] = re * cos + im * sin
                mid[k // 8 * 8 + g, to, LANES : 2 * LANES] = im * cos - re * sin

        items = [(a, g) for g in range(low_g, high_g) for a in range(4)]
        for at_item in range(0, len(items), 2):
            two = items[at_item : at_item + 2]
            got = pair_dot(wide_ref[...], *[mid[a * 8 + g] for a, g in two])
            for one, (a, g) in enumerate(two):
                for term in range(2):
                    field = got[term * LANES : (term + 1) * LANES, one * LANES : (one + 1) * LANES]
                    value = jnp.exp((0.4 if term == 0 else 0.25) * field) * (lift if term == 0 else grip)[a, g]
                    if g == 0:
                        mask = lax.broadcasted_iota(jnp.int32, (LANES, LANES), 1) % TILE_LANES < R
                        sent = jnp.where(first & ~mask, 0.0, value)
                        value = jnp.where(first & mask, 0.0, value)
                        halo_out[a, term] = sent.astype(jnp.bfloat16)
                    spread(gathered, term * TERM, a, g, slice(None), value.astype(jnp.bfloat16))
                    if a in (0, 3):
                        moved = slice(9, 9 + LANES) if a == 0 else slice(7, 7 + LANES)
                        edge[term, g, 8 : 8 + LANES, :] = value
                        near = edge[term, g, moved, :].astype(jnp.bfloat16)
                        spot(gathered, term * TERM, 3 - a, g, slice(None), 2 if a == 0 else 0, near)
                        if g == 0:
                            edge_send[term, 8 : 8 + LANES, :] = sent
                            halo_out[4 if a == 0 else 5, term] = edge_send[term, moved, :].astype(jnp.bfloat16)
                if g == 0:
                    halo_copy(a).start()
                    if a in (0, 3):
                        halo_copy(4 if a == 0 else 5).start()

        if c == 1:
            for slot in range(6):
                halo_copy(slot).wait()
                for term in range(2):
                    value = halo_in[slot, term]
                    if slot < 4:
                        spread(gathered, term * TERM, slot, GROUPS, slice(None), value)
                    else:
                        to, shift = (3, 2) if slot == 4 else (0, 0)
                        spot(gathered, term * TERM, to, GROUPS, slice(None), shift, value)

        tiles = slice(c * 4, c * 4 + 4)

        @pl.loop(0, 2)
        def _(step):
            half_at = (home // 2) ^ (1 - step)
            cells = []
            for q in range(2):
                at = pl.ds(pl.multiple_of((half_at * 2 + q) * CHUNK, CHUNK), CHUNK)
                cells.append(gathered[:, tiles, at, :].reshape(16 * CHUNK, 2 * TERM))
            cells = jnp.concatenate(cells, axis=0)
            low = None
            for pair in range(pairs):
                lanes = slice(pair * 2 * PHASE, (pair + 1) * 2 * PHASE)
                ratio = jnp.dot(cells, band[:, lanes], preferred_element_type=jnp.float32)
                ratio = ratio * inv[pl.ds(half_at * 2, 2), :, tiles, :, lanes].reshape(32 * CHUNK, 2 * PHASE)
                least = jnp.minimum(ratio[:, 0:PHASE], ratio[:, PHASE:])
                low = least if low is None else jnp.minimum(low, least)
            largest = jnp.max(jnp.max(low, axis=0, keepdims=True), axis=1, keepdims=True)
            largest = jnp.broadcast_to(jnp.maximum(largest, 1e-30), (8, LANES))
            factor[c, half_at] = jnp.sqrt(largest) * (1.0 / 65535.0)
            upward = (65535.0 * lax.rsqrt(largest))[0:1, :]
            low = low.reshape(2, 4, 4, 2, CHUNK // 2, LANES)
            for q in range(2):
                for a in range(4):
                    turned = swap8([low[q, a, g % 4, g // 4] for g in range(GROUPS)])
                    for r in range(8):
                        code = jnp.sqrt(turned[r]) * upward + 0.5
                        natural[q, pl.ds(8 * a + r, CHUNK // 2, stride=32), :] = code
                for piece in range(4):
                    code = natural[q, piece * LANES : (piece + 1) * LANES, :]
                    code = (code.astype(jnp.int32) - 32768).T.astype(jnp.int16)
                    for upper in range(2):
                        block = (half_at * 2 + q) * per_chunk + upper * 2 + piece // 2
                        staged[c, block, :, piece % 2 * LANES : (piece % 2 + 1) * LANES] = code[upper * 64 : upper * 64 + 64]

            @pl.loop(0, 2 * per_chunk)
            def _(i):
                block = half_at * 2 * per_chunk + (i ^ (per_chunk * (1 - home % 2)))

                @pl.when(block != block_here)
                def _():
                    out_copy(c, block, mine).start()
                    scale_copy(c, block, mine).start()

    def done_copy(c, source):
        rows = pl.ds(pl.multiple_of(source * LANES + c * 64, 64), 64)
        return pltpu.make_async_copy(done.at[source, c], out_any.at[rows], done_sem.at[c, source])

    def finish(c, source, code, scale):
        root = (code.astype(jnp.float32) + 32768.0) * scale[0:1, 0:1]
        done[source, c] = root * root
        done_copy(c, source).start()

    for c in range(2):
        finish(c, mine, staged[c, block_here], factor[c, home // 2])

        @pl.loop(0, group)
        def _(at):
            block = (home ^ (3 - at // per_chunk)) * per_chunk + at % per_chunk
            source = strip_of(0, block // 2, block % 2, cols)

            @pl.when(block != block_here)
            def _():
                out_copy(c, block, source).wait_recv()
                scale_copy(c, block, source).wait_recv()
                finish(c, source, code_in[source, c], scale_in[source, c])

    @pl.loop(1, group)
    def _(turned):
        block = lax.rem(block_here + turned, group)
        for c in range(2):
            out_copy(c, block, mine).wait_send()
            scale_copy(c, block, mine).wait_send()

    @pl.loop(0, group)
    def _(source):
        for c in range(2):
            done_copy(c, source).wait()


def whole_safety(noise, choices, headings, extents, library, row_count, cols):
    length = noise.shape[2]
    outer = length // LANES
    group = 2 * cols
    devices = group * row_count
    turns, wide = tables(length)
    dma = pltpu.SemaphoreType.DMA
    f32, bf16 = jnp.float32, jnp.bfloat16
    early, late = SPLIT * 16, LANES - SPLIT * 16
    return pl.pallas_call(
        functools.partial(whole_kernel, (row_count, cols)),
        out_shape=jax.ShapeDtypeStruct((group * LANES, 2 * LANES), f32),
        in_specs=[pl.BlockSpec(memory_space=pl.ANY)] * 7,
        out_specs=pl.BlockSpec(memory_space=pl.ANY),
        scratch_shapes=[
            pltpu.VMEM((outer, LANES, 2 * LANES), f32),
            pltpu.VMEM((2, length, LANES), f32),
            pltpu.VMEM((devices, 2, early, LANES), bf16),
            pltpu.VMEM((devices, 2, late, LANES), bf16),
            pltpu.VMEM((devices, 2, early, LANES), bf16),
            pltpu.VMEM((devices, 2, late, LANES), bf16),
            pltpu.VMEM((4, GROUPS, LANES, LANES), f32),
            pltpu.VMEM((4, GROUPS, LANES, LANES), f32),
            pltpu.VMEM((4, GROUPS, LANES, 2 * TERM), bf16),
            pltpu.VMEM((CHUNKS, 4, GROUPS, CHUNK, 8 * PHASE), f32),
            pltpu.VMEM((2 * TERM, 8 * PHASE), bf16),
            pltpu.VMEM((2, GROUPS + 1, LANES + 16, LANES), f32),
            pltpu.VMEM((2, LANES + 16, LANES), f32),
            pltpu.VMEM((6, 2, LANES, LANES), bf16),
            pltpu.VMEM((6, 2, LANES, LANES), bf16),
            pltpu.VMEM((2, length // CHUNKS // 2, LANES), f32),
            pltpu.VMEM((2, group, LANES // 2, 2 * LANES), jnp.int16),
            pltpu.VMEM((2, 2, 8, LANES), f32),
            pltpu.VMEM((group, 2, LANES // 2, 2 * LANES), jnp.int16),
            pltpu.VMEM((group, 2, 8, LANES), f32),
            pltpu.VMEM((group, 2, LANES // 2, 2 * LANES), f32),
            pltpu.VMEM(library.shape, f32),
            pltpu.VMEM((row_count * cols, 8, LANES), jnp.int32),
            pltpu.VMEM((2, 8, LANES), jnp.int32),
            pltpu.SMEM((row_count * cols, 8, LANES), jnp.int32),
            pltpu.VMEM(choices.shape, jnp.int32),
            pltpu.SMEM(headings.shape, jnp.int32),
            pltpu.SMEM(extents.shape, jnp.int32),
            pltpu.VMEM(turns.shape, f32),
            pltpu.VMEM(wide.shape, bf16),
            dma((CHUNKS, 8)), dma((2, devices)), dma((2, devices)),
            dma((row_count * cols,)), dma((row_count * cols,)), dma, dma, dma,
            dma((6,)), dma((6,)), dma((2, group)), dma((2, group)), dma((2, group)), dma((2, group)), dma, dma((2, group)), dma((5,)),
        ],
        compiler_params=pltpu.CompilerParams(
            vmem_limit_bytes=62 << 20, collective_id=0, has_side_effects=True
        ),
    )(noise, choices, headings, extents, library, turns, wide)


def strip_body(noise, elevation_library, tile_choice_index, family_heading_index, family_extent_index):
    row_count, cols = lax.axis_size("row"), lax.axis_size("col")
    return whole_safety(
        noise, tile_choice_index.T, family_heading_index, family_extent_index, elevation_library, row_count, cols
    )


def chosen_body(noise, elevation_library, tile_choice_index, family_heading_index, family_extent_index):
    shape = (lax.axis_size("row"), lax.axis_size("col"), lax.axis_size("orient"))
    side_cells = noise.shape[2]
    fits = (
        shape == (2, 8, 2)
        and side_cells == 32 * LANES
        and elevation_library.shape[1] == LANES
        and tile_choice_index.shape == (16, 4)
        and family_heading_index.shape[0] == 4
    )
    chosen = strip_body if fits else body
    return chosen(noise, elevation_library, tile_choice_index, family_heading_index, family_extent_index)


def solution(mesh):
    placed = (P(None, ("row", "col"), None), P(), P("row", "col"), P("orient"), P("orient"))
    return jax.shard_map(
        chosen_body, mesh=mesh, in_specs=placed, out_specs=P("row", ("col", "orient")), check_vma=False
    )
```
